32 devices in a mesh: dp: 8 (over y, x, core), seq: 4 (over z).
Axes of the slice: x: 2, y: 2, z: 4, core: 2. Of those that a mesh axis runs over, the one named last changes fastest.
Arguments:
- block_input: bfloat16 [24, 1024, 1024], P('dp', 'seq'), may hold values from -6 to 6
- seg_start: int32 [24, 1024], P('dp'), may hold values from 0 to 1023, as said below
- ln1_gain: float32 [1024], replicated, may hold values from 0.5 to 1.5
- ln1_bias: float32 [1024], replicated, may hold values from -1.75 to 1.75
- qkv_weight: bfloat16 [1024, 3072], P('dp'), may hold values from -0.1875 to 0.1875
- query_bias: float32 [1024], replicated, may hold values from -1.75 to 1.75
- value_bias: float32 [1024], replicated, may hold values from -1.75 to 1.75
- query_adapter_reduce: bfloat16 [1024, 4], replicated, may hold values from -0.1875 to 0.1875
- query_up: bfloat16 [4, 1024], replicated, may hold values from -0.1875 to 0.1875
- value_adapter_reduce: bfloat16 [1024, 4], replicated, may hold values from -0.1875 to 0.1875
- value_up: bfloat16 [4, 1024], replicated, may hold values from -0.1875 to 0.1875
- out_weight: bfloat16 [1024, 1024], P('dp'), may hold values from -0.75 to 0.75
- out_bias: float32 [1024], replicated, may hold values from -1.75 to 1.75
- ln2_gain: float32 [1024], replicated, may hold values from 0.5 to 1.5
- ln2_bias: float32 [1024], replicated, may hold values from -1.75 to 1.75
- fc_weight: bfloat16 [1024, 4096], P('dp'), may hold values from -0.1875 to 0.1875
- fc_bias: float32 [4096], replicated, may hold values from -1.75 to 1.75
- proj_weight: bfloat16 [4096, 1024], P('dp'), may hold values from -0.09375 to 0.09375
- proj_bias: float32 [1024], replicated, may hold values from -1.75 to 1.75
- grad_out: bfloat16 [24, 1024, 1024], P('dp', 'seq'), may hold values from -6 to 6
Outputs:
- block_output: bfloat16 [24, 1024, 1024], P('dp', 'seq')
- grad_input: float32 [24, 1024, 1024], P('dp', 'seq')
- grad_query_down: float32 [1024, 4], replicated
- grad_query_up: float32 [4, 1024], replicated
- grad_value_down: float32 [1024, 4], replicated
- grad_value_up: float32 [4, 1024], replicated
The draws below stay inside these ranges and needn't reach their ends.
Inputs may be any that keep to these rules, and one draw needn't show every extreme that they name: `seg_start`: each entry is the first position of its token's document within the row: it is at most the token's own position, position 0 has 0, and equal entries form runs of consecutive tokens whose start is the entry itself. The last position of every row starts its own document. In every row one document begins within the row's first 1 / N of positions and ends within its last 1 / N, N being the number of devices along seq.
All inputs are finite; a program needn't handle non-finite values.
Results may differ from the reference program's by a relative error of at most 0.014.
Values may be sent and summed in bfloat16 or wider, within the bound.
A program may use at most 192 MiB of HBM per device.

```python
import jax
import jax.numpy as jnp
from jax import lax

D = 1024
HEAD = 64
FF = 4096
RANK = 4
LEN = 1024
ROWS = 24
N_SEQ = 4


def draw_seg_start(key, part):
    slab_width = LEN // N_SEQ
    keys_list = jax.random.split(key, 3)
    positions = jnp.arange(LEN, dtype=jnp.int32)[None, :]
    leading = jax.random.randint(keys_list[0], (ROWS, 1), 0, slab_width)
    trailing = jax.random.randint(keys_list[1], (ROWS, 1), LEN - slab_width + 1, LEN)
    random_cuts = jax.random.randint(keys_list[2], (ROWS, LEN), 0, 48) == 0
    outside = (positions < leading) | (positions > trailing)
    boundary = random_cuts & outside | (positions == 0) | (positions == leading) | (positions == trailing) | (positions == LEN - 1)
    marked = jnp.where(boundary, positions, 0).astype(jnp.int32)
    return lax.cummax(marked, axis=1)


def steps_of(own_key, shape, cuts, low, top_value):
    level, own = 1.0, jax.random.fold_in(own_key, 6)
    for dim, shards_of in cuts:
        steps = jnp.exp(jax.random.uniform(jax.random.fold_in(own, dim), (shards_of,), jnp.float32, low / len(cuts), top_value / len(cuts)))
        level = level * jnp.repeat(steps, shape[dim] // shards_of).reshape([-1 if axis == dim else 1 for axis in range(len(shape))])
    return level


def scatter_about(stream_key, dims, width, limit, pieces=(), kind=jnp.bfloat16):
    gain = steps_of(stream_key, dims, pieces, -0.22, 0.18) if pieces else 1.0
    entries = jax.random.normal(stream_key, dims, jnp.float32) * width * gain
    return jnp.minimum(jnp.maximum(entries, -limit), limit).astype(kind)


def setup_inputs(seed: int = 0) -> dict:
    splits = jax.random.split(jax.random.key(seed), 21)
    return {
        "block_input": scatter_about(splits[0], (ROWS, LEN, D), 1.0, 6.0, ((0, 8), (1, 4))),
        "seg_start": draw_seg_start(jax.random.fold_in(splits[20], 71), 0),
        "ln1_gain": jnp.clip(1.0 + 0.1 * jax.random.normal(splits[2], (D,), jnp.float32), 0.5, 1.5),
        "ln1_bias": scatter_about(splits[3], (D,), 0.3, 1.75, (), jnp.float32),
        "qkv_weight": scatter_about(splits[4], (D, 3 * D), D ** -0.5, 0.1875, ((0, 8),)),
        "query_bias": scatter_about(splits[5], (D,), 0.3, 1.75, (), jnp.float32),
        "value_bias": scatter_about(splits[6], (D,), 0.3, 1.75, (), jnp.float32),
        "query_adapter_reduce": scatter_about(splits[7], (D, RANK), D ** -0.5, 0.1875),
        "query_up": scatter_about(splits[8], (RANK, D), 0.03, 0.1875),
        "value_adapter_reduce": scatter_about(splits[9], (D, RANK), D ** -0.5, 0.1875),
        "value_up": scatter_about(splits[10], (RANK, D), 0.03, 0.1875),
        "out_weight": scatter_about(splits[11], (D, D), (D // 16) ** -0.5, 0.75, ((0, 8),)),
        "out_bias": scatter_about(splits[12], (D,), 0.3, 1.75, (), jnp.float32),
        "ln2_gain": jnp.clip(1.0 + 0.1 * jax.random.normal(splits[13], (D,), jnp.float32), 0.5, 1.5),
        "ln2_bias": scatter_about(splits[14], (D,), 0.3, 1.75, (), jnp.float32),
        "fc_weight": scatter_about(splits[15], (D, FF), D ** -0.5, 0.1875, ((0, 8),)),
        "fc_bias": scatter_about(splits[16], (FF,), 0.3, 1.75, (), jnp.float32),
        "proj_weight": scatter_about(splits[17], (FF, D), FF ** -0.5, 0.09375, ((0, 8),)),
        "proj_bias": scatter_about(splits[18], (D,), 0.3, 1.75, (), jnp.float32),
        "grad_out": scatter_about(splits[19], (ROWS, LEN, D), 1.0, 6.0, ((0, 8), (1, 4))),
    }


NORM_EPSILON = 1e-05
ADAPTER_SCALE = 8.0
MASKED = -1e+30

@jax.custom_vjp
def reduced_rank_part(v):
    return lax.optimization_barrier(v.astype(jnp.bfloat16)).astype(jnp.float32)

@jax.custom_vjp
def reduced_rank_backward(v):
    return v

def low_keep(v):
    return (reduced_rank_part(v), None)

def low_pass(kept, grad):
    return (grad,)

def back_keep(v):
    return (v, None)

def back_low(kept, grad):
    return (reduced_rank_part(grad),)
reduced_rank_part.defvjp(low_keep, low_pass)
reduced_rank_backward.defvjp(back_keep, back_low)

def matrix_product(left_side, right_side):
    return jnp.einsum('...i,ij->...j', left_side, right_side, precision=lax.Precision.HIGHEST)

def layer_norm(row_values, norm_gain, norm_shift):
    average = lax.optimization_barrier(jnp.mean(row_values, axis=-1, keepdims=True))
    centered = row_values - average
    inverse = lax.rsqrt(lax.optimization_barrier(jnp.mean(centered * centered, axis=-1, keepdims=True)) + NORM_EPSILON)
    return centered * inverse * norm_gain + norm_shift

def forward_block_pass(row_values, document_starts, adapters, fixed_params):
    qkv_weight, query_bias, value_bias, out_weight, out_bias, ln1_gain, ln1_bias, ln2_gain, ln2_bias, fc_weight, fc_bias, proj_weight, proj_bias = fixed_params
    query_adapter_reduce, query_up, value_adapter_reduce, value_up = adapters
    row_count = row_values.shape[0]
    length = row_values.shape[1]
    model_width = row_values.shape[2]
    first_hidden_layer = reduced_rank_part(layer_norm(row_values, ln1_gain, ln1_bias))
    projected = matrix_product(first_hidden_layer, qkv_weight)
    query_reduce = reduced_rank_backward(reduced_rank_part(ADAPTER_SCALE * matrix_product(first_hidden_layer, query_adapter_reduce)))
    value_reduce = reduced_rank_backward(reduced_rank_part(ADAPTER_SCALE * matrix_product(first_hidden_layer, value_adapter_reduce)))
    queries = reduced_rank_backward(reduced_rank_part(projected[..., :model_width] + query_bias + matrix_product(query_reduce, query_up)))
    keyed = reduced_rank_backward(reduced_rank_part(projected[..., model_width:2 * model_width]))
    valued = reduced_rank_backward(reduced_rank_part(projected[..., 2 * model_width:] + value_bias + matrix_product(value_reduce, value_up)))
    split_shape = (row_count, length, model_width // HEAD, HEAD)
    scores = jnp.einsum('rqhd,rkhd->rhqk', queries.reshape(split_shape), keyed.reshape(split_shape), precision=lax.Precision.HIGHEST) * HEAD ** (-0.5)
    scores = reduced_rank_backward(scores)
    positions = jnp.arange(length, dtype=jnp.int32)
    allowed = (positions[None, None, :] <= positions[None, :, None]) & (positions[None, None, :] >= document_starts[:, :, None])
    scores = jnp.where(allowed[:, None], scores, MASKED)
    highest = lax.optimization_barrier(jnp.max(scores, axis=-1, keepdims=True))
    weights = jnp.exp(scores - highest)
    probabilities = weights / lax.optimization_barrier(jnp.sum(weights, axis=-1, keepdims=True))
    mixed_rows = jnp.einsum('rhqk,rkhd->rqhd', reduced_rank_part(probabilities), valued.reshape(split_shape), precision=lax.Precision.HIGHEST).reshape(row_count, length, model_width)
    mixed_rows = reduced_rank_backward(reduced_rank_part(mixed_rows))
    attended = reduced_rank_backward(matrix_product(mixed_rows, out_weight) + out_bias)
    middle = row_values + attended
    hidden_second = reduced_rank_part(layer_norm(middle, ln2_gain, ln2_bias))
    before = reduced_rank_backward(matrix_product(hidden_second, fc_weight) + fc_bias)
    activated = reduced_rank_part(jax.nn.gelu(before, approximate=True))
    return middle + matrix_product(activated, proj_weight) + proj_bias

def widen(array_value):
    return array_value.astype(jnp.float32)

def reference(block_input, seg_start, ln1_gain, ln1_bias, qkv_weight, query_bias, value_bias, query_adapter_reduce, query_up, value_adapter_reduce, value_up, out_weight, out_bias, ln2_gain, ln2_bias, fc_weight, fc_bias, proj_weight, proj_bias, grad_out):
    fixed_params = (widen(qkv_weight), widen(query_bias), widen(value_bias), widen(out_weight), widen(out_bias), widen(ln1_gain), widen(ln1_bias), widen(ln2_gain), widen(ln2_bias), widen(fc_weight), widen(fc_bias), widen(proj_weight), widen(proj_bias))
    adapters = (widen(query_adapter_reduce), widen(query_up), widen(value_adapter_reduce), widen(value_up))
    rows_total = block_input.shape[0]
    length = block_input.shape[1]
    model_width = block_input.shape[2]
    group_rows = 4 if rows_total % 4 == 0 else 2 if rows_total % 2 == 0 else 1
    step_count = rows_total // group_rows
    inputs_split = widen(block_input).reshape(step_count, group_rows, length, model_width)
    starts_split = seg_start.astype(jnp.int32).reshape(step_count, group_rows, length)
    cotangent_split = widen(grad_out).reshape(step_count, group_rows, length, model_width)

    def advance(running_sums, row_entry):
        row_values, document_starts, output_gradient = row_entry

        def forward_pass_alone(input_tokens, adapter_weight_set):
            return forward_block_pass(input_tokens, document_starts, adapter_weight_set, fixed_params)
        result, backward_function = jax.vjp(forward_pass_alone, row_values, adapters)
        gradient_row_list, adapter_gradient = backward_function(output_gradient)
        running_sums = jax.tree.map(jnp.add, running_sums, adapter_gradient)
        return (running_sums, (result.astype(jnp.bfloat16), gradient_row_list))
    zeros_start = tuple((jnp.zeros_like(adapter_part) for adapter_part in adapters))
    running_sums, outputs = lax.scan(advance, zeros_start, (inputs_split, starts_split, cotangent_split))
    block_output = outputs[0].reshape(rows_total, length, model_width)
    grad_input = outputs[1].reshape(rows_total, length, model_width).astype(jnp.float32)
    return (block_output, grad_input, running_sums[0], running_sums[1], running_sums[2], running_sums[3])
```

```python
from functools import partial

import jax
import jax.numpy as jnp
from jax import lax
from jax.experimental import pallas as pl
from jax.experimental.pallas import tpu as pltpu
from jax.sharding import PartitionSpec as P

HEAD = 64
QUAD = 256
PAIR = 128
NORM_EPSILON = 1e-05
ADAPTER_SCALE = 8.0
MASKED = -1e30
GELU_A = 0.7978845608028654
GELU_B = 0.044715

F32 = jnp.float32
BF16 = jnp.bfloat16
VMEM_BYTES = 56 * 1024 * 1024


def dot_nn(left, right):
    return lax.dot_general(left, right, (((1,), (0,)), ((), ())), preferred_element_type=F32)


def dot_nt(left, right):
    return lax.dot_general(left, right, (((1,), (1,)), ((), ())), preferred_element_type=F32)


def norm_parts(values):
    average = jnp.mean(values, axis=-1, keepdims=True)
    centered = values - average
    inverse = lax.rsqrt(jnp.mean(centered * centered, axis=-1, keepdims=True) + NORM_EPSILON)
    return centered * inverse, inverse


def norm_backward(gradient, normed, inverse, gain):
    scaled = gradient * gain
    return inverse * (
        scaled
        - jnp.mean(scaled, axis=-1, keepdims=True)
        - normed * jnp.mean(scaled * normed, axis=-1, keepdims=True)
    )


def head_lanes(rows, dtype):
    lane = lax.broadcasted_iota(jnp.int32, (rows, PAIR), 1)
    return lane < HEAD


def forward_kernel(chunks, place_ref, start_ref, *refs):
    hidden = refs[:chunks]
    wq, wk, wv, bias_q, bias_v, reduce_ref = refs[chunks : chunks + 6]
    q_out, k_out, v_out, mix_out, lse_out, down_out, mask_ref = refs[chunks + 6 :]
    tokens = hidden[0].shape[0]
    quad = pl.program_id(0)

    @pl.when(quad == 0)
    def _():
        place = place_ref[0]
        query = place * tokens + lax.broadcasted_iota(jnp.int32, (tokens, tokens), 0)
        start = start_ref[...]
        for s in range(chunks):
            key = (place - s) * tokens + lax.broadcasted_iota(jnp.int32, (tokens, tokens), 1)
            allowed = key >= start
            if s == 0:
                allowed = allowed & (key <= query)
            mask_ref[:, s * tokens : (s + 1) * tokens] = jnp.where(allowed, 0.0, MASKED)
            down = dot_nn(hidden[s][...], reduce_ref[...]) * ADAPTER_SCALE
            down_out[:, s * tokens : (s + 1) * tokens] = down.T[:8].astype(BF16)

    q_out[...] = ((dot_nn(hidden[0][...], wq[...]) + bias_q[...]).astype(BF16) * (HEAD**-0.5)).astype(BF16)
    for s in range(chunks):
        span = slice(s * tokens, (s + 1) * tokens)
        k_out[span, :] = dot_nn(hidden[s][...], wk[...]).astype(BF16)
        v_out[span, :] = (dot_nn(hidden[s][...], wv[...]) + bias_v[...]).astype(BF16)
    low = head_lanes(tokens, BF16)
    lane = lax.broadcasted_iota(jnp.int32, (tokens, PAIR), 1)
    totals = jnp.zeros((tokens, PAIR), F32)
    for pair in range(QUAD // PAIR):
        span = slice(pair * PAIR, (pair + 1) * PAIR)
        q_pair = q_out[:, span]
        mixed = []
        for half in range(2):
            own = low if half == 0 else jnp.logical_not(low)
            q_head = jnp.where(own, q_pair, jnp.zeros_like(q_pair))
            score = dot_nt(q_head, k_out[:, span]) + mask_ref[...]
            highest = jnp.max(score, axis=-1, keepdims=True)
            weight = jnp.exp(score - highest)
            total = jnp.sum(weight, axis=-1, keepdims=True)
            mixed.append(dot_nn(weight.astype(BF16), v_out[:, span]) * (1.0 / total))
            totals = jnp.where(lane == pair * 2 + half, highest + jnp.log(total), totals)
        mix_out[:, span] = jnp.where(low, mixed[0], mixed[1]).astype(BF16)
    lse_out[0] = totals.T[:8]


def feed_kernel(
    mix_ref, x_ref, gout_ref, wo_ref, out_bias, gain, shift, proj_bias, fc_ref, fc_bias, proj_ref,
    out_ref, gmid_ref, gmix_ref, middle_ref, hidden_ref, acc_ref, grad_ref,
):
    step = pl.program_id(0)

    @pl.when(step == 0)
    def _():
        middle = x_ref[...].astype(F32) + dot_nn(mix_ref[...], wo_ref[...]) + out_bias[...]
        middle_ref[...] = middle
        normed, _ = norm_parts(middle)
        hidden_ref[...] = (normed * gain[...] + shift[...]).astype(BF16)

    before = dot_nn(hidden_ref[...], fc_ref[...]) + fc_bias[...]
    square = before * before
    bend = jnp.tanh(GELU_A * before * (1.0 + GELU_B * square))
    half = 0.5 * (1.0 + bend)
    slope = half + 0.5 * before * (1.0 - bend * bend) * (GELU_A * (1.0 + 3.0 * GELU_B * square))
    act = (before * half).astype(BF16)
    g_before = (dot_nt(gout_ref[...], proj_ref[...]) * slope).astype(BF16)
    fed = dot_nn(act, proj_ref[...])
    back = dot_nt(g_before, fc_ref[...])

    @pl.when(step == 0)
    def _():
        acc_ref[...] = fed
        grad_ref[...] = back

    @pl.when(step > 0)
    def _():
        acc_ref[...] += fed
        grad_ref[...] += back

    @pl.when(step == pl.num_programs(0) - 1)
    def _():
        middle = middle_ref[...]
        out_ref[...] = (middle + acc_ref[...] + proj_bias[...]).astype(BF16)
        normed, inverse = norm_parts(middle)
        g_middle = gout_ref[...].astype(F32) + norm_backward(grad_ref[...], normed, inverse, gain[...])
        gmid_ref[...] = g_middle
        gmix_ref[...] = dot_nt(g_middle.astype(BF16), wo_ref[...]).astype(BF16)


def backward_kernel(chunks, place_ref, start_ref, *refs):
    hidden = refs[:chunks]
    q_ref, k_ref, v_ref, mix_ref, g_ref, lse_ref, down_ref, up_ref, w_ref = refs[chunks : chunks + 9]
    grads = refs[chunks + 9 : 2 * chunks + 9]
    reduce_out, up_out, mask_ref, dq_ref, dkv_ref, w_held, w_sem = refs[2 * chunks + 9 :]
    tokens = hidden[0].shape[0]
    width = hidden[0].shape[1]
    quad = pl.program_id(0)

    @pl.when(quad == 0)
    def _():
        pltpu.make_async_copy(w_ref, w_held, w_sem).start()
        place = place_ref[0]
        query = place * tokens + lax.broadcasted_iota(jnp.int32, (tokens, tokens), 1)
        start = start_ref[...]
        for s in range(chunks):
            key = (place - s) * tokens + lax.broadcasted_iota(jnp.int32, (tokens, tokens), 0)
            allowed = key >= start
            if s == 0:
                allowed = allowed & (key <= query)
            mask_ref[s * tokens : (s + 1) * tokens, :] = jnp.where(allowed, 0.0, MASKED)

    low = head_lanes(tokens, BF16)
    for pair in range(QUAD // PAIR):
        span = slice(pair * PAIR, (pair + 1) * PAIR)
        q_pair = q_ref[:, span]
        g_pair = g_ref[:, span]
        product = (g_pair.astype(F32) * mix_ref[:, span].astype(F32)).T
        heads = []
        for half in range(2):
            own = low if half == 0 else jnp.logical_not(low)
            inner = jnp.sum(product[half * HEAD : (half + 1) * HEAD], axis=0, keepdims=True)
            row = pair * 2 + half
            heads.append(
                (
                    jnp.where(own, q_pair, jnp.zeros_like(q_pair)),
                    jnp.where(own, g_pair, jnp.zeros_like(g_pair)),
                    inner,
                    lse_ref[0, row : row + 1, :],
                )
            )
        dq_parts = [jnp.zeros((HEAD, tokens), F32)] * 2
        for s in range(chunks):
            rows = slice(s * tokens, (s + 1) * tokens)
            k_pair = k_ref[rows, span]
            v_pair = v_ref[rows, span]
            k_turned = k_pair.astype(F32).T.astype(BF16)
            dk = None
            for half, (q_head, g_head, inner, lse) in enumerate(heads):
                score = dot_nt(k_pair, q_head) + mask_ref[rows, :]
                prob = jnp.exp(score - lse)
                g_score = (prob * (dot_nt(v_pair, g_head) - inner)).astype(BF16)
                part_v = dot_nn(prob.astype(BF16), g_head)
                part_k = dot_nn(g_score, q_head)
                dk = part_k if dk is None else dk + part_k
                dv = part_v if half == 0 else dv + part_v
                dq_parts[half] = dq_parts[half] + dot_nn(k_turned[half * HEAD : (half + 1) * HEAD], g_score)
            columns = pl.ds(pl.multiple_of(quad * QUAD, QUAD) + pair * PAIR, PAIR)
            dkv_ref[rows, columns] = dk.astype(BF16)
            columns = pl.ds(pl.multiple_of(quad * QUAD, QUAD) + (width + pair * PAIR), PAIR)
            dkv_ref[rows, columns] = dv.astype(BF16)
        dq = jnp.concatenate(dq_parts, axis=0).T * (HEAD**-0.5)
        dq_ref[:, pl.ds(pl.multiple_of(quad * QUAD, QUAD) + pair * PAIR, PAIR)] = dq.astype(BF16)

    @pl.when(quad == pl.num_programs(0) - 1)
    def _():
        pltpu.make_async_copy(w_ref, w_held, w_sem).wait()
        rank_row = lax.broadcasted_iota(jnp.int32, (8, width), 0) < 4
        up_grad = jnp.zeros((8, width), F32)
        reduce_grad = jnp.zeros((8, width), F32)
        for s in range(chunks - 1, -1, -1):
            rows = slice(s * tokens, (s + 1) * tokens)
            dkv = dkv_ref[rows, :]
            grad = dot_nt(dkv, w_held[:, width:])
            if s == 0:
                grad = grad + dot_nt(dq_ref[...], w_held[:, :width])
            grads[s][...] = grad.astype(grads[s].dtype)
            dv = dkv_ref[rows, width:]
            down = down_ref[:, rows]
            up_grad = up_grad + dot_nn(down, dv)
            g_down = dot_nt(dv, up_ref[...]).T[:8].astype(BF16)
            reduce_grad = reduce_grad + dot_nn(g_down, hidden[s][...])
        dq = dq_ref[...]
        g_down = dot_nt(dq, up_ref[...]).T[:8].astype(BF16)
        up_out[...] = jnp.where(rank_row, dot_nn(down_ref[:, :tokens], dq), up_grad)
        reduce_out[...] = jnp.where(rank_row, dot_nn(g_down, hidden[0][...]), reduce_grad)


def whole(shape):
    return pl.BlockSpec(shape, lambda i: (0,) * len(shape))


def run_forward(place, start, hidden, weight, query_bias, value_bias, reduce_wide):
    chunks = len(hidden)
    tokens, width = hidden[0].shape
    length = chunks * tokens
    quads = width // QUAD
    flops = 2 * width * width * (tokens + 2 * length) + 4 * tokens * length * width
    return pl.pallas_call(
        partial(forward_kernel, chunks),
        grid=(quads,),
        in_specs=[pl.BlockSpec(memory_space=pltpu.SMEM), whole((tokens, 1))]
        + [whole((tokens, width))] * chunks
        + [
            pl.BlockSpec((width, QUAD), lambda i: (0, i)),
            pl.BlockSpec((width, QUAD), lambda i: (0, i + quads)),
            pl.BlockSpec((width, QUAD), lambda i: (0, i + 2 * quads)),
            pl.BlockSpec((1, QUAD), lambda i: (0, i)),
            pl.BlockSpec((1, QUAD), lambda i: (0, i)),
            whole((width, PAIR)),
        ],
        out_specs=[
            pl.BlockSpec((tokens, QUAD), lambda i: (0, i)),
            pl.BlockSpec((length, QUAD), lambda i: (0, i)),
            pl.BlockSpec((length, QUAD), lambda i: (0, i)),
            pl.BlockSpec((tokens, QUAD), lambda i: (0, i)),
            pl.BlockSpec((1, 8, tokens), lambda i: (i, 0, 0)),
            whole((8, length)),
        ],
        out_shape=[
            jax.ShapeDtypeStruct((tokens, width), BF16),
            jax.ShapeDtypeStruct((length, width), BF16),
            jax.ShapeDtypeStruct((length, width), BF16),
            jax.ShapeDtypeStruct((tokens, width), BF16),
            jax.ShapeDtypeStruct((quads, 8, tokens), F32),
            jax.ShapeDtypeStruct((8, length), BF16),
        ],
        scratch_shapes=[pltpu.VMEM((tokens, length), F32)],
        compiler_params=pltpu.CompilerParams(vmem_limit_bytes=VMEM_BYTES),
        cost_estimate=pl.CostEstimate(
            flops=flops, bytes_accessed=8 * width * width + 10 * length * width,
            transcendentals=tokens * length * width // HEAD,
        ),
        name="attend_forward",
    )(place, start, *hidden, weight, weight, weight, query_bias, value_bias, reduce_wide)


def run_feed(mixed, x, grad_out, out_weight, vectors, fc_weight, fc_bias, proj_weight):
    tokens, width = x.shape
    hidden_units = fc_weight.shape[1]
    block = 1024
    out_bias, gain, shift, proj_bias = vectors
    return pl.pallas_call(
        feed_kernel,
        grid=(hidden_units // block,),
        in_specs=[whole((tokens, width))] * 3
        + [whole((width, width))]
        + [whole((1, width))] * 4
        + [
            pl.BlockSpec((width, block), lambda i: (0, i)),
            pl.BlockSpec((1, block), lambda i: (0, i)),
            pl.BlockSpec((block, width), lambda i: (i, 0)),
        ],
        out_specs=[whole((tokens, width))] * 3,
        out_shape=[
            jax.ShapeDtypeStruct((tokens, width), BF16),
            jax.ShapeDtypeStruct((tokens, width), F32),
            jax.ShapeDtypeStruct((tokens, width), BF16),
        ],
        scratch_shapes=[
            pltpu.VMEM((tokens, width), F32),
            pltpu.VMEM((tokens, width), BF16),
            pltpu.VMEM((tokens, width), F32),
            pltpu.VMEM((tokens, width), F32),
        ],
        compiler_params=pltpu.CompilerParams(vmem_limit_bytes=VMEM_BYTES),
        cost_estimate=pl.CostEstimate(
            flops=2 * tokens * width * (4 * hidden_units + 2 * width),
            bytes_accessed=2 * width * (2 * hidden_units + width) + 16 * tokens * width,
            transcendentals=tokens * hidden_units,
        ),
        name="feed",
    )(mixed, x, grad_out, out_weight, out_bias, gain, shift, proj_bias, fc_weight, fc_bias, proj_weight)


def run_backward(place, start, hidden, q, k, v, mixed, g_mixed, lse, down, up_wide, weight):
    chunks = len(hidden)
    tokens, width = hidden[0].shape
    length = chunks * tokens
    quads = width // QUAD
    flops = 2 * width * width * (tokens + 2 * length) + 10 * tokens * length * width
    own = pl.BlockSpec((tokens, QUAD), lambda i: (0, i))
    every = pl.BlockSpec((length, QUAD), lambda i: (0, i))
    return pl.pallas_call(
        partial(backward_kernel, chunks),
        grid=(quads,),
        in_specs=[pl.BlockSpec(memory_space=pltpu.SMEM), whole((1, tokens))]
        + [whole((tokens, width))] * chunks
        + [
            own, every, every, own, own,
            pl.BlockSpec((1, 8, tokens), lambda i: (i, 0, 0)),
            whole((8, length)),
            whole((PAIR, width)),
            pl.BlockSpec(memory_space=pl.ANY),
        ],
        out_specs=[whole((tokens, width))] * chunks + [whole((8, width))] * 2,
        out_shape=[jax.ShapeDtypeStruct((tokens, width), F32 if s == 0 else BF16) for s in range(chunks)]
        + [jax.ShapeDtypeStruct((8, width), F32)] * 2,
        scratch_shapes=[
            pltpu.VMEM((length, tokens), F32),
            pltpu.VMEM((tokens, width), BF16),
            pltpu.VMEM((length, 2 * width), BF16),
            pltpu.VMEM((width, 3 * width), BF16),
            pltpu.SemaphoreType.DMA,
        ],
        compiler_params=pltpu.CompilerParams(vmem_limit_bytes=VMEM_BYTES),
        cost_estimate=pl.CostEstimate(
            flops=flops, bytes_accessed=6 * width * width + 14 * length * width,
            transcendentals=tokens * length * width // HEAD,
        ),
        name="attend_backward",
    )(place, start, *hidden, q, k, v, mixed, g_mixed, lse, down, up_wide, weight)


def on_device(
    seq,
    block_input,
    seg_start,
    ln1_gain,
    ln1_bias,
    qkv_weight,
    query_bias,
    value_bias,
    query_adapter_reduce,
    query_up,
    value_adapter_reduce,
    value_up,
    out_weight,
    out_bias,
    ln2_gain,
    ln2_bias,
    fc_weight,
    fc_bias,
    proj_weight,
    proj_bias,
    grad_out,
):
    rows, tokens, width = block_input.shape
    rank = query_up.shape[0]
    shard = qkv_weight.shape[0]
    place = lax.axis_index("seq")
    upward = [(i, i + 1) for i in range(seq - 1)]
    downward = [(i + 1, i) for i in range(seq - 1)]

    def own_rows(reduce):
        return lax.dynamic_slice(reduce, (lax.axis_index("dp") * shard, 0), (shard, rank))

    def folded(part, reduce, up):
        change = jnp.dot(own_rows(reduce), up, preferred_element_type=F32) * ADAPTER_SCALE
        return (part.astype(F32) + change).astype(BF16)

    weight_shard = jnp.concatenate(
        [
            folded(qkv_weight[:, :width], query_adapter_reduce, query_up),
            qkv_weight[:, width : 2 * width],
            folded(qkv_weight[:, 2 * width :], value_adapter_reduce, value_up),
        ],
        axis=1,
    )
    weight = lax.all_gather(weight_shard, "dp", axis=0, tiled=True)
    whole_out = lax.all_gather(out_weight, "dp", axis=0, tiled=True)
    whole_fc = lax.all_gather(fc_weight, "dp", axis=0, tiled=True)
    whole_proj = lax.all_gather(proj_weight, "dp", axis=0, tiled=True)

    pad = jnp.zeros((width, PAIR - 2 * rank), BF16)
    reduce_wide = jnp.concatenate([query_adapter_reduce, value_adapter_reduce, pad], axis=1)
    up_wide = jnp.concatenate([query_up, value_up, pad.T], axis=0)
    starts = lax.dynamic_slice(seg_start, (0, place * tokens), (rows, tokens))
    place_ref = place.astype(jnp.int32).reshape(1)

    def as_row(vector):
        return vector.reshape(1, -1)

    vectors = tuple(as_row(a) for a in (out_bias, ln2_gain, ln2_bias, proj_bias))

    hidden_rows = []
    for r in range(rows):
        normed, _ = norm_parts(block_input[r].astype(F32))
        first = (normed * ln1_gain + ln1_bias).astype(BF16)
        hidden = [first]
        for _ in range(seq - 1):
            hidden.append(lax.ppermute(hidden[-1], "seq", upward))
        hidden_rows.append(hidden)

    outs, grads, reduce_sum, up_sum = [], [], 0.0, 0.0
    for r in range(rows):
        hidden = hidden_rows[r]
        q, k, v, mixed, lse, down = run_forward(
            place_ref, starts[r].reshape(tokens, 1), hidden, weight, as_row(query_bias), as_row(value_bias), reduce_wide
        )
        out, g_middle, g_mixed = run_feed(
            mixed, block_input[r], grad_out[r], whole_out, vectors, whole_fc, as_row(fc_bias), whole_proj
        )
        outs.append(out)
        result = run_backward(
            place_ref, starts[r].reshape(1, tokens), hidden, q, k, v, mixed, g_mixed, lse, down, up_wide, weight
        )
        reduce_sum = reduce_sum + result[seq]
        up_sum = up_sum + result[seq + 1]
        moving = result[seq - 1]
        for s in range(seq - 2, -1, -1):
            arrived = lax.ppermute(moving, "seq", downward)
            total = result[s].astype(F32) + arrived.astype(F32)
            moving = total.astype(BF16)
        normed, inverse = norm_parts(block_input[r].astype(F32))
        grads.append(g_middle + norm_backward(total, normed, inverse, ln1_gain))

    summed = lax.psum(jnp.concatenate([reduce_sum * ADAPTER_SCALE, up_sum], axis=0), ("dp", "seq"))
    return (
        jnp.stack(outs),
        jnp.stack(grads),
        summed[:rank].T,
        summed[8 : 8 + rank],
        summed[rank : 2 * rank].T,
        summed[8 + rank : 8 + 2 * rank],
    )


def solution(mesh):
    return jax.shard_map(
        partial(on_device, mesh.shape["seq"]),
        mesh=mesh,
        in_specs=(
            P("dp", "seq", None),
            P("dp", None),
            P(),
            P(),
            P("dp", None),
            P(),
            P(),
            P(),
            P(),
            P(),
            P(),
            P("dp", None),
            P(),
            P(),
            P(),
            P("dp", None),
            P(),
            P("dp", None),
            P(),
            P("dp", "seq", None),
        ),
        out_specs=(P("dp", "seq", None), P("dp", "seq", None), P(), P(), P(), P()),
        check_vma=False,
    )
```

```python
from functools import partial

import jax
import jax.numpy as jnp
from jax import lax
from jax.experimental import pallas as pl
from jax.experimental.pallas import tpu as pltpu
from jax.sharding import PartitionSpec as P

HEAD = 64
QUAD = 256
PAIR = 128
NORM_EPSILON = 1e-05
ADAPTER_SCALE = 8.0
MASKED = -1e30
GELU_A = 0.7978845608028654
GELU_B = 0.044715

F32 = jnp.float32
BF16 = jnp.bfloat16
VMEM_BYTES = 56 * 1024 * 1024


def dot_nn(left, right):
    return lax.dot_general(left, right, (((1,), (0,)), ((), ())), preferred_element_type=F32)


def dot_nt(left, right):
    return lax.dot_general(left, right, (((1,), (1,)), ((), ())), preferred_element_type=F32)


def norm_parts(values):
    average = jnp.mean(values, axis=-1, keepdims=True)
    centered = values - average
    inverse = lax.rsqrt(jnp.mean(centered * centered, axis=-1, keepdims=True) + NORM_EPSILON)
    return centered * inverse, inverse


def norm_backward(gradient, normed, inverse, gain):
    scaled = gradient * gain
    return inverse * (
        scaled
        - jnp.mean(scaled, axis=-1, keepdims=True)
        - normed * jnp.mean(scaled * normed, axis=-1, keepdims=True)
    )


def head_lanes(rows, dtype):
    lane = lax.broadcasted_iota(jnp.int32, (rows, PAIR), 1)
    return lane < HEAD


def forward_kernel(chunks, place_ref, start_ref, *refs):
    hidden = refs[:chunks]
    wq, wk, wv, bias_q, bias_v, reduce_ref = refs[chunks : chunks + 6]
    q_out, k_out, v_out, mix_out, lse_out, down_out, mask_ref = refs[chunks + 6 :]
    tokens = hidden[0].shape[0]
    quad = pl.program_id(0)

    @pl.when(quad == 0)
    def _():
        place = place_ref[0]
        query = place * tokens + lax.broadcasted_iota(jnp.int32, (tokens, tokens), 0)
        start = start_ref[...]
        for s in range(chunks):
            key = (place - s) * tokens + lax.broadcasted_iota(jnp.int32, (tokens, tokens), 1)
            allowed = key >= start
            if s == 0:
                allowed = allowed & (key <= query)
            mask_ref[:, s * tokens : (s + 1) * tokens] = jnp.where(allowed, 0.0, MASKED)
            down = dot_nn(hidden[s][...], reduce_ref[...]) * ADAPTER_SCALE
            down_out[:, s * tokens : (s + 1) * tokens] = down.T[:8].astype(BF16)

    q_out[...] = ((dot_nn(hidden[0][...], wq[...]) + bias_q[...]).astype(BF16) * (HEAD**-0.5)).astype(BF16)
    for s in range(chunks):
        span = slice(s * tokens, (s + 1) * tokens)
        k_out[span, :] = dot_nn(hidden[s][...], wk[...]).astype(BF16)
        v_out[span, :] = (dot_nn(hidden[s][...], wv[...]) + bias_v[...]).astype(BF16)
    low = head_lanes(tokens, BF16)
    lane = lax.broadcasted_iota(jnp.int32, (tokens, PAIR), 1)
    totals = jnp.zeros((tokens, PAIR), F32)
    for pair in range(QUAD // PAIR):
        span = slice(pair * PAIR, (pair + 1) * PAIR)
        q_pair = q_out[:, span]
        mixed = []
        for half in range(2):
            own = low if half == 0 else jnp.logical_not(low)
            q_head = jnp.where(own, q_pair, jnp.zeros_like(q_pair))
            score = dot_nt(q_head, k_out[:, span]) + mask_ref[...]
            highest = jnp.max(score, axis=-1, keepdims=True)
            weight = jnp.exp(score - highest)
            total = jnp.sum(weight, axis=-1, keepdims=True)
            mixed.append(dot_nn(weight.astype(BF16), v_out[:, span]) * (1.0 / total))
            totals = jnp.where(lane == pair * 2 + half, highest + jnp.log(total), totals)
        mix_out[:, span] = jnp.where(low, mixed[0], mixed[1]).astype(BF16)
    lse_out[0] = totals.T[:8]


def feed_kernel(
    mix_ref, x_ref, gout_ref, wo_ref, out_bias, gain, shift, proj_bias, fc_ref, fc_bias, proj_ref,
    out_ref, gmid_ref, gmix_ref, middle_ref, hidden_ref, acc_ref, grad_ref,
):
    step = pl.program_id(0)

    @pl.when(step == 0)
    def _():
        middle = x_ref[...].astype(F32) + dot_nn(mix_ref[...], wo_ref[...]) + out_bias[...]
        middle_ref[...] = middle
        normed, _ = norm_parts(middle)
        hidden_ref[...] = (normed * gain[...] + shift[...]).astype(BF16)

    before = dot_nn(hidden_ref[...], fc_ref[...]) + fc_bias[...]
    square = before * before
    bend = jnp.tanh(GELU_A * before * (1.0 + GELU_B * square))
    half = 0.5 * (1.0 + bend)
    slope = half + 0.5 * before * (1.0 - bend * bend) * (GELU_A * (1.0 + 3.0 * GELU_B * square))
    act = (before * half).astype(BF16)
    g_before = (dot_nt(gout_ref[...], proj_ref[...]) * slope).astype(BF16)
    fed = dot_nn(act, proj_ref[...])
    back = dot_nt(g_before, fc_ref[...])

    @pl.when(step == 0)
    def _():
        acc_ref[...] = fed
        grad_ref[...] = back

    @pl.when(step > 0)
    def _():
        acc_ref[...] += fed
        grad_ref[...] += back

    @pl.when(step == pl.num_programs(0) - 1)
    def _():
        middle = middle_ref[...]
        out_ref[...] = (middle + acc_ref[...] + proj_bias[...]).astype(BF16)
        normed, inverse = norm_parts(middle)
        g_middle = gout_ref[...].astype(F32) + norm_backward(grad_ref[...], normed, inverse, gain[...])
        gmid_ref[...] = g_middle
        gmix_ref[...] = dot_nt(g_middle.astype(BF16), wo_ref[...]).astype(BF16)


def backward_kernel(chunks, place_ref, start_ref, *refs):
    hidden = refs[:chunks]
    q_ref, k_ref, v_ref, mix_ref, g_ref, lse_ref, down_ref, up_ref, w_ref = refs[chunks : chunks + 9]
    grads = refs[chunks + 9 : 2 * chunks + 9]
    reduce_out, up_out, mask_ref, dq_ref, dkv_ref, w_held, w_sem = refs[2 * chunks + 9 :]
    tokens = hidden[0].shape[0]
    width = hidden[0].shape[1]
    quad = pl.program_id(0)

    @pl.when(quad == 0)
    def _():
        pltpu.make_async_copy(w_ref, w_held, w_sem).start()
        place = place_ref[0]
        query = place * tokens + lax.broadcasted_iota(jnp.int32, (tokens, tokens), 1)
        start = start_ref[...]
        for s in range(chunks):
            key = (place - s) * tokens + lax.broadcasted_iota(jnp.int32, (tokens, tokens), 0)
            allowed = key >= start
            if s == 0:
                allowed = allowed & (key <= query)
            mask_ref[s * tokens : (s + 1) * tokens, :] = jnp.where(allowed, 0.0, MASKED)

    low = head_lanes(tokens, BF16)
    for pair in range(QUAD // PAIR):
        span = slice(pair * PAIR, (pair + 1) * PAIR)
        q_pair = q_ref[:, span]
        g_pair = g_ref[:, span]
        product = (g_pair.astype(F32) * mix_ref[:, span].astype(F32)).T
        heads = []
        for half in range(2):
            own = low if half == 0 else jnp.logical_not(low)
            inner = jnp.sum(product[half * HEAD : (half + 1) * HEAD], axis=0, keepdims=True)
            row = pair * 2 + half
            heads.append(
                (
                    jnp.where(own, q_pair, jnp.zeros_like(q_pair)),
                    jnp.where(own, g_pair, jnp.zeros_like(g_pair)),
                    inner,
                    lse_ref[0, row : row + 1, :],
                )
            )
        dq_parts = [jnp.zeros((HEAD, tokens), F32)] * 2
        for s in range(chunks):
            rows = slice(s * tokens, (s + 1) * tokens)
            k_pair = k_ref[rows, span]
            v_pair = v_ref[rows, span]
            k_turned = k_pair.astype(F32).T.astype(BF16)
            dk = None
            for half, (q_head, g_head, inner, lse) in enumerate(heads):
                score = dot_nt(k_pair, q_head) + mask_ref[rows, :]
                prob = jnp.exp(score - lse)
                g_score = (prob * (dot_nt(v_pair, g_head) - inner)).astype(BF16)
                part_v = dot_nn(prob.astype(BF16), g_head)
                part_k = dot_nn(g_score, q_head)
                dk = part_k if dk is None else dk + part_k
                dv = part_v if half == 0 else dv + part_v
                dq_parts[half] = dq_parts[half] + dot_nn(k_turned[half * HEAD : (half + 1) * HEAD], g_score)
            columns = pl.ds(pl.multiple_of(quad * QUAD, QUAD) + pair * PAIR, PAIR)
            dkv_ref[rows, columns] = dk.astype(BF16)
            columns = pl.ds(pl.multiple_of(quad * QUAD, QUAD) + (width + pair * PAIR), PAIR)
            dkv_ref[rows, columns] = dv.astype(BF16)
        dq = jnp.concatenate(dq_parts, axis=0).T * (HEAD**-0.5)
        dq_ref[:, pl.ds(pl.multiple_of(quad * QUAD, QUAD) + pair * PAIR, PAIR)] = dq.astype(BF16)

    @pl.when(quad == pl.num_programs(0) - 1)
    def _():
        pltpu.make_async_copy(w_ref, w_held, w_sem).wait()
        rank_row = lax.broadcasted_iota(jnp.int32, (8, width), 0) < 4
        up_grad = jnp.zeros((8, width), F32)
        reduce_grad = jnp.zeros((8, width), F32)
        for s in range(chunks - 1, -1, -1):
            rows = slice(s * tokens, (s + 1) * tokens)
            dkv = dkv_ref[rows, :]
            grad = dot_nt(dkv, w_held[:, width:])
            if s == 0:
                grad = grad + dot_nt(dq_ref[...], w_held[:, :width])
            grads[s][...] = grad.astype(grads[s].dtype)
            dv = dkv_ref[rows, width:]
            down = down_ref[:, rows]
            up_grad = up_grad + dot_nn(down, dv)
            g_down = dot_nt(dv, up_ref[...]).T[:8].astype(BF16)
            reduce_grad = reduce_grad + dot_nn(g_down, hidden[s][...])
        dq = dq_ref[...]
        g_down = dot_nt(dq, up_ref[...]).T[:8].astype(BF16)
        up_out[...] = jnp.where(rank_row, dot_nn(down_ref[:, :tokens], dq), up_grad)
        reduce_out[...] = jnp.where(rank_row, dot_nn(g_down, hidden[0][...]), reduce_grad)


def whole(shape):
    return pl.BlockSpec(shape, lambda i: (0,) * len(shape))


def run_forward(place, start, hidden, weight, query_bias, value_bias, reduce_wide):
    chunks = len(hidden)
    tokens, width = hidden[0].shape
    length = chunks * tokens
    quads = width // QUAD
    flops = 2 * width * width * (tokens + 2 * length) + 4 * tokens * length * width
    return pl.pallas_call(
        partial(forward_kernel, chunks),
        grid=(quads,),
        in_specs=[pl.BlockSpec(memory_space=pltpu.SMEM), whole((tokens, 1))]
        + [whole((tokens, width))] * chunks
        + [
            pl.BlockSpec((width, QUAD), lambda i: (0, i)),
            pl.BlockSpec((width, QUAD), lambda i: (0, i + quads)),
            pl.BlockSpec((width, QUAD), lambda i: (0, i + 2 * quads)),
            pl.BlockSpec((1, QUAD), lambda i: (0, i)),
            pl.BlockSpec((1, QUAD), lambda i: (0, i)),
            whole((width, PAIR)),
        ],
        out_specs=[
            pl.BlockSpec((tokens, QUAD), lambda i: (0, i)),
            pl.BlockSpec((length, QUAD), lambda i: (0, i)),
            pl.BlockSpec((length, QUAD), lambda i: (0, i)),
            pl.BlockSpec((tokens, QUAD), lambda i: (0, i)),
            pl.BlockSpec((1, 8, tokens), lambda i: (i, 0, 0)),
            whole((8, length)),
        ],
        out_shape=[
            jax.ShapeDtypeStruct((tokens, width), BF16),
            jax.ShapeDtypeStruct((length, width), BF16),
            jax.ShapeDtypeStruct((length, width), BF16),
            jax.ShapeDtypeStruct((tokens, width), BF16),
            jax.ShapeDtypeStruct((quads, 8, tokens), F32),
            jax.ShapeDtypeStruct((8, length), BF16),
        ],
        scratch_shapes=[pltpu.VMEM((tokens, length), F32)],
        compiler_params=pltpu.CompilerParams(vmem_limit_bytes=VMEM_BYTES),
        cost_estimate=pl.CostEstimate(
            flops=flops, bytes_accessed=8 * width * width + 10 * length * width,
            transcendentals=tokens * length * width // HEAD,
        ),
        name="attend_forward",
    )(place, start, *hidden, weight, weight, weight, query_bias, value_bias, reduce_wide)


def run_feed(mixed, x, grad_out, out_weight, vectors, fc_weight, fc_bias, proj_weight):
    tokens, width = x.shape
    hidden_units = fc_weight.shape[1]
    block = 1024
    out_bias, gain, shift, proj_bias = vectors
    return pl.pallas_call(
        feed_kernel,
        grid=(hidden_units // block,),
        in_specs=[whole((tokens, width))] * 3
        + [whole((width, width))]
        + [whole((1, width))] * 4
        + [
            pl.BlockSpec((width, block), lambda i: (0, i)),
            pl.BlockSpec((1, block), lambda i: (0, i)),
            pl.BlockSpec((block, width), lambda i: (i, 0)),
        ],
        out_specs=[whole((tokens, width))] * 3,
        out_shape=[
            jax.ShapeDtypeStruct((tokens, width), BF16),
            jax.ShapeDtypeStruct((tokens, width), F32),
            jax.ShapeDtypeStruct((tokens, width), BF16),
        ],
        scratch_shapes=[
            pltpu.VMEM((tokens, width), F32),
            pltpu.VMEM((tokens, width), BF16),
            pltpu.VMEM((tokens, width), F32),
            pltpu.VMEM((tokens, width), F32),
        ],
        compiler_params=pltpu.CompilerParams(vmem_limit_bytes=VMEM_BYTES),
        cost_estimate=pl.CostEstimate(
            flops=2 * tokens * width * (4 * hidden_units + 2 * width),
            bytes_accessed=2 * width * (2 * hidden_units + width) + 16 * tokens * width,
            transcendentals=tokens * hidden_units,
        ),
        name="feed",
    )(mixed, x, grad_out, out_weight, out_bias, gain, shift, proj_bias, fc_weight, fc_bias, proj_weight)


def run_backward(place, start, hidden, q, k, v, mixed, g_mixed, lse, down, up_wide, weight):
    chunks = len(hidden)
    tokens, width = hidden[0].shape
    length = chunks * tokens
    quads = width // QUAD
    flops = 2 * width * width * (tokens + 2 * length) + 10 * tokens * length * width
    own = pl.BlockSpec((tokens, QUAD), lambda i: (0, i))
    every = pl.BlockSpec((length, QUAD), lambda i: (0, i))
    return pl.pallas_call(
        partial(backward_kernel, chunks),
        grid=(quads,),
        in_specs=[pl.BlockSpec(memory_space=pltpu.SMEM), whole((1, tokens))]
        + [whole((tokens, width))] * chunks
        + [
            own, every, every, own, own,
            pl.BlockSpec((1, 8, tokens), lambda i: (i, 0, 0)),
            whole((8, length)),
            whole((PAIR, width)),
            pl.BlockSpec(memory_space=pl.ANY),
        ],
        out_specs=[whole((tokens, width))] * chunks + [whole((8, width))] * 2,
        out_shape=[jax.ShapeDtypeStruct((tokens, width), F32 if s == 0 else BF16) for s in range(chunks)]
        + [jax.ShapeDtypeStruct((8, width), F32)] * 2,
        scratch_shapes=[
            pltpu.VMEM((length, tokens), F32),
            pltpu.VMEM((tokens, width), BF16),
            pltpu.VMEM((length, 2 * width), BF16),
            pltpu.VMEM((width, 3 * width), BF16),
            pltpu.SemaphoreType.DMA,
        ],
        compiler_params=pltpu.CompilerParams(vmem_limit_bytes=VMEM_BYTES),
        cost_estimate=pl.CostEstimate(
            flops=flops, bytes_accessed=6 * width * width + 14 * length * width,
            transcendentals=tokens * length * width // HEAD,
        ),
        name="attend_backward",
    )(place, start, *hidden, q, k, v, mixed, g_mixed, lse, down, up_wide, weight)


def sum_kernel(dp, seq, part_ref, out_ref, plane_ref, line_ref, send_sems, recv_sems):
    me, place = lax.axis_index("dp"), lax.axis_index("seq")
    barrier = pltpu.get_barrier_semaphore()
    mesh_type = pl.DeviceIdType.MESH

    def peer(delta):
        return lax.rem(me + delta, dp), place

    def line_peer(delta):
        return me, lax.rem(place + delta, seq)

    for delta in range(1, dp):
        pl.semaphore_signal(barrier, inc=1, device_id=peer(delta), device_id_type=mesh_type)
    for delta in range(1, seq):
        pl.semaphore_signal(barrier, inc=1, device_id=line_peer(delta), device_id_type=mesh_type)
    pl.semaphore_wait(barrier, dp + seq - 2)

    def send(source, target, slot, device):
        copy = pltpu.make_async_remote_copy(
            src_ref=source, dst_ref=target, send_sem=send_sems.at[slot], recv_sem=recv_sems.at[slot],
            device_id=device, device_id_type=mesh_type,
        )
        copy.start()
        return copy

    copies = [
        send(part_ref.at[lax.rem(me + delta, dp)], plane_ref.at[delta], delta, peer(delta))
        for delta in range(1, dp)
    ]
    total = part_ref[me]
    for delta in range(1, dp):
        copies[delta - 1].wait()
        total = total + plane_ref[delta]
    line_ref[place] = total
    copies = [
        send(line_ref.at[place], line_ref.at[place], dp + delta, line_peer(delta)) for delta in range(1, seq)
    ]
    for copy in copies:
        copy.wait()
    total = line_ref[0]
    for index in range(1, seq):
        total = total + line_ref[index]
    out_ref[me] = total
    copies = [
        send(out_ref.at[me], out_ref.at[me], dp + seq + delta, peer(delta)) for delta in range(1, dp)
    ]
    for copy in copies:
        copy.wait()


def run_sum(dp, seq, part):
    rows, width = part.shape
    piece = max(8, rows * width // (PAIR * dp))
    flat = part.reshape(-1, PAIR)
    used = flat.shape[0]
    flat = jnp.pad(flat, ((0, dp * piece - used), (0, 0)))
    slots = 2 * dp + seq
    total = pl.pallas_call(
        partial(sum_kernel, dp, seq),
        in_specs=[pl.BlockSpec(memory_space=pltpu.VMEM)],
        out_specs=pl.BlockSpec(memory_space=pltpu.VMEM),
        out_shape=jax.ShapeDtypeStruct((dp, piece, PAIR), F32),
        scratch_shapes=[
            pltpu.VMEM((dp, piece, PAIR), F32),
            pltpu.VMEM((seq, piece, PAIR), F32),
            pltpu.SemaphoreType.DMA((slots,)),
            pltpu.SemaphoreType.DMA((slots,)),
        ],
        compiler_params=pltpu.CompilerParams(collective_id=1, has_side_effects=True),
        name="sum_all",
    )(flat.reshape(dp, piece, PAIR))
    return total.reshape(-1, PAIR)[:used].reshape(rows, width)


def on_device(
    dp,
    seq,
    block_input,
    seg_start,
    ln1_gain,
    ln1_bias,
    qkv_weight,
    query_bias,
    value_bias,
    query_adapter_reduce,
    query_up,
    value_adapter_reduce,
    value_up,
    out_weight,
    out_bias,
    ln2_gain,
    ln2_bias,
    fc_weight,
    fc_bias,
    proj_weight,
    proj_bias,
    grad_out,
):
    rows, tokens, width = block_input.shape
    rank = query_up.shape[0]
    shard = qkv_weight.shape[0]
    place = lax.axis_index("seq")
    upward = [(i, i + 1) for i in range(seq - 1)]
    downward = [(i + 1, i) for i in range(seq - 1)]

    def own_rows(reduce):
        return lax.dynamic_slice(reduce, (lax.axis_index("dp") * shard, 0), (shard, rank))

    def folded(part, reduce, up):
        change = jnp.dot(own_rows(reduce), up, preferred_element_type=F32) * ADAPTER_SCALE
        return (part.astype(F32) + change).astype(BF16)

    weight_shard = jnp.concatenate(
        [
            folded(qkv_weight[:, :width], query_adapter_reduce, query_up),
            qkv_weight[:, width : 2 * width],
            folded(qkv_weight[:, 2 * width :], value_adapter_reduce, value_up),
        ],
        axis=1,
    )
    weight = lax.all_gather(weight_shard, "dp", axis=0, tiled=True)
    whole_out = lax.all_gather(out_weight, "dp", axis=0, tiled=True)
    whole_fc = lax.all_gather(fc_weight, "dp", axis=0, tiled=True)
    whole_proj = lax.all_gather(proj_weight, "dp", axis=0, tiled=True)

    pad = jnp.zeros((width, PAIR - 2 * rank), BF16)
    reduce_wide = jnp.concatenate([query_adapter_reduce, value_adapter_reduce, pad], axis=1)
    up_wide = jnp.concatenate([query_up, value_up, pad.T], axis=0)
    starts = lax.dynamic_slice(seg_start, (0, place * tokens), (rows, tokens))
    place_ref = place.astype(jnp.int32).reshape(1)

    def as_row(vector):
        return vector.reshape(1, -1)

    vectors = tuple(as_row(a) for a in (out_bias, ln2_gain, ln2_bias, proj_bias))

    hidden_rows = []
    for r in range(rows):
        normed, _ = norm_parts(block_input[r].astype(F32))
        first = (normed * ln1_gain + ln1_bias).astype(BF16)
        if r > 0:
            first = lax.optimization_barrier((first, hidden_rows[-1][-1]))[0]
        hidden = [first]
        for _ in range(seq - 1):
            hidden.append(lax.ppermute(hidden[-1], "seq", upward))
        hidden_rows.append(hidden)

    outs, grads, reduce_sum, up_sum = [], [], 0.0, 0.0
    for r in range(rows):
        hidden = hidden_rows[r]
        q, k, v, mixed, lse, down = run_forward(
            place_ref, starts[r].reshape(tokens, 1), hidden, weight, as_row(query_bias), as_row(value_bias), reduce_wide
        )
        out, g_middle, g_mixed = run_feed(
            mixed, block_input[r], grad_out[r], whole_out, vectors, whole_fc, as_row(fc_bias), whole_proj
        )
        outs.append(out)
        result = run_backward(
            place_ref, starts[r].reshape(1, tokens), hidden, q, k, v, mixed, g_mixed, lse, down, up_wide, weight
        )
        reduce_sum = reduce_sum + result[seq]
        up_sum = up_sum + result[seq + 1]
        moving = result[seq - 1]
        for s in range(seq - 2, -1, -1):
            arrived = lax.ppermute(moving, "seq", downward)
            total = result[s].astype(F32) + arrived.astype(F32)
            moving = total.astype(BF16)
        normed, inverse = norm_parts(block_input[r].astype(F32))
        grads.append(g_middle + norm_backward(total, normed, inverse, ln1_gain))

    summed = run_sum(dp, seq, jnp.concatenate([reduce_sum * ADAPTER_SCALE, up_sum], axis=0))
    return (
        jnp.stack(outs),
        jnp.stack(grads),
        summed[:rank].T,
        summed[8 : 8 + rank],
        summed[rank : 2 * rank].T,
        summed[8 + rank : 8 + 2 * rank],
    )


def solution(mesh):
    return jax.shard_map(
        partial(on_device, mesh.shape["dp"], mesh.shape["seq"]),
        mesh=mesh,
        in_specs=(
            P("dp", "seq", None),
            P("dp", None),
            P(),
            P(),
            P("dp", None),
            P(),
            P(),
            P(),
            P(),
            P(),
            P(),
            P("dp", None),
            P(),
            P(),
            P(),
            P("dp", None),
            P(),
            P("dp", None),
            P(),
            P("dp", "seq", None),
        ),
        out_specs=(P("dp", "seq", None), P("dp", "seq", None), P(), P(), P(), P()),
        check_vma=False,
    )
```

```python
import math
from functools import partial

import jax
import jax.numpy as jnp
from jax import lax
from jax.experimental import pallas as pl
from jax.experimental.pallas import tpu as pltpu
from jax.sharding import PartitionSpec as P

HEAD = 64
QUAD = 256
PAIR = 128
NORM_EPSILON = 1e-05
ADAPTER_SCALE = 8.0
MASKED = -1e30
GELU_A = 0.7978845608028654
GELU_B = 0.044715

F32 = jnp.float32
BF16 = jnp.bfloat16
VMEM_BYTES = 56 * 1024 * 1024


def dot_nn(left, right):
    return lax.dot_general(left, right, (((1,), (0,)), ((), ())), preferred_element_type=F32)


def dot_nt(left, right):
    return lax.dot_general(left, right, (((1,), (1,)), ((), ())), preferred_element_type=F32)


def norm_parts(values):
    average = jnp.mean(values, axis=-1, keepdims=True)
    centered = values - average
    inverse = lax.rsqrt(jnp.mean(centered * centered, axis=-1, keepdims=True) + NORM_EPSILON)
    return centered * inverse, inverse


def norm_backward(gradient, normed, inverse, gain):
    scaled = gradient * gain
    return inverse * (
        scaled
        - jnp.mean(scaled, axis=-1, keepdims=True)
        - normed * jnp.mean(scaled * normed, axis=-1, keepdims=True)
    )


def head_lanes(rows, dtype):
    lane = lax.broadcasted_iota(jnp.int32, (rows, PAIR), 1)
    return lane < HEAD


def start_kernel(
    plane, seq, rows,
    x_ref, start_ref, gain_ref, shift_ref, shard_ref, reduce_ref, up_ref, bias_q, bias_v, wo_in, fc_in, proj_in,
    w_out, wo_out, fc_out, proj_out, hidden_out, q_out, k_out, v_out, mix_out, lse_out, down_out,
    w_held, hidden, q_held, k_held, v_held, mix_held, mask_ref,
    send_sems, recv_sems, hop_send, hop_recv, own_sems, store_sems,
):
    nx, ny = plane
    tokens, width = x_ref.shape[1], x_ref.shape[2]
    length = seq * tokens
    mesh_type = pl.DeviceIdType.MESH
    me, place = lax.axis_index("dp"), lax.axis_index("seq")
    core = lax.rem(me, 2)
    my_x = lax.rem(me // 2, nx)
    my_y = me // (2 * nx)

    def index(y, x, c):
        return (y * nx + x) * 2 + c

    def x_peer(delta):
        return index(my_y, lax.rem(my_x + delta, nx), core), place

    def y_peer(delta):
        return index(lax.rem(my_y + delta, ny), my_x, core), place

    twin = (index(my_y, my_x, 1 - core), place)

    def owner(dy, dx, c):
        return index(lax.rem(my_y + ny - dy, ny), lax.rem(my_x + nx - dx, nx), c)

    barrier = pltpu.get_barrier_semaphore()
    for delta in range(1, nx):
        pl.semaphore_signal(barrier, inc=1, device_id=x_peer(delta), device_id_type=mesh_type)
    for delta in range(1, ny):
        pl.semaphore_signal(barrier, inc=1, device_id=y_peer(delta), device_id_type=mesh_type)
    pl.semaphore_signal(barrier, inc=1, device_id=twin, device_id_type=mesh_type)

    @pl.when(place > 0)
    def _():
        pl.semaphore_signal(barrier, inc=1, device_id=(me, place - 1), device_id_type=mesh_type)

    @pl.when(place < seq - 1)
    def _():
        pl.semaphore_signal(barrier, inc=1, device_id=(me, place + 1), device_id_type=mesh_type)

    shards = [shard_ref.shape[0], wo_in.shape[0], fc_in.shape[0], proj_in.shape[0]]
    sources = [None, wo_in, fc_in, proj_in]
    targets = [w_held, wo_out, fc_out, proj_out]

    def region(t, device, half=None):
        size = shards[t]
        if half is None:
            return targets[t].at[pl.ds(pl.multiple_of(device * size, size), size), :]
        part = size // 2
        return targets[t].at[pl.ds(pl.multiple_of(device * size + half * part, part), part), :]

    pending = []

    def send(t, slot, source, target, device):
        copy = pltpu.make_async_remote_copy(
            src_ref=source, dst_ref=target, send_sem=send_sems.at[t, slot], recv_sem=recv_sems.at[t, slot],
            device_id=device, device_id_type=mesh_type,
        )
        copy.start()
        pending.append(copy)
        return copy

    first_x, first_y = nx - 1, nx - 1 + ny - 1
    cross = (nx - 1) * (ny - 1)

    def slot_a(dy, dx):
        return first_y + (dy - 1) * (nx - 1) + dx - 1

    def slot_b(dy, dx):
        return first_y + cross + (dy - 1) * (nx - 1) + dx - 1

    def slot_twin(dy, dx):
        return first_y + 2 * cross + dy * nx + dx

    flights = {}

    def wave_one(t):
        mine = region(t, me) if sources[t] is None else sources[t]
        for delta in range(1, nx):
            flights[t, "x", delta] = send(t, delta - 1, mine, region(t, me), x_peer(delta))
        for delta in range(1, ny):
            flights[t, "y", delta] = send(t, first_x + delta - 1, mine, region(t, me), y_peer(delta))
        flights[t, "t", 0, 0] = send(t, slot_twin(0, 0), mine, region(t, me), twin)

    def wave_two(t):
        for dx in range(1, nx):
            flights[t, "x", dx].wait_recv()
            device = owner(0, dx, core)
            for dy in range(1, ny):
                part = region(t, device, 0)
                flights[t, "a", dy, dx] = send(t, slot_a(dy, dx), part, part, y_peer(dy))
        for dy in range(1, ny):
            flights[t, "y", dy].wait_recv()
            device = owner(dy, 0, core)
            for dx in range(1, nx):
                part = region(t, device, 1)
                flights[t, "b", dy, dx] = send(t, slot_b(dy, dx), part, part, x_peer(dx))
        for dx in range(1, nx):
            part = region(t, owner(0, dx, core))
            flights[t, "t", 0, dx] = send(t, slot_twin(0, dx), part, part, twin)
        for dy in range(1, ny):
            part = region(t, owner(dy, 0, core))
            flights[t, "t", dy, 0] = send(t, slot_twin(dy, 0), part, part, twin)

    def wave_three(t):
        for dy in range(1, ny):
            for dx in range(1, nx):
                flights[t, "a", dy, dx].wait_recv()
                flights[t, "b", dy, dx].wait_recv()
                part = region(t, owner(dy, dx, core))
                flights[t, "t", dy, dx] = send(t, slot_twin(dy, dx), part, part, twin)

    def wave_end(t):
        for dy in range(ny):
            for dx in range(nx):
                flights[t, "t", dy, dx].wait_recv()

    def hop(row, s):
        return pltpu.make_async_remote_copy(
            src_ref=hidden.at[row, s - 1], dst_ref=hidden.at[row, s],
            send_sem=hop_send.at[row, s - 1], recv_sem=hop_recv.at[row, s - 1],
            device_id=(me, place + 1), device_id_type=mesh_type,
        )

    def hop_start(row, s):
        @pl.when((place >= s - 1) & (place < seq - 1))
        def _():
            hop(row, s).start()

    size = shards[0]
    mine = pl.ds(pl.multiple_of(me * size, size), size)
    reduce_own = reduce_ref[mine, :]
    up = up_ref[...]
    low_rank = lax.broadcasted_iota(jnp.int32, up.shape, 0) < 4
    for column, rank_up in ((0, jnp.where(low_rank, up, jnp.zeros_like(up))), (2, jnp.where(low_rank, jnp.zeros_like(up), up))):
        span = slice(column * width, (column + 1) * width)
        change = dot_nn(reduce_own, rank_up) * ADAPTER_SCALE
        w_held[mine, span] = (shard_ref[:, span].astype(F32) + change).astype(BF16)
    w_held[mine, width : 2 * width] = shard_ref[:, width : 2 * width]

    def first_norm(row):
        normed, _ = norm_parts(x_ref[row].astype(F32))
        hidden[row, 0] = (normed * gain_ref[...] + shift_ref[...]).astype(BF16)

    first_norm(0)
    heard = (nx - 1) + (ny - 1) + 1 + (place > 0).astype(jnp.int32) + (place < seq - 1).astype(jnp.int32)
    pl.semaphore_wait(barrier, heard)
    hop_start(0, 1)
    wave_one(0)
    own_copies = [
        pltpu.make_async_copy(sources[t], region(t, me), own_sems.at[t]) for t in range(1, 4)
    ]
    for copy in own_copies:
        copy.start()
    for row in range(1, rows):
        first_norm(row)
    for s in range(1, seq):
        @pl.when(place < s)
        def _():
            for row in range(rows):
                hidden[row, s] = jnp.zeros((tokens, width), BF16)

    low = head_lanes(tokens, BF16)
    lane = lax.broadcasted_iota(jnp.int32, (tokens, PAIR), 1)

    def row_hops(row):
        for s in range(1, seq):
            @pl.when(place >= s)
            def _():
                hop(row, s).wait_recv()

            if s < seq - 1:
                hop_start(row, s + 1)
            elif row < rows - 1:
                hop_start(row + 1, 1)

    def stores(row):
        slot = row % 2
        return [
            pltpu.make_async_copy(held.at[slot], out.at[row], store_sems.at[slot, i])
            for i, (held, out) in enumerate(
                ((q_held, q_out), (k_held, k_out), (v_held, v_out), (mix_held, mix_out))
            )
        ]

    def attend(row):
        slot = row % 2
        query = place * tokens + lax.broadcasted_iota(jnp.int32, (tokens, tokens), 0)
        start = start_ref[row]
        for s in range(seq):
            key = (place - s) * tokens + lax.broadcasted_iota(jnp.int32, (tokens, tokens), 1)
            allowed = key >= start
            if s == 0:
                allowed = allowed & (key <= query)
            span = slice(s * tokens, (s + 1) * tokens)
            mask_ref[:, span] = jnp.where(allowed, 0.0, MASKED)
            down = dot_nn(hidden[row, s], reduce_ref[...]) * ADAPTER_SCALE
            down_out[row, :, span] = down.T[:8].astype(BF16)

        @pl.loop(0, width // QUAD)
        def _(quad):
            def part(block):
                return pl.ds(pl.multiple_of(block * width + quad * QUAD, QUAD), QUAD)

            q = dot_nn(hidden[row, 0], w_held[:, part(0)]) + bias_q[:, part(0)]
            q_held[slot, :, part(0)] = (q.astype(BF16) * (HEAD**-0.5)).astype(BF16)
            for s in range(seq):
                span = slice(s * tokens, (s + 1) * tokens)
                k_held[slot, span, part(0)] = dot_nn(hidden[row, s], w_held[:, part(1)]).astype(BF16)
                v = dot_nn(hidden[row, s], w_held[:, part(2)]) + bias_v[:, part(0)]
                v_held[slot, span, part(0)] = v.astype(BF16)
            totals = jnp.zeros((tokens, PAIR), F32)
            for pair in range(QUAD // PAIR):
                span = pl.ds(pl.multiple_of(quad * QUAD, QUAD) + pair * PAIR, PAIR)
                q_pair = q_held[slot, :, span]
                mixed = []
                for half in range(2):
                    own = low if half == 0 else jnp.logical_not(low)
                    q_head = jnp.where(own, q_pair, jnp.zeros_like(q_pair))
                    score = dot_nt(q_head, k_held[slot, :, span]) + mask_ref[...]
                    highest = jnp.max(score, axis=-1, keepdims=True)
                    weight = jnp.exp(score - highest)
                    total = jnp.sum(weight, axis=-1, keepdims=True)
                    mixed.append(dot_nn(weight.astype(BF16), v_held[slot, :, span]) * (1.0 / total))
                    totals = jnp.where(lane == pair * 2 + half, highest + jnp.log(total), totals)
                mix_held[slot, :, span] = jnp.where(low, mixed[0], mixed[1]).astype(BF16)
            lse_out[row, quad] = totals.T[:8]

    hidden_copies = [pltpu.make_async_copy(hidden.at[row], hidden_out.at[row], own_sems.at[4 + row]) for row in range(rows)]
    w_copy = pltpu.make_async_copy(w_held, w_out, own_sems.at[0])
    for row in range(rows):
        if row == 0:
            wave_two(0)
            wave_one(1)
            wave_one(2)
        elif row == 1:
            wave_two(1)
            wave_two(2)
            wave_one(3)
        elif row == 2:
            wave_three(1)
            wave_three(2)
            wave_two(3)
        row_hops(row)
        if row == 0:
            wave_three(0)
            wave_end(0)
            w_copy.start()
        hidden_copies[row].start()
        if row >= 2:
            for copy in stores(row - 2):
                copy.wait()
        attend(row)
        for copy in stores(row):
            copy.start()
    done = min(rows, 3)
    if done < 2:
        wave_two(1)
        wave_two(2)
        wave_one(3)
    if done < 3:
        wave_three(1)
        wave_three(2)
        wave_two(3)
    wave_three(3)
    for t in range(1, 4):
        wave_end(t)
    for row in range(max(0, rows - 2), rows):
        for copy in stores(row):
            copy.wait()
    for copy in own_copies + hidden_copies + [w_copy]:
        copy.wait()
    for copy in pending:
        copy.wait_send()
    for row in range(rows):
        for s in range(1, seq):
            @pl.when((place >= s - 1) & (place < seq - 1))
            def _():
                hop(row, s).wait_send()


def feed_kernel(
    mix_ref, x_ref, gout_ref, wo_ref, out_bias, gain, shift, proj_bias, fc_ref, fc_bias, proj_ref,
    out_ref, gmid_ref, gmix_ref, middle_ref, hidden_ref, acc_ref, grad_ref,
):
    step = pl.program_id(0)

    @pl.when(step == 0)
    def _():
        middle = x_ref[...].astype(F32) + dot_nn(mix_ref[...], wo_ref[...]) + out_bias[...]
        middle_ref[...] = middle
        normed, _ = norm_parts(middle)
        hidden_ref[...] = (normed * gain[...] + shift[...]).astype(BF16)

    before = dot_nn(hidden_ref[...], fc_ref[...]) + fc_bias[...]
    square = before * before
    bend = jnp.tanh(GELU_A * before * (1.0 + GELU_B * square))
    half = 0.5 * (1.0 + bend)
    slope = half + 0.5 * before * (1.0 - bend * bend) * (GELU_A * (1.0 + 3.0 * GELU_B * square))
    act = (before * half).astype(BF16)
    g_before = (dot_nt(gout_ref[...], proj_ref[...]) * slope).astype(BF16)
    fed = dot_nn(act, proj_ref[...])
    back = dot_nt(g_before, fc_ref[...])

    @pl.when(step == 0)
    def _():
        acc_ref[...] = fed
        grad_ref[...] = back

    @pl.when(step > 0)
    def _():
        acc_ref[...] += fed
        grad_ref[...] += back

    @pl.when(step == pl.num_programs(0) - 1)
    def _():
        middle = middle_ref[...]
        out_ref[...] = (middle + acc_ref[...] + proj_bias[...]).astype(BF16)
        normed, inverse = norm_parts(middle)
        g_middle = gout_ref[...].astype(F32) + norm_backward(grad_ref[...], normed, inverse, gain[...])
        gmid_ref[...] = g_middle
        gmix_ref[...] = dot_nt(g_middle.astype(BF16), wo_ref[...]).astype(BF16)


def backward_kernel(chunks, place_ref, start_ref, *refs):
    hidden_ref, q_ref, k_ref, v_ref, mix_ref, g_ref, lse_ref, down_ref, up_ref, w_ref = refs[:10]
    grads = refs[10 : chunks + 10]
    reduce_out, up_out, mask_ref, dq_ref, dkv_ref, w_held, w_sem = refs[chunks + 10 :]
    hidden = [hidden_ref.at[s] for s in range(chunks)]
    tokens = hidden[0].shape[0]
    width = hidden[0].shape[1]
    quad = pl.program_id(0)

    @pl.when(quad == 0)
    def _():
        pltpu.make_async_copy(w_ref, w_held, w_sem).start()
        place = place_ref[0]
        query = place * tokens + lax.broadcasted_iota(jnp.int32, (tokens, tokens), 1)
        start = start_ref[...]
        for s in range(chunks):
            key = (place - s) * tokens + lax.broadcasted_iota(jnp.int32, (tokens, tokens), 0)
            allowed = key >= start
            if s == 0:
                allowed = allowed & (key <= query)
            mask_ref[s * tokens : (s + 1) * tokens, :] = jnp.where(allowed, 0.0, MASKED)

    low = head_lanes(tokens, BF16)
    for pair in range(QUAD // PAIR):
        span = slice(pair * PAIR, (pair + 1) * PAIR)
        q_pair = q_ref[:, span]
        g_pair = g_ref[:, span]
        product = (g_pair.astype(F32) * mix_ref[:, span].astype(F32)).T
        heads = []
        for half in range(2):
            own = low if half == 0 else jnp.logical_not(low)
            inner = jnp.sum(product[half * HEAD : (half + 1) * HEAD], axis=0, keepdims=True)
            row = pair * 2 + half
            heads.append(
                (
                    jnp.where(own, q_pair, jnp.zeros_like(q_pair)),
                    jnp.where(own, g_pair, jnp.zeros_like(g_pair)),
                    inner,
                    lse_ref[0, row : row + 1, :],
                )
            )
        dq_parts = [jnp.zeros((HEAD, tokens), F32)] * 2
        for s in range(chunks):
            rows = slice(s * tokens, (s + 1) * tokens)
            k_pair = k_ref[rows, span]
            v_pair = v_ref[rows, span]
            k_turned = k_pair.astype(F32).T.astype(BF16)
            dk = None
            for half, (q_head, g_head, inner, lse) in enumerate(heads):
                score = dot_nt(k_pair, q_head) + mask_ref[rows, :]
                prob = jnp.exp(score - lse)
                g_score = (prob * (dot_nt(v_pair, g_head) - inner)).astype(BF16)
                part_v = dot_nn(prob.astype(BF16), g_head)
                part_k = dot_nn(g_score, q_head)
                dk = part_k if dk is None else dk + part_k
                dv = part_v if half == 0 else dv + part_v
                dq_parts[half] = dq_parts[half] + dot_nn(k_turned[half * HEAD : (half + 1) * HEAD], g_score)
            columns = pl.ds(pl.multiple_of(quad * QUAD, QUAD) + pair * PAIR, PAIR)
            dkv_ref[rows, columns] = dk.astype(BF16)
            columns = pl.ds(pl.multiple_of(quad * QUAD, QUAD) + (width + pair * PAIR), PAIR)
            dkv_ref[rows, columns] = dv.astype(BF16)
        dq = jnp.concatenate(dq_parts, axis=0).T * (HEAD**-0.5)
        dq_ref[:, pl.ds(pl.multiple_of(quad * QUAD, QUAD) + pair * PAIR, PAIR)] = dq.astype(BF16)

    @pl.when(quad == pl.num_programs(0) - 1)
    def _():
        pltpu.make_async_copy(w_ref, w_held, w_sem).wait()
        rank_row = lax.broadcasted_iota(jnp.int32, (8, width), 0) < 4
        up_grad = jnp.zeros((8, width), F32)
        reduce_grad = jnp.zeros((8, width), F32)
        for s in range(chunks - 1, -1, -1):
            rows = slice(s * tokens, (s + 1) * tokens)
            dkv = dkv_ref[rows, :]
            grad = dot_nt(dkv, w_held[:, width:])
            if s == 0:
                grad = grad + dot_nt(dq_ref[...], w_held[:, :width])
            grads[s][...] = grad.astype(grads[s].dtype)
            dv = dkv_ref[rows, width:]
            down = down_ref[:, rows]
            up_grad = up_grad + dot_nn(down, dv)
            g_down = dot_nt(dv, up_ref[...]).T[:8].astype(BF16)
            reduce_grad = reduce_grad + dot_nn(g_down, hidden[s][...])
        dq = dq_ref[...]
        g_down = dot_nt(dq, up_ref[...]).T[:8].astype(BF16)
        up_out[...] = jnp.where(rank_row, dot_nn(down_ref[:, :tokens], dq), up_grad)
        reduce_out[...] = jnp.where(rank_row, dot_nn(g_down, hidden[0][...]), reduce_grad)


def whole(shape):
    return pl.BlockSpec(shape, lambda i: (0,) * len(shape))


def run_start(plane, seq, x, starts, gain, shift, shard, reduce_wide, up_wide, bias_q, bias_v, wo, fc, proj):
    rows, tokens, width = x.shape
    length = seq * tokens
    quads = width // QUAD
    dp = plane[0] * plane[1] * 2
    anywhere = pl.BlockSpec(memory_space=pl.ANY)
    vmem = pl.BlockSpec(memory_space=pltpu.VMEM)
    nx, ny = plane
    slots = nx - 1 + ny - 1 + 2 * (nx - 1) * (ny - 1) + nx * ny

    def shape(*dims, dtype=BF16):
        return jax.ShapeDtypeStruct(dims, dtype)

    def whole_of(part):
        return shape(part.shape[0] * dp, part.shape[1])

    return pl.pallas_call(
        partial(start_kernel, plane, seq, rows),
        in_specs=[vmem] * 9 + [anywhere] * 3,
        out_specs=[anywhere] * 9 + [vmem] * 2,
        out_shape=[
            whole_of(shard), whole_of(wo), whole_of(fc), whole_of(proj),
            shape(rows, seq, tokens, width),
            shape(rows, tokens, width), shape(rows, length, width), shape(rows, length, width),
            shape(rows, tokens, width),
            shape(rows, quads, 8, tokens, dtype=F32),
            shape(rows, 8, length),
        ],
        scratch_shapes=[
            pltpu.VMEM((width, 3 * width), BF16),
            pltpu.VMEM((rows, seq, tokens, width), BF16),
            pltpu.VMEM((2, tokens, width), BF16),
            pltpu.VMEM((2, length, width), BF16),
            pltpu.VMEM((2, length, width), BF16),
            pltpu.VMEM((2, tokens, width), BF16),
            pltpu.VMEM((tokens, length), F32),
            pltpu.SemaphoreType.DMA((4, slots)),
            pltpu.SemaphoreType.DMA((4, slots)),
            pltpu.SemaphoreType.DMA((rows, seq - 1)),
            pltpu.SemaphoreType.DMA((rows, seq - 1)),
            pltpu.SemaphoreType.DMA((4 + rows,)),
            pltpu.SemaphoreType.DMA((2, 4)),
        ],
        compiler_params=pltpu.CompilerParams(
            vmem_limit_bytes=VMEM_BYTES, collective_id=0, has_side_effects=True
        ),
        name="start",
    )(x, starts, gain, shift, shard, reduce_wide, up_wide, bias_q, bias_v, wo, fc, proj)


def run_feed(row, mixed, x, grad_out, out_weight, vectors, fc_weight, fc_bias, proj_weight):
    _, tokens, width = x.shape
    hidden_units = fc_weight.shape[1]
    block = 1024
    out_bias, gain, shift, proj_bias = vectors
    return pl.pallas_call(
        feed_kernel,
        grid=(hidden_units // block,),
        in_specs=[pl.BlockSpec((None, tokens, width), lambda i: (row, 0, 0))] * 3
        + [whole((width, width))]
        + [whole((1, width))] * 4
        + [
            pl.BlockSpec((width, block), lambda i: (0, i)),
            pl.BlockSpec((1, block), lambda i: (0, i)),
            pl.BlockSpec((block, width), lambda i: (i, 0)),
        ],
        out_specs=[whole((tokens, width))] * 3,
        out_shape=[
            jax.ShapeDtypeStruct((tokens, width), BF16),
            jax.ShapeDtypeStruct((tokens, width), F32),
            jax.ShapeDtypeStruct((tokens, width), BF16),
        ],
        scratch_shapes=[
            pltpu.VMEM((tokens, width), F32),
            pltpu.VMEM((tokens, width), BF16),
            pltpu.VMEM((tokens, width), F32),
            pltpu.VMEM((tokens, width), F32),
        ],
        compiler_params=pltpu.CompilerParams(vmem_limit_bytes=VMEM_BYTES),
        cost_estimate=pl.CostEstimate(
            flops=2 * tokens * width * (4 * hidden_units + 2 * width),
            bytes_accessed=2 * width * (2 * hidden_units + width) + 16 * tokens * width,
            transcendentals=tokens * hidden_units,
        ),
        name="feed",
    )(mixed, x, grad_out, out_weight, out_bias, gain, shift, proj_bias, fc_weight, fc_bias, proj_weight)


def run_backward(row, place, start, hidden, q, k, v, mixed, g_mixed, lse, down, up_wide, weight):
    _, chunks, tokens, width = hidden.shape
    length = chunks * tokens
    quads = width // QUAD
    flops = 2 * width * width * (tokens + 2 * length) + 10 * tokens * length * width
    own = pl.BlockSpec((None, tokens, QUAD), lambda i: (row, 0, i))
    every = pl.BlockSpec((None, length, QUAD), lambda i: (row, 0, i))
    return pl.pallas_call(
        partial(backward_kernel, chunks),
        grid=(quads,),
        in_specs=[pl.BlockSpec(memory_space=pltpu.SMEM), whole((1, tokens))]
        + [
            pl.BlockSpec((None, chunks, tokens, width), lambda i: (row, 0, 0, 0)),
            own, every, every, own, pl.BlockSpec((tokens, QUAD), lambda i: (0, i)),
            pl.BlockSpec((None, 1, 8, tokens), lambda i: (row, i, 0, 0)),
            pl.BlockSpec((None, 8, length), lambda i: (row, 0, 0)),
            whole((PAIR, width)),
            pl.BlockSpec(memory_space=pl.ANY),
        ],
        out_specs=[whole((tokens, width))] * chunks + [whole((8, width))] * 2,
        out_shape=[jax.ShapeDtypeStruct((tokens, width), F32 if s == 0 else BF16) for s in range(chunks)]
        + [jax.ShapeDtypeStruct((8, width), F32)] * 2,
        scratch_shapes=[
            pltpu.VMEM((length, tokens), F32),
            pltpu.VMEM((tokens, width), BF16),
            pltpu.VMEM((length, 2 * width), BF16),
            pltpu.VMEM((width, 3 * width), BF16),
            pltpu.SemaphoreType.DMA,
        ],
        compiler_params=pltpu.CompilerParams(vmem_limit_bytes=VMEM_BYTES),
        cost_estimate=pl.CostEstimate(
            flops=flops, bytes_accessed=6 * width * width + 14 * length * width,
            transcendentals=tokens * length * width // HEAD,
        ),
        name="attend_backward",
    )(place, start, hidden, q, k, v, mixed, g_mixed, lse, down, up_wide, weight)


def sum_kernel(dp, seq, part_ref, out_ref, plane_ref, line_ref, send_sems, recv_sems):
    me, place = lax.axis_index("dp"), lax.axis_index("seq")
    barrier = pltpu.get_barrier_semaphore()
    mesh_type = pl.DeviceIdType.MESH

    def peer(delta):
        return lax.rem(me + delta, dp), place

    def line_peer(delta):
        return me, lax.rem(place + delta, seq)

    for delta in range(1, dp):
        pl.semaphore_signal(barrier, inc=1, device_id=peer(delta), device_id_type=mesh_type)
    for delta in range(1, seq):
        pl.semaphore_signal(barrier, inc=1, device_id=line_peer(delta), device_id_type=mesh_type)
    pl.semaphore_wait(barrier, dp + seq - 2)

    def send(source, target, slot, device):
        copy = pltpu.make_async_remote_copy(
            src_ref=source, dst_ref=target, send_sem=send_sems.at[slot], recv_sem=recv_sems.at[slot],
            device_id=device, device_id_type=mesh_type,
        )
        copy.start()
        return copy

    copies = [
        send(part_ref.at[lax.rem(me + delta, dp)], plane_ref.at[delta], delta, peer(delta))
        for delta in range(1, dp)
    ]
    total = part_ref[me]
    for delta in range(1, dp):
        copies[delta - 1].wait()
        total = total + plane_ref[delta]
    line_ref[place] = total
    copies = [
        send(line_ref.at[place], line_ref.at[place], dp + delta, line_peer(delta)) for delta in range(1, seq)
    ]
    for copy in copies:
        copy.wait()
    total = line_ref[0]
    for index in range(1, seq):
        total = total + line_ref[index]
    out_ref[me] = total
    copies = [
        send(out_ref.at[me], out_ref.at[me], dp + seq + delta, peer(delta)) for delta in range(1, dp)
    ]
    for copy in copies:
        copy.wait()


def run_sum(dp, seq, part):
    rows, width = part.shape
    piece = max(8, rows * width // (PAIR * dp))
    flat = part.reshape(-1, PAIR)
    used = flat.shape[0]
    flat = jnp.pad(flat, ((0, dp * piece - used), (0, 0)))
    slots = 2 * dp + seq
    total = pl.pallas_call(
        partial(sum_kernel, dp, seq),
        in_specs=[pl.BlockSpec(memory_space=pltpu.VMEM)],
        out_specs=pl.BlockSpec(memory_space=pltpu.VMEM),
        out_shape=jax.ShapeDtypeStruct((dp, piece, PAIR), F32),
        scratch_shapes=[
            pltpu.VMEM((dp, piece, PAIR), F32),
            pltpu.VMEM((seq, piece, PAIR), F32),
            pltpu.SemaphoreType.DMA((slots,)),
            pltpu.SemaphoreType.DMA((slots,)),
        ],
        compiler_params=pltpu.CompilerParams(collective_id=1, has_side_effects=True),
        name="sum_all",
    )(flat.reshape(dp, piece, PAIR))
    return total.reshape(-1, PAIR)[:used].reshape(rows, width)


def on_device(
    dp,
    seq,
    block_input,
    seg_start,
    ln1_gain,
    ln1_bias,
    qkv_weight,
    query_bias,
    value_bias,
    query_adapter_reduce,
    query_up,
    value_adapter_reduce,
    value_up,
    out_weight,
    out_bias,
    ln2_gain,
    ln2_bias,
    fc_weight,
    fc_bias,
    proj_weight,
    proj_bias,
    grad_out,
):
    rows, tokens, width = block_input.shape
    rank = query_up.shape[0]
    place = lax.axis_index("seq")
    downward = [(i + 1, i) for i in range(seq - 1)]
    side = math.isqrt(dp // 2)

    pad = jnp.zeros((width, PAIR - 2 * rank), BF16)
    reduce_wide = jnp.concatenate([query_adapter_reduce, value_adapter_reduce, pad], axis=1)
    up_wide = jnp.concatenate([query_up, value_up, pad.T], axis=0)
    starts = lax.dynamic_slice(seg_start, (0, place * tokens), (rows, tokens))
    place_ref = place.astype(jnp.int32).reshape(1)

    def as_row(vector):
        return vector.reshape(1, -1)

    vectors = tuple(as_row(a) for a in (out_bias, ln2_gain, ln2_bias, proj_bias))
    weight, whole_out, whole_fc, whole_proj, hidden, q, k, v, mixed, lse, down = run_start(
        (side, dp // (2 * side)), seq, block_input, starts[:, :, None], as_row(ln1_gain), as_row(ln1_bias), qkv_weight,
        reduce_wide, up_wide, as_row(query_bias), as_row(value_bias), out_weight, fc_weight, proj_weight,
    )

    outs, grads, reduce_sum, up_sum = [], [], 0.0, 0.0
    for r in range(rows):
        out, g_middle, g_mixed = run_feed(
            r, mixed, block_input, grad_out, whole_out, vectors, whole_fc, as_row(fc_bias), whole_proj
        )
        outs.append(out)
        result = run_backward(
            r, place_ref, starts[r].reshape(1, tokens), hidden, q, k, v, mixed, g_mixed, lse, down, up_wide, weight
        )
        reduce_sum = reduce_sum + result[seq]
        up_sum = up_sum + result[seq + 1]
        moving = result[seq - 1]
        for s in range(seq - 2, -1, -1):
            arrived = lax.ppermute(moving, "seq", downward)
            total = result[s].astype(F32) + arrived.astype(F32)
            moving = total.astype(BF16)
        normed, inverse = norm_parts(block_input[r].astype(F32))
        grads.append(g_middle + norm_backward(total, normed, inverse, ln1_gain))

    summed = run_sum(dp, seq, jnp.concatenate([reduce_sum * ADAPTER_SCALE, up_sum], axis=0))
    return (
        jnp.stack(outs),
        jnp.stack(grads),
        summed[:rank].T,
        summed[8 : 8 + rank],
        summed[rank : 2 * rank].T,
        summed[8 + rank : 8 + 2 * rank],
    )


def solution(mesh):
    return jax.shard_map(
        partial(on_device, mesh.shape["dp"], mesh.shape["seq"]),
        mesh=mesh,
        in_specs=(
            P("dp", "seq", None),
            P("dp", None),
            P(),
            P(),
            P("dp", None),
            P(),
            P(),
            P(),
            P(),
            P(),
            P(),
            P("dp", None),
            P(),
            P(),
            P(),
            P("dp", None),
            P(),
            P("dp", None),
            P(),
            P("dp", "seq", None),
        ),
        out_specs=(P("dp", "seq", None), P("dp", "seq", None), P(), P(), P(), P()),
        check_vma=False,
    )
```

```python
import math
from functools import partial

import jax
import jax.numpy as jnp
from jax import lax
from jax.experimental import pallas as pl
from jax.experimental.pallas import tpu as pltpu
from jax.sharding import PartitionSpec as P

HEAD = 64
QUAD = 256
PAIR = 128
NORM_EPSILON = 1e-05
ADAPTER_SCALE = 8.0
MASKED = -1e30
GELU_A = 0.7978845608028654
GELU_B = 0.044715

F32 = jnp.float32
BF16 = jnp.bfloat16
VMEM_BYTES = 56 * 1024 * 1024
FINISH_BYTES = 63 * 1024 * 1024


def dot_nn(left, right):
    return lax.dot_general(left, right, (((1,), (0,)), ((), ())), preferred_element_type=F32)


def dot_nt(left, right):
    return lax.dot_general(left, right, (((1,), (1,)), ((), ())), preferred_element_type=F32)


def norm_parts(values):
    average = jnp.mean(values, axis=-1, keepdims=True)
    centered = values - average
    inverse = lax.rsqrt(jnp.mean(centered * centered, axis=-1, keepdims=True) + NORM_EPSILON)
    return centered * inverse, inverse


def norm_backward(gradient, normed, inverse, gain):
    scaled = gradient * gain
    return inverse * (
        scaled
        - jnp.mean(scaled, axis=-1, keepdims=True)
        - normed * jnp.mean(scaled * normed, axis=-1, keepdims=True)
    )


def head_lanes(rows, dtype):
    lane = lax.broadcasted_iota(jnp.int32, (rows, PAIR), 1)
    return lane < HEAD


def start_kernel(
    plane, seq, rows,
    x_ref, start_ref, gain_ref, shift_ref, shard_ref, reduce_ref, up_ref, bias_q, bias_v, wo_in, fc_in, proj_in,
    w_out, wo_out, fc_out, proj_out, hidden_out, q_out, k_out, v_out, mix_out, lse_out, down_out,
    w_held, hidden, q_held, k_held, v_held, mix_held, mask_ref,
    send_sems, recv_sems, hop_send, hop_recv, own_sems, store_sems,
):
    nx, ny = plane
    tokens, width = x_ref.shape[1], x_ref.shape[2]
    length = seq * tokens
    mesh_type = pl.DeviceIdType.MESH
    me, place = lax.axis_index("dp"), lax.axis_index("seq")
    core = lax.rem(me, 2)
    my_x = lax.rem(me // 2, nx)
    my_y = me // (2 * nx)

    def index(y, x, c):
        return (y * nx + x) * 2 + c

    def x_peer(delta):
        return index(my_y, lax.rem(my_x + delta, nx), core), place

    def y_peer(delta):
        return index(lax.rem(my_y + delta, ny), my_x, core), place

    twin = (index(my_y, my_x, 1 - core), place)

    def owner(dy, dx, c):
        return index(lax.rem(my_y + ny - dy, ny), lax.rem(my_x + nx - dx, nx), c)

    barrier = pltpu.get_barrier_semaphore()
    for delta in range(1, nx):
        pl.semaphore_signal(barrier, inc=1, device_id=x_peer(delta), device_id_type=mesh_type)
    for delta in range(1, ny):
        pl.semaphore_signal(barrier, inc=1, device_id=y_peer(delta), device_id_type=mesh_type)
    pl.semaphore_signal(barrier, inc=1, device_id=twin, device_id_type=mesh_type)

    @pl.when(place > 0)
    def _():
        pl.semaphore_signal(barrier, inc=1, device_id=(me, place - 1), device_id_type=mesh_type)

    @pl.when(place < seq - 1)
    def _():
        pl.semaphore_signal(barrier, inc=1, device_id=(me, place + 1), device_id_type=mesh_type)

    shards = [shard_ref.shape[0], wo_in.shape[0], fc_in.shape[0], proj_in.shape[0]]
    sources = [None, wo_in, fc_in, proj_in]
    targets = [w_held, wo_out, fc_out, proj_out]

    def region(t, device, half=None):
        size = shards[t]
        if half is None:
            return targets[t].at[pl.ds(pl.multiple_of(device * size, size), size), :]
        part = size // 2
        return targets[t].at[pl.ds(pl.multiple_of(device * size + half * part, part), part), :]

    pending = []

    def send(t, slot, source, target, device):
        copy = pltpu.make_async_remote_copy(
            src_ref=source, dst_ref=target, send_sem=send_sems.at[t, slot], recv_sem=recv_sems.at[t, slot],
            device_id=device, device_id_type=mesh_type,
        )
        copy.start()
        pending.append(copy)
        return copy

    first_x, first_y = nx - 1, nx - 1 + ny - 1
    cross = (nx - 1) * (ny - 1)

    def slot_a(dy, dx):
        return first_y + (dy - 1) * (nx - 1) + dx - 1

    def slot_b(dy, dx):
        return first_y + cross + (dy - 1) * (nx - 1) + dx - 1

    def slot_twin(dy, dx):
        return first_y + 2 * cross + dy * nx + dx

    flights = {}

    def wave_one(t):
        mine = region(t, me) if sources[t] is None else sources[t]
        for delta in range(1, nx):
            flights[t, "x", delta] = send(t, delta - 1, mine, region(t, me), x_peer(delta))
        for delta in range(1, ny):
            flights[t, "y", delta] = send(t, first_x + delta - 1, mine, region(t, me), y_peer(delta))
        flights[t, "t", 0, 0] = send(t, slot_twin(0, 0), mine, region(t, me), twin)

    def wave_two(t):
        for dx in range(1, nx):
            flights[t, "x", dx].wait_recv()
            device = owner(0, dx, core)
            for dy in range(1, ny):
                part = region(t, device, 0)
                flights[t, "a", dy, dx] = send(t, slot_a(dy, dx), part, part, y_peer(dy))
        for dy in range(1, ny):
            flights[t, "y", dy].wait_recv()
            device = owner(dy, 0, core)
            for dx in range(1, nx):
                part = region(t, device, 1)
                flights[t, "b", dy, dx] = send(t, slot_b(dy, dx), part, part, x_peer(dx))
        for dx in range(1, nx):
            part = region(t, owner(0, dx, core))
            flights[t, "t", 0, dx] = send(t, slot_twin(0, dx), part, part, twin)
        for dy in range(1, ny):
            part = region(t, owner(dy, 0, core))
            flights[t, "t", dy, 0] = send(t, slot_twin(dy, 0), part, part, twin)

    def wave_three(t):
        for dy in range(1, ny):
            for dx in range(1, nx):
                flights[t, "a", dy, dx].wait_recv()
                flights[t, "b", dy, dx].wait_recv()
                part = region(t, owner(dy, dx, core))
                flights[t, "t", dy, dx] = send(t, slot_twin(dy, dx), part, part, twin)

    def wave_end(t):
        for dy in range(ny):
            for dx in range(nx):
                flights[t, "t", dy, dx].wait_recv()

    def hop(row, s):
        return pltpu.make_async_remote_copy(
            src_ref=hidden.at[row, s - 1], dst_ref=hidden.at[row, s],
            send_sem=hop_send.at[row, s - 1], recv_sem=hop_recv.at[row, s - 1],
            device_id=(me, place + 1), device_id_type=mesh_type,
        )

    def hop_start(row, s):
        @pl.when((place >= s - 1) & (place < seq - 1))
        def _():
            hop(row, s).start()

    size = shards[0]
    mine = pl.ds(pl.multiple_of(me * size, size), size)
    reduce_own = reduce_ref[mine, :]
    up = up_ref[...]
    low_rank = lax.broadcasted_iota(jnp.int32, up.shape, 0) < 4
    for column, rank_up in ((0, jnp.where(low_rank, up, jnp.zeros_like(up))), (2, jnp.where(low_rank, jnp.zeros_like(up), up))):
        span = slice(column * width, (column + 1) * width)
        change = dot_nn(reduce_own, rank_up) * ADAPTER_SCALE
        w_held[mine, span] = (shard_ref[:, span].astype(F32) + change).astype(BF16)
    w_held[mine, width : 2 * width] = shard_ref[:, width : 2 * width]

    def first_norm(row):
        normed, _ = norm_parts(x_ref[row].astype(F32))
        hidden[row, 0] = (normed * gain_ref[...] + shift_ref[...]).astype(BF16)

    first_norm(0)
    heard = (nx - 1) + (ny - 1) + 1 + (place > 0).astype(jnp.int32) + (place < seq - 1).astype(jnp.int32)
    pl.semaphore_wait(barrier, heard)
    hop_start(0, 1)
    wave_one(0)
    own_copies = [
        pltpu.make_async_copy(sources[t], region(t, me), own_sems.at[t]) for t in range(1, 4)
    ]
    for copy in own_copies:
        copy.start()
    for row in range(1, rows):
        first_norm(row)
    for s in range(1, seq):
        @pl.when(place < s)
        def _():
            for row in range(rows):
                hidden[row, s] = jnp.zeros((tokens, width), BF16)

    low = head_lanes(tokens, BF16)
    lane = lax.broadcasted_iota(jnp.int32, (tokens, PAIR), 1)

    def row_hops(row):
        for s in range(1, seq):
            @pl.when(place >= s)
            def _():
                hop(row, s).wait_recv()

            if s < seq - 1:
                hop_start(row, s + 1)
            elif row < rows - 1:
                hop_start(row + 1, 1)

    def stores(row):
        slot = row % 2
        return [
            pltpu.make_async_copy(held.at[slot], out.at[row], store_sems.at[slot, i])
            for i, (held, out) in enumerate(
                ((q_held, q_out), (k_held, k_out), (v_held, v_out), (mix_held, mix_out))
            )
        ]

    def attend(row):
        slot = row % 2
        query = place * tokens + lax.broadcasted_iota(jnp.int32, (tokens, tokens), 0)
        start = start_ref[row]
        for s in range(seq):
            key = (place - s) * tokens + lax.broadcasted_iota(jnp.int32, (tokens, tokens), 1)
            allowed = key >= start
            if s == 0:
                allowed = allowed & (key <= query)
            span = slice(s * tokens, (s + 1) * tokens)
            mask_ref[:, span] = jnp.where(allowed, 0.0, MASKED)
            down = dot_nn(hidden[row, s], reduce_ref[...]) * ADAPTER_SCALE
            down_out[row, :, span] = down.T[:8].astype(BF16)

        @pl.loop(0, width // QUAD)
        def _(quad):
            def part(block):
                return pl.ds(pl.multiple_of(block * width + quad * QUAD, QUAD), QUAD)

            q = dot_nn(hidden[row, 0], w_held[:, part(0)]) + bias_q[:, part(0)]
            q_held[slot, :, part(0)] = (q.astype(BF16) * (HEAD**-0.5)).astype(BF16)
            for s in range(seq):
                span = slice(s * tokens, (s + 1) * tokens)
                k_held[slot, span, part(0)] = dot_nn(hidden[row, s], w_held[:, part(1)]).astype(BF16)
                v = dot_nn(hidden[row, s], w_held[:, part(2)]) + bias_v[:, part(0)]
                v_held[slot, span, part(0)] = v.astype(BF16)
            totals = jnp.zeros((tokens, PAIR), F32)
            for pair in range(QUAD // PAIR):
                span = pl.ds(pl.multiple_of(quad * QUAD, QUAD) + pair * PAIR, PAIR)
                q_pair = q_held[slot, :, span]
                mixed = []
                for half in range(2):
                    own = low if half == 0 else jnp.logical_not(low)
                    q_head = jnp.where(own, q_pair, jnp.zeros_like(q_pair))
                    score = dot_nt(q_head, k_held[slot, :, span]) + mask_ref[...]
                    highest = jnp.max(score, axis=-1, keepdims=True)
                    weight = jnp.exp(score - highest)
                    total = jnp.sum(weight, axis=-1, keepdims=True)
                    mixed.append(dot_nn(weight.astype(BF16), v_held[slot, :, span]) * (1.0 / total))
                    totals = jnp.where(lane == pair * 2 + half, highest + jnp.log(total), totals)
                mix_held[slot, :, span] = jnp.where(low, mixed[0], mixed[1]).astype(BF16)
            lse_out[row, quad] = totals.T[:8]

    hidden_copies = [pltpu.make_async_copy(hidden.at[row], hidden_out.at[row], own_sems.at[4 + row]) for row in range(rows)]
    w_copy = pltpu.make_async_copy(w_held, w_out, own_sems.at[0])
    for row in range(rows):
        if row == 0:
            wave_two(0)
            wave_one(1)
            wave_one(2)
        elif row == 1:
            wave_two(1)
            wave_two(2)
            wave_one(3)
        elif row == 2:
            wave_three(1)
            wave_three(2)
            wave_two(3)
        row_hops(row)
        if row == 0:
            wave_three(0)
            wave_end(0)
            w_copy.start()
        hidden_copies[row].start()
        if row >= 2:
            for copy in stores(row - 2):
                copy.wait()
        attend(row)
        for copy in stores(row):
            copy.start()
    done = min(rows, 3)
    if done < 2:
        wave_two(1)
        wave_two(2)
        wave_one(3)
    if done < 3:
        wave_three(1)
        wave_three(2)
        wave_two(3)
    wave_three(3)
    for t in range(1, 4):
        wave_end(t)
    for row in range(max(0, rows - 2), rows):
        for copy in stores(row):
            copy.wait()
    for copy in own_copies + hidden_copies + [w_copy]:
        copy.wait()
    for copy in pending:
        copy.wait_send()
    for row in range(rows):
        for s in range(1, seq):
            @pl.when((place >= s - 1) & (place < seq - 1))
            def _():
                hop(row, s).wait_send()


def finish_kernel(
    dp, seq, rows, block,
    x_ref, start_ref, lse_ref, down_ref, up_ref, gain1, out_bias, gain2, shift2, proj_bias, fc_bias,
    gout_in, w_in, wo_in, fc_in, proj_in, hidden_in, q_in, k_in, v_in, mix_in,
    out_out, grad_out, sum_out,
    w_held, wo_held, fc_held, proj_held, hidden, q_held, k_held, v_held, mix_held, gout_held,
    gmix_ref, middle_ref, h2_ref, acc_ref, back_ref, gmid_ref, own_ref, mask_ref, delta_ref, dq_ref, dkv_ref,
    leaving, arriving, stage_ref, up_sum, reduce_sum, part_ref, plane_ref, line_ref,
    weight_sems, row_sems, store_sems, leave_sems, arrive_sems, sum_send, sum_recv,
):
    tokens, width = x_ref.shape[1], x_ref.shape[2]
    quads = width // QUAD
    steps = fc_held.shape[1] // block
    mesh_type = pl.DeviceIdType.MESH
    me, place = lax.axis_index("dp"), lax.axis_index("seq")
    top = seq - 1

    def peer(delta):
        return lax.rem(me + delta, dp), place

    def line_peer(delta):
        return me, lax.rem(place + delta, seq)

    barrier = pltpu.get_barrier_semaphore()
    for delta in range(1, dp):
        pl.semaphore_signal(barrier, inc=1, device_id=peer(delta), device_id_type=mesh_type)
    for delta in range(1, seq):
        pl.semaphore_signal(barrier, inc=1, device_id=line_peer(delta), device_id_type=mesh_type)

    def feed_loads(row):
        return [
            pltpu.make_async_copy(mix_in.at[row], mix_held, row_sems.at[0]),
            pltpu.make_async_copy(gout_in.at[row], gout_held, row_sems.at[1]),
        ]

    def attend_loads(row):
        return [
            pltpu.make_async_copy(q_in.at[row], q_held, row_sems.at[2]),
            pltpu.make_async_copy(k_in.at[row], k_held, row_sems.at[3]),
            pltpu.make_async_copy(v_in.at[row], v_held, row_sems.at[4]),
            pltpu.make_async_copy(hidden_in.at[row], hidden, row_sems.at[5]),
        ]

    def chunk_loads(step):
        part = pl.ds(pl.multiple_of(step * block, block), block)
        return [
            pltpu.make_async_copy(fc_in.at[:, part], fc_held.at[:, part], weight_sems.at[0, step]),
            pltpu.make_async_copy(proj_in.at[part, :], proj_held.at[part, :], weight_sems.at[1, step]),
        ]

    wo_load = pltpu.make_async_copy(wo_in, wo_held, weight_sems.at[2, 0])
    w_load = pltpu.make_async_copy(w_in, w_held, weight_sems.at[2, 1])
    for copy in feed_loads(0):
        copy.start()
    wo_load.start()
    for step in range(steps):
        for copy in chunk_loads(step):
            copy.start()
    for copy in attend_loads(0):
        copy.start()
    w_load.start()
    up_sum[...] = jnp.zeros_like(up_sum)
    reduce_sum[...] = jnp.zeros_like(reduce_sum)
    pl.semaphore_wait(barrier, dp + seq - 2)
    wo_load.wait()

    def out_store(row):
        return pltpu.make_async_copy(stage_ref, out_out.at[row], store_sems.at[0])

    def grad_store(row):
        slot = lax.rem(row, 2)
        return pltpu.make_async_copy(gmid_ref.at[slot], grad_out.at[row], store_sems.at[1 + slot])

    def leave(row, s):
        return pltpu.make_async_remote_copy(
            src_ref=leaving.at[s - 1], dst_ref=arriving.at[row, s - 1],
            send_sem=leave_sems.at[s - 1], recv_sem=arrive_sems.at[row, s - 1],
            device_id=(me, place - 1), device_id_type=mesh_type,
        )

    def chain(row, k):
        s = seq - 1 - k

        @pl.when((place < top) & (place >= s))
        def _():
            leave(row, s + 1).wait_recv()
            arrived = arriving[row, s].astype(F32)
            if s > 0:
                leaving[s - 1] = (leaving[s - 1].astype(F32) + arrived).astype(BF16)
                leave(row, s).start()
            else:
                own_ref[...] = own_ref[...] + arrived

        if s == 0:
            slot = lax.rem(row, 2)
            normed, inverse = norm_parts(x_ref[row].astype(F32))
            gmid_ref[slot] = gmid_ref[slot] + norm_backward(own_ref[...], normed, inverse, gain1[...])
            grad_store(row).start()

    def feed(row):
        for copy in feed_loads(row):
            copy.wait()
        middle = x_ref[row].astype(F32) + dot_nn(mix_held[...], wo_held[...]) + out_bias[...]
        middle_ref[...] = middle
        normed, _ = norm_parts(middle)
        h2_ref[...] = (normed * gain2[...] + shift2[...]).astype(BF16)
        acc_ref[...] = jnp.zeros_like(acc_ref)
        back_ref[...] = jnp.zeros_like(back_ref)

        @pl.loop(0, steps)
        def _(step):
            @pl.when(row == 0)
            def _():
                for copy in chunk_loads(step):
                    copy.wait()

            part = pl.ds(pl.multiple_of(step * block, block), block)
            before = dot_nn(h2_ref[...], fc_held[:, part]) + fc_bias[:, part]
            square = before * before
            bend = jnp.tanh(GELU_A * before * (1.0 + GELU_B * square))
            half = 0.5 * (1.0 + bend)
            slope = half + 0.5 * before * (1.0 - bend * bend) * (GELU_A * (1.0 + 3.0 * GELU_B * square))
            act = (before * half).astype(BF16)
            g_before = (dot_nt(gout_held[...], proj_held[part, :]) * slope).astype(BF16)
            acc_ref[...] += dot_nn(act, proj_held[part, :])
            back_ref[...] += dot_nt(g_before, fc_held[:, part])

        slot = lax.rem(row, 2)

        @pl.when(row >= 1)
        def _():
            out_store(row - 1).wait()

        @pl.when(row >= 2)
        def _():
            grad_store(row - 2).wait()

        middle = middle_ref[...]
        stage_ref[...] = (middle + acc_ref[...] + proj_bias[...]).astype(BF16)
        out_store(row).start()
        normed, inverse = norm_parts(middle)
        g_middle = gout_held[...].astype(F32) + norm_backward(back_ref[...], normed, inverse, gain2[...])
        gmid_ref[slot] = g_middle
        gmix_ref[...] = dot_nt(g_middle.astype(BF16), wo_held[...]).astype(BF16)
        for pair in range(width // PAIR):
            span = slice(pair * PAIR, (pair + 1) * PAIR)
            product = (gmix_ref[:, span].astype(F32) * mix_held[:, span].astype(F32)).T
            for half in range(2):
                head = pair * 2 + half
                delta_ref[head // 4, head % 4 : head % 4 + 1, :] = jnp.sum(
                    product[half * HEAD : (half + 1) * HEAD], axis=0, keepdims=True
                )

        @pl.when(row < rows - 1)
        def _():
            for copy in feed_loads(row + 1):
                copy.start()

    low = head_lanes(tokens, BF16)
    rank_row = lax.broadcasted_iota(jnp.int32, (8, width), 0) < 4

    def attend_chunk(row, s):
        query = place * tokens + lax.broadcasted_iota(jnp.int32, (tokens, tokens), 1)
        key = (place - s) * tokens + lax.broadcasted_iota(jnp.int32, (tokens, tokens), 0)
        allowed = key >= start_ref[row]
        if s == 0:
            allowed = allowed & (key <= query)
        mask_ref[...] = jnp.where(allowed, 0.0, MASKED)
        rows_s = slice(s * tokens, (s + 1) * tokens)

        @pl.loop(0, quads)
        def _(quad):
            base = pl.multiple_of(quad * QUAD, QUAD)
            for pair in range(QUAD // PAIR):
                span = pl.ds(base + pair * PAIR, PAIR)
                q_pair, g_pair = q_held[:, span], gmix_ref[:, span]
                k_pair, v_pair = k_held[rows_s, span], v_held[rows_s, span]
                k_turned = k_pair.astype(F32).T.astype(BF16)
                dk, dv = None, None
                for half in range(2):
                    own = low if half == 0 else jnp.logical_not(low)
                    q_head = jnp.where(own, q_pair, jnp.zeros_like(q_pair))
                    g_head = jnp.where(own, g_pair, jnp.zeros_like(g_pair))
                    head = pair * 2 + half
                    lse = lse_ref[row, quad, head : head + 1, :]
                    inner = delta_ref[quad, head : head + 1, :]
                    prob = jnp.exp(dot_nt(k_pair, q_head) + mask_ref[...] - lse)
                    g_score = (prob * (dot_nt(v_pair, g_head) - inner)).astype(BF16)
                    part_v = dot_nn(prob.astype(BF16), g_head)
                    part_k = dot_nn(g_score, q_head)
                    dv = part_v if dv is None else dv + part_v
                    dk = part_k if dk is None else dk + part_k
                    lines = pl.ds(base + (pair * PAIR + half * HEAD), HEAD)
                    dq_ref[lines, :] += dot_nn(k_turned[half * HEAD : (half + 1) * HEAD], g_score)
                dkv_ref[:, span] = dk.astype(BF16)
                dkv_ref[:, pl.ds(base + (width + pair * PAIR), PAIR)] = dv.astype(BF16)

        grad = dot_nt(dkv_ref[...], w_held[:, width:])
        dv = dkv_ref[:, width:]
        up_grad = dot_nn(down_ref[row, :, rows_s], dv)
        g_down = dot_nt(dv, up_ref[...]).T[:8].astype(BF16)
        reduce_grad = dot_nn(g_down, hidden[s])
        up_sum[...] += jnp.where(rank_row, 0.0, up_grad)
        reduce_sum[...] += jnp.where(rank_row, 0.0, reduce_grad)
        if s > 0:
            @pl.when(row > 0)
            def _():
                leave(row - 1, s).wait_send()

            leaving[s - 1] = grad.astype(BF16)

            @pl.when(place == top)
            def _():
                leave(row, s).start()
        else:
            dq = (dq_ref[...].T * (HEAD**-0.5)).astype(BF16)
            own_ref[...] = grad + dot_nt(dq, w_held[:, :width])
            up_grad = dot_nn(down_ref[row, :, rows_s], dq)
            g_down = dot_nt(dq, up_ref[...]).T[:8].astype(BF16)
            reduce_grad = dot_nn(g_down, hidden[s])
            up_sum[...] += jnp.where(rank_row, up_grad, 0.0)
            reduce_sum[...] += jnp.where(rank_row, reduce_grad, 0.0)

    @pl.loop(0, rows)
    def _(row):
        feed(row)

        @pl.when(row > 0)
        def _():
            chain(row - 1, 2)

        for copy in attend_loads(row):
            copy.wait()

        @pl.when(row == 0)
        def _():
            w_load.wait()

        dq_ref[...] = jnp.zeros_like(dq_ref)
        for s in range(seq - 1, -1, -1):
            if s < seq - 3:
                @pl.when(row > 0)
                def _():
                    chain(row - 1, seq - 1 - s)

            @pl.when(place >= s)
            def _():
                attend_chunk(row, s)

            if s == 1:
                chain(row, 1)

        @pl.when(row < rows - 1)
        def _():
            for copy in attend_loads(row + 1):
                copy.start()

    def send(source, target, slot, device):
        copy = pltpu.make_async_remote_copy(
            src_ref=source, dst_ref=target, send_sem=sum_send.at[slot], recv_sem=sum_recv.at[slot],
            device_id=device, device_id_type=mesh_type,
        )
        copy.start()
        return copy

    pieces, piece = part_ref.shape[0], part_ref.shape[1]
    lanes = width // PAIR
    part_ref[...] = jnp.zeros_like(part_ref)
    for half, total in enumerate((reduce_sum[...] * ADAPTER_SCALE, up_sum[...])):
        for lane in range(lanes):
            line = (half * lanes + lane) * 8
            part_ref[line // piece, line % piece : line % piece + 8, :] = total[:, lane * PAIR : (lane + 1) * PAIR]
    copies = [send(part_ref.at[lax.rem(me + delta, dp)], plane_ref.at[delta], delta, peer(delta)) for delta in range(1, dp)]
    last = rows - 1
    chain(last, 2)
    total = part_ref[me]
    for delta in range(1, dp):
        copies[delta - 1].wait()
        total = total + plane_ref[delta]
    line_ref[place] = total
    copies = [send(line_ref.at[place], line_ref.at[place], dp + delta, line_peer(delta)) for delta in range(1, seq)]
    for copy in copies:
        copy.wait()
    total = line_ref[0]
    for index in range(1, seq):
        total = total + line_ref[index]
    sum_out[me] = total
    copies = [send(sum_out.at[me], sum_out.at[me], dp + seq + delta, peer(delta)) for delta in range(1, dp)]
    for k in range(3, seq):
        chain(last, k)
    for copy in copies:
        copy.wait()
    for s in range(1, seq):
        @pl.when(place >= s)
        def _():
            leave(last, s).wait_send()
    out_store(last).wait()
    for row in range(max(0, rows - 2), rows):
        grad_store(row).wait()


def run_finish(dp, seq, x, starts, lse, down, up_wide, vectors, gout, w, wo, fc, proj, hidden, q, k, v, mixed):
    rows, tokens, width = x.shape
    length = seq * tokens
    hidden_units = fc.shape[1]
    block = 1024
    quads = width // QUAD
    piece = max(8, 16 * width // (PAIR * dp))
    anywhere = pl.BlockSpec(memory_space=pl.ANY)
    vmem = pl.BlockSpec(memory_space=pltpu.VMEM)
    slots = 2 * dp + seq

    def held(*dims, dtype=BF16):
        return pltpu.VMEM(dims, dtype)

    out, grad, total = pl.pallas_call(
        partial(finish_kernel, dp, seq, rows, block),
        in_specs=[vmem] * 11 + [anywhere] * 10,
        out_specs=[anywhere, anywhere, vmem],
        out_shape=[
            jax.ShapeDtypeStruct((rows, tokens, width), BF16),
            jax.ShapeDtypeStruct((rows, tokens, width), F32),
            jax.ShapeDtypeStruct((dp, piece, PAIR), F32),
        ],
        scratch_shapes=[
            held(width, 3 * width), held(width, width), held(width, hidden_units), held(hidden_units, width),
            held(seq, tokens, width), held(tokens, width), held(length, width), held(length, width),
            held(tokens, width), held(tokens, width),
            held(tokens, width), held(tokens, width, dtype=F32), held(tokens, width),
            held(tokens, width, dtype=F32), held(tokens, width, dtype=F32), held(2, tokens, width, dtype=F32),
            held(tokens, width, dtype=F32), held(tokens, tokens, dtype=F32), held(quads, 8, tokens, dtype=F32),
            held(width, tokens, dtype=F32), held(tokens, 2 * width),
            held(seq - 1, tokens, width), held(rows, seq - 1, tokens, width), held(tokens, width),
            held(8, width, dtype=F32), held(8, width, dtype=F32),
            held(dp, piece, PAIR, dtype=F32), held(dp, piece, PAIR, dtype=F32), held(seq, piece, PAIR, dtype=F32),
            pltpu.SemaphoreType.DMA((3, max(2, hidden_units // block))),
            pltpu.SemaphoreType.DMA((6,)),
            pltpu.SemaphoreType.DMA((3,)),
            pltpu.SemaphoreType.DMA((seq - 1,)),
            pltpu.SemaphoreType.DMA((rows, seq - 1)),
            pltpu.SemaphoreType.DMA((slots,)),
            pltpu.SemaphoreType.DMA((slots,)),
        ],
        compiler_params=pltpu.CompilerParams(
            vmem_limit_bytes=FINISH_BYTES, collective_id=1, has_side_effects=True
        ),
        name="finish",
    )(x, starts, lse, down, up_wide, *vectors, gout, w, wo, fc, proj, hidden, q, k, v, mixed)
    flat = total.reshape(-1, PAIR)[: 16 * width // PAIR]
    return out, grad, flat.reshape(2, width // PAIR, 8, PAIR).transpose(0, 2, 1, 3).reshape(2, 8, width)


def run_start(plane, seq, x, starts, gain, shift, shard, reduce_wide, up_wide, bias_q, bias_v, wo, fc, proj):
    rows, tokens, width = x.shape
    length = seq * tokens
    quads = width // QUAD
    dp = plane[0] * plane[1] * 2
    anywhere = pl.BlockSpec(memory_space=pl.ANY)
    vmem = pl.BlockSpec(memory_space=pltpu.VMEM)
    nx, ny = plane
    slots = nx - 1 + ny - 1 + 2 * (nx - 1) * (ny - 1) + nx * ny

    def shape(*dims, dtype=BF16):
        return jax.ShapeDtypeStruct(dims, dtype)

    def whole_of(part):
        return shape(part.shape[0] * dp, part.shape[1])

    return pl.pallas_call(
        partial(start_kernel, plane, seq, rows),
        in_specs=[vmem] * 9 + [anywhere] * 3,
        out_specs=[anywhere] * 9 + [vmem] * 2,
        out_shape=[
            whole_of(shard), whole_of(wo), whole_of(fc), whole_of(proj),
            shape(rows, seq, tokens, width),
            shape(rows, tokens, width), shape(rows, length, width), shape(rows, length, width),
            shape(rows, tokens, width),
            shape(rows, quads, 8, tokens, dtype=F32),
            shape(rows, 8, length),
        ],
        scratch_shapes=[
            pltpu.VMEM((width, 3 * width), BF16),
            pltpu.VMEM((rows, seq, tokens, width), BF16),
            pltpu.VMEM((2, tokens, width), BF16),
            pltpu.VMEM((2, length, width), BF16),
            pltpu.VMEM((2, length, width), BF16),
            pltpu.VMEM((2, tokens, width), BF16),
            pltpu.VMEM((tokens, length), F32),
            pltpu.SemaphoreType.DMA((4, slots)),
            pltpu.SemaphoreType.DMA((4, slots)),
            pltpu.SemaphoreType.DMA((rows, seq - 1)),
            pltpu.SemaphoreType.DMA((rows, seq - 1)),
            pltpu.SemaphoreType.DMA((4 + rows,)),
            pltpu.SemaphoreType.DMA((2, 4)),
        ],
        compiler_params=pltpu.CompilerParams(
            vmem_limit_bytes=VMEM_BYTES, collective_id=0, has_side_effects=True
        ),
        name="start",
    )(x, starts, gain, shift, shard, reduce_wide, up_wide, bias_q, bias_v, wo, fc, proj)


def on_device(
    dp,
    seq,
    block_input,
    seg_start,
    ln1_gain,
    ln1_bias,
    qkv_weight,
    query_bias,
    value_bias,
    query_adapter_reduce,
    query_up,
    value_adapter_reduce,
    value_up,
    out_weight,
    out_bias,
    ln2_gain,
    ln2_bias,
    fc_weight,
    fc_bias,
    proj_weight,
    proj_bias,
    grad_out,
):
    rows, tokens, width = block_input.shape
    rank = query_up.shape[0]
    place = lax.axis_index("seq")
    side = math.isqrt(dp // 2)

    pad = jnp.zeros((width, PAIR - 2 * rank), BF16)
    reduce_wide = jnp.concatenate([query_adapter_reduce, value_adapter_reduce, pad], axis=1)
    up_wide = jnp.concatenate([query_up, value_up, pad.T], axis=0)
    starts = lax.dynamic_slice(seg_start, (0, place * tokens), (rows, tokens))
    def as_row(vector):
        return vector.reshape(1, -1)

    weight, whole_out, whole_fc, whole_proj, hidden, q, k, v, mixed, lse, down = run_start(
        (side, dp // (2 * side)), seq, block_input, starts[:, :, None], as_row(ln1_gain), as_row(ln1_bias), qkv_weight,
        reduce_wide, up_wide, as_row(query_bias), as_row(value_bias), out_weight, fc_weight, proj_weight,
    )

    vectors = tuple(as_row(a) for a in (ln1_gain, out_bias, ln2_gain, ln2_bias, proj_bias, fc_bias))
    out, grad, small = run_finish(
        dp, seq, block_input, starts[:, None, :], lse, down, up_wide, vectors, grad_out,
        weight, whole_out, whole_fc, whole_proj, hidden, q, k, v, mixed,
    )
    reduce, up = small[0], small[1]
    return out, grad, reduce[:rank].T, up[:rank], reduce[rank : 2 * rank].T, up[rank : 2 * rank]


def solution(mesh):
    return jax.shard_map(
        partial(on_device, mesh.shape["dp"], mesh.shape["seq"]),
        mesh=mesh,
        in_specs=(
            P("dp", "seq", None),
            P("dp", None),
            P(),
            P(),
            P("dp", None),
            P(),
            P(),
            P(),
            P(),
            P(),
            P(),
            P("dp", None),
            P(),
            P(),
            P(),
            P("dp", None),
            P(),
            P("dp", None),
            P(),
            P("dp", "seq", None),
        ),
        out_specs=(P("dp", "seq", None), P("dp", "seq", None), P(), P(), P(), P()),
        check_vma=False,
    )
```

```python
import math
from functools import partial

import jax
import jax.numpy as jnp
from jax import lax
from jax.experimental import pallas as pl
from jax.experimental.pallas import tpu as pltpu
from jax.sharding import PartitionSpec as P

HEAD = 64
QUAD = 256
PAIR = 128
NORM_EPSILON = 1e-05
ADAPTER_SCALE = 8.0
MASKED = -1e30
GELU_A = 0.7978845608028654
GELU_B = 0.044715

F32 = jnp.float32
BF16 = jnp.bfloat16
VMEM_BYTES = 65400 * 1024


def dot_nn(left, right):
    return lax.dot_general(left, right, (((1,), (0,)), ((), ())), preferred_element_type=F32)


def dot_nt(left, right):
    return lax.dot_general(left, right, (((1,), (1,)), ((), ())), preferred_element_type=F32)


def norm_parts(values):
    average = jnp.mean(values, axis=-1, keepdims=True)
    centered = values - average
    inverse = lax.rsqrt(jnp.mean(centered * centered, axis=-1, keepdims=True) + NORM_EPSILON)
    return centered * inverse, inverse


def norm_backward(gradient, normed, inverse, gain):
    scaled = gradient * gain
    return inverse * (
        scaled
        - jnp.mean(scaled, axis=-1, keepdims=True)
        - normed * jnp.mean(scaled * normed, axis=-1, keepdims=True)
    )


def head_lanes(rows, dtype):
    lane = lax.broadcasted_iota(jnp.int32, (rows, PAIR), 1)
    return lane < HEAD


def own_starts(seg_ref, begin_ref, place, seq):
    rows, _, tokens = begin_ref.shape
    own = jnp.zeros((rows, tokens), jnp.int32)
    for index in range(seq):
        own = jnp.where(place == index, seg_ref[:, index * tokens : (index + 1) * tokens], own)
    own = own.astype(F32)
    for row in range(rows):
        begin_ref[row] = jnp.broadcast_to(own[row : row + 1], (8, tokens))


def block_kernel(
    plane, seq, rows, block,
    x_ref, seg_ref, small_ref, gain1, shift1, bias_q, bias_v, out_bias, gain2, shift2, proj_bias, fc_bias,
    shard_in, wo_in, fc_in, proj_in, gout_in,
    out_out, grad_out, sum_out, q_spill, k_spill, v_spill,
    w_held, wo_held, fc_held, proj_held, hidden, q_held, k_held, v_held, mix_held, gout_held,
    gmix_ref, h2_ref, acc_ref, back_ref, gmid_ref, own_ref, mask_ref, delta_ref, dq_ref, dkv_ref,
    leaving, arriving, begin_ref, turned_ref, lse_ref, down_ref, up_sum, reduce_sum,
    part_ref, plane_ref, line_ref,
    send_sems, recv_sems, hop_send, hop_recv, own_sems, spill_sems, gout_sem, store_sems,
    leave_sems, arrive_sems, sum_send, sum_recv,
):
    nx, ny = plane
    dp = nx * ny * 2
    tokens, width = x_ref.shape[1], x_ref.shape[2]
    quads = width // QUAD
    steps = fc_held.shape[1] // block
    top = seq - 1
    mesh_type = pl.DeviceIdType.MESH
    me, place = lax.axis_index("dp"), lax.axis_index("seq")
    core = lax.rem(me, 2)
    my_x = lax.rem(me // 2, nx)
    my_y = me // (2 * nx)

    def index(y, x, c):
        return (y * nx + x) * 2 + c

    def x_peer(delta):
        return index(my_y, lax.rem(my_x + delta, nx), core), place

    def y_peer(delta):
        return index(lax.rem(my_y + delta, ny), my_x, core), place

    twin = (index(my_y, my_x, 1 - core), place)

    def owner(dy, dx, c):
        return index(lax.rem(my_y + ny - dy, ny), lax.rem(my_x + nx - dx, nx), c)

    def peer(delta):
        return lax.rem(me + delta, dp), place

    def line_peer(delta):
        return me, lax.rem(place + delta, seq)

    barrier = pltpu.get_barrier_semaphore()
    for delta in range(1, dp):
        pl.semaphore_signal(barrier, inc=1, device_id=peer(delta), device_id_type=mesh_type)
    for delta in range(1, seq):
        pl.semaphore_signal(barrier, inc=1, device_id=line_peer(delta), device_id_type=mesh_type)

    sources = [shard_in, wo_in, fc_in, proj_in]
    targets = [w_held, wo_held, fc_held, proj_held]

    def region(t, device, half=None):
        size = sources[t].shape[0]
        if half is None:
            return targets[t].at[pl.ds(pl.multiple_of(device * size, size), size), :]
        part = size // 2
        return targets[t].at[pl.ds(pl.multiple_of(device * size + half * part, part), part), :]

    def flight(t, slot, part, device):
        return pltpu.make_async_remote_copy(
            src_ref=part, dst_ref=part, send_sem=send_sems.at[t, slot], recv_sem=recv_sems.at[t, slot],
            device_id=device, device_id_type=mesh_type,
        )

    flights = {}
    for t in range(4):
        names = [("x", 0, dx) for dx in range(1, nx)] + [("y", dy, 0) for dy in range(1, ny)]
        names += [(kind, dy, dx) for kind in "ab" for dy in range(1, ny) for dx in range(1, nx)]
        names += [("t", dy, dx) for dy in range(ny) for dx in range(nx)]
        for slot, (kind, dy, dx) in enumerate(names):
            if kind == "x":
                part, device = region(t, me), x_peer(dx)
            elif kind == "y":
                part, device = region(t, me), y_peer(dy)
            elif kind == "a":
                part, device = region(t, owner(0, dx, core), 0), y_peer(dy)
            elif kind == "b":
                part, device = region(t, owner(dy, 0, core), 1), x_peer(dx)
            else:
                part, device = region(t, owner(dy, dx, core)), twin
            flights[t, kind, dy, dx] = flight(t, slot, part, device)

    def wave_one(t):
        for dx in range(1, nx):
            flights[t, "x", 0, dx].start()
        for dy in range(1, ny):
            flights[t, "y", dy, 0].start()
        flights[t, "t", 0, 0].start()

    def wave_two(t):
        for dx in range(1, nx):
            flights[t, "x", 0, dx].wait_recv()
            for dy in range(1, ny):
                flights[t, "a", dy, dx].start()
        for dy in range(1, ny):
            flights[t, "y", dy, 0].wait_recv()
            for dx in range(1, nx):
                flights[t, "b", dy, dx].start()
        for dx in range(1, nx):
            flights[t, "t", 0, dx].start()
        for dy in range(1, ny):
            flights[t, "t", dy, 0].start()

    def wave_three(t):
        for dy in range(1, ny):
            for dx in range(1, nx):
                flights[t, "a", dy, dx].wait_recv()
                flights[t, "b", dy, dx].wait_recv()
                flights[t, "t", dy, dx].start()

    def wave_end(t):
        for dy in range(ny):
            for dx in range(nx):
                flights[t, "t", dy, dx].wait_recv()

    def hop(row, s):
        return pltpu.make_async_remote_copy(
            src_ref=hidden.at[row, s - 1], dst_ref=hidden.at[row, s],
            send_sem=hop_send.at[row, s - 1], recv_sem=hop_recv.at[row, s - 1],
            device_id=(me, place + 1), device_id_type=mesh_type,
        )

    def hop_start(row, s):
        @pl.when((place >= s - 1) & (place < top))
        def _():
            hop(row, s).start()

    def arrive(row, s):
        @pl.when(place >= s)
        def _():
            hop(row, s).wait_recv()

        if s < seq - 1:
            hop_start(row, s + 1)
        if s == seq - 1 and row < rows - 1:
            hop_start(row + 1, 1)

    def first_norm(row):
        normed, _ = norm_parts(x_ref[row].astype(F32))
        hidden[row, 0] = (normed * gain1[...] + shift1[...]).astype(BF16)

    def gout_load(row):
        return pltpu.make_async_copy(gout_in.at[row], gout_held, gout_sem)

    own_copies = [pltpu.make_async_copy(sources[t], region(t, me), own_sems.at[t]) for t in range(4)]
    for copy in own_copies:
        copy.start()
    gout_load(0).start()
    first_norm(0)
    turned_ref[...] = small_ref[:8, :].astype(F32).T
    pl.semaphore_wait(barrier, dp + seq - 2)
    hop_start(0, 1)
    own_copies[0].wait()
    size = shard_in.shape[0]
    mine = pl.ds(pl.multiple_of(me * size, size), size)
    reduce_own = turned_ref[mine, :].astype(BF16)
    up = small_ref[8:, :]
    low_rank = lax.broadcasted_iota(jnp.int32, up.shape, 0) < 4
    for column, rank_up in ((0, jnp.where(low_rank, up, jnp.zeros_like(up))), (2, jnp.where(low_rank, jnp.zeros_like(up), up))):
        span = slice(column * width, (column + 1) * width)
        change = dot_nn(reduce_own, rank_up) * ADAPTER_SCALE
        w_held[mine, span] = (w_held[mine, span].astype(F32) + change).astype(BF16)
    wave_one(0)
    for copy in own_copies[1:]:
        copy.wait()
    wave_one(1)
    own_starts(seg_ref, begin_ref, place, seq)
    for row in range(1, rows):
        first_norm(row)
    for s in range(1, seq):
        @pl.when(place < s)
        def _():
            for row in range(rows):
                hidden[row, s] = jnp.zeros((tokens, width), BF16)
    up_sum[...] = jnp.zeros_like(up_sum)
    reduce_sum[...] = jnp.zeros_like(reduce_sum)

    low = head_lanes(tokens, BF16)
    lane = lax.broadcasted_iota(jnp.int32, (tokens, PAIR), 1)
    rank_row = lax.broadcasted_iota(jnp.int32, (8, width), 0) < 4

    def both_heads(pair):
        none = jnp.zeros_like(pair)
        return jnp.concatenate([jnp.where(low, pair, none), jnp.where(low, none, pair)], axis=0)

    def spills(row):
        return [
            pltpu.make_async_copy(held, spill.at[row], spill_sems.at[i])
            for i, (held, spill) in enumerate(((q_held, q_spill), (k_held, k_spill), (v_held, v_spill)))
        ]

    def reloads(row):
        return [
            pltpu.make_async_copy(spill.at[row], held, spill_sems.at[3 + i])
            for i, (held, spill) in enumerate(((q_held, q_spill), (k_held, k_spill), (v_held, v_spill)))
        ]

    def attend(row, middle):
        slot = lax.rem(row, 2)
        query = place * tokens + lax.broadcasted_iota(jnp.int32, (tokens, tokens), 0)
        start = begin_ref[row].T[:, :1].astype(jnp.int32)
        for s in range(seq):
            key = (place - s) * tokens + lax.broadcasted_iota(jnp.int32, (tokens, tokens), 1)
            span = slice(s * tokens, (s + 1) * tokens)
            mask_ref[:, span] = jnp.where((key >= start) & (key <= query), 0.0, MASKED)
            down_ref[row, :, span] = (dot_nt(small_ref[:8, :], hidden[row, s]) * ADAPTER_SCALE).astype(BF16)

        for quad in range(quads):
            own = slice(quad * QUAD, (quad + 1) * QUAD)
            key_span = slice(width + quad * QUAD, width + (quad + 1) * QUAD)
            value_span = slice(2 * width + quad * QUAD, 2 * width + (quad + 1) * QUAD)
            q = dot_nn(hidden[row, 0], w_held[:, own]) + bias_q[:, own]
            q_held[:, own] = (q.astype(BF16) * (HEAD**-0.5)).astype(BF16)
            for s in range(seq):
                span = slice(s * tokens, (s + 1) * tokens)
                k_held[span, own] = dot_nn(hidden[row, s], w_held[:, key_span]).astype(BF16)
                v_held[span, own] = (dot_nn(hidden[row, s], w_held[:, value_span]) + bias_v[:, own]).astype(BF16)
            totals = jnp.zeros((tokens, PAIR), F32)
            for pair in range(QUAD // PAIR):
                span = slice(quad * QUAD + pair * PAIR, quad * QUAD + (pair + 1) * PAIR)
                score = dot_nt(both_heads(q_held[:, span]), k_held[:, span])
                score = jnp.concatenate([score[:tokens] + mask_ref[...], score[tokens:] + mask_ref[...]], axis=0)
                highest = jnp.max(score, axis=-1, keepdims=True)
                weight = jnp.exp(score - highest)
                total = jnp.sum(weight, axis=-1, keepdims=True)
                mixed = dot_nn(weight.astype(BF16), v_held[:, span]) * (1.0 / total)
                mix_held[slot, :, span] = jnp.where(low, mixed[:tokens], mixed[tokens:]).astype(BF16)
                lse = highest + jnp.log(total)
                totals = jnp.where(lane == 2 * pair, lse[:tokens], totals)
                totals = jnp.where(lane == 2 * pair + 1, lse[tokens:], totals)
            lse_ref[row, quad] = totals.T[:8]
            if 2 * (quad + 1) == quads:
                middle()

    def out_store(row):
        return pltpu.make_async_copy(h2_ref, out_out.at[row], store_sems.at[0])

    def grad_store(row):
        slot = lax.rem(row, 2)
        return pltpu.make_async_copy(gmid_ref.at[slot], grad_out.at[row], store_sems.at[1 + slot])

    def leave(row, s):
        return pltpu.make_async_remote_copy(
            src_ref=leaving.at[s - 1], dst_ref=arriving.at[row, s - 1],
            send_sem=leave_sems.at[s - 1], recv_sem=arrive_sems.at[row, s - 1],
            device_id=(me, place - 1), device_id_type=mesh_type,
        )

    def chain(row, s):
        @pl.when((place < top) & (place >= s))
        def _():
            leave(row, s + 1).wait_recv()
            leaving[s - 1] = (leaving[s - 1].astype(F32) + arriving[row, s].astype(F32)).astype(BF16)
            leave(row, s).start()

    def chain_end(row):
        @pl.when(place < top)
        def _():
            leave(row, 1).wait_recv()
            own_ref[...] += arriving[row, 0].astype(F32)

        slot = lax.rem(row, 2)
        normed, inverse = norm_parts(x_ref[row].astype(F32))
        gmid_ref[slot] = gmid_ref[slot] + norm_backward(own_ref[...], normed, inverse, gain1[...])
        grad_store(row).start()

    def feed(row):
        slot = lax.rem(row, 2)
        gout_load(row).wait()

        @pl.when(row >= 1)
        def _():
            out_store(row - 1).wait()

        @pl.when(row >= 2)
        def _():
            grad_store(row - 2).wait()

        middle = x_ref[row].astype(F32) + dot_nn(mix_held[slot], wo_held[...]) + out_bias[...]
        gmid_ref[slot] = middle
        normed, _ = norm_parts(middle)
        h2_ref[...] = (normed * gain2[...] + shift2[...]).astype(BF16)
        acc_ref[...] = jnp.zeros_like(acc_ref)
        back_ref[...] = jnp.zeros_like(back_ref)

        @pl.when(row < rows - 1)
        def _():
            for copy in spills(row + 1):
                copy.wait()

        for copy in reloads(row):
            copy.start()

        @pl.loop(0, steps)
        def _(step):
            part = pl.ds(pl.multiple_of(step * block, block), block)
            before = dot_nn(h2_ref[...], fc_held[:, part]) + fc_bias[:, part]
            square = before * before
            bend = jnp.tanh(GELU_A * before * (1.0 + GELU_B * square))
            half = 0.5 * (1.0 + bend)
            slope = half + 0.5 * before * (1.0 - bend * bend) * (GELU_A * (1.0 + 3.0 * GELU_B * square))
            act = (before * half).astype(BF16)
            g_before = (dot_nt(gout_held[...], proj_held[part, :]) * slope).astype(BF16)
            acc_ref[...] += dot_nn(act, proj_held[part, :])
            back_ref[...] += dot_nt(g_before, fc_held[:, part])

        middle = gmid_ref[slot]
        h2_ref[...] = (middle + acc_ref[...] + proj_bias[...]).astype(BF16)
        out_store(row).start()
        normed, inverse = norm_parts(middle)
        g_middle = gout_held[...].astype(F32) + norm_backward(back_ref[...], normed, inverse, gain2[...])
        gmid_ref[slot] = g_middle
        gmix_ref[...] = dot_nt(g_middle.astype(BF16), wo_held[...]).astype(BF16)
        for pair in range(width // PAIR):
            span = slice(pair * PAIR, (pair + 1) * PAIR)
            product = (gmix_ref[:, span].astype(F32) * mix_held[slot, :, span].astype(F32)).T
            for half in range(2):
                head = pair * 2 + half
                delta_ref[head // 4, head % 4 : head % 4 + 1, :] = jnp.sum(
                    product[half * HEAD : (half + 1) * HEAD], axis=0, keepdims=True
                )

        @pl.when(row < rows - 1)
        def _():
            gout_load(row + 1).start()

    def attend_chunk(row, s):
        query = place * tokens + lax.broadcasted_iota(jnp.int32, (tokens, tokens), 1)
        key = (place - s) * tokens + lax.broadcasted_iota(jnp.int32, (tokens, tokens), 0)
        start = begin_ref[row, :1, :].astype(jnp.int32)
        mask = jnp.where((key >= start) & (key <= query), 0.0, MASKED)
        mask_ref[:, :tokens] = mask
        mask_ref[:, tokens : 2 * tokens] = mask
        rows_s = pl.ds(pl.multiple_of(s * tokens, tokens), tokens)
        for pair in range(width // PAIR):
            span = slice(pair * PAIR, (pair + 1) * PAIR)
            k_pair, v_pair = k_held[rows_s, span], v_held[rows_s, span]
            q_both, g_both = both_heads(q_held[:, span]), both_heads(gmix_ref[:, span])
            head = 2 * (pair % 2)
            lse, inner = [
                jnp.concatenate([ref[head : head + 1, :], ref[head + 1 : head + 2, :]], axis=1)
                for ref in (lse_ref.at[row, pair // 2], delta_ref.at[pair // 2])
            ]
            prob = jnp.exp(dot_nt(k_pair, q_both) + mask_ref[:, : 2 * tokens] - lse)
            g_score = (prob * (dot_nt(v_pair, g_both) - inner)).astype(BF16)
            dkv_ref[:, span] = dot_nn(g_score, q_both).astype(BF16)
            dkv_ref[:, width + pair * PAIR : width + (pair + 1) * PAIR] = dot_nn(prob.astype(BF16), g_both).astype(BF16)
            k_turned = k_pair.astype(F32).T.astype(BF16)
            for half in range(2):
                lines = slice(pair * PAIR + half * HEAD, pair * PAIR + (half + 1) * HEAD)
                part = g_score[:, half * tokens : (half + 1) * tokens]
                dq_ref[lines, :] += dot_nn(k_turned[half * HEAD : (half + 1) * HEAD], part)

        grad = dot_nt(dkv_ref[...], w_held[:, width:])
        dv = dkv_ref[:, width:]
        up_grad = dot_nn(down_ref[row, :, rows_s], dv)
        g_down = dot_nt(small_ref[8:, :], dv).astype(BF16)
        reduce_grad = dot_nn(g_down, hidden[row, s])
        up_sum[...] += jnp.where(rank_row, 0.0, up_grad)
        reduce_sum[...] += jnp.where(rank_row, 0.0, reduce_grad)
        if not isinstance(s, int):
            @pl.when(row > 0)
            def _():
                leave(row - 1, s).wait_send()

            leaving[s - 1] = grad.astype(BF16)

            @pl.when(place == top)
            def _():
                leave(row, s).start()
        else:
            dq = (dq_ref[...].T * (HEAD**-0.5)).astype(BF16)
            own_ref[...] = grad + dot_nt(dq, w_held[:, :width])
            up_grad = dot_nn(down_ref[row, :, rows_s], dq)
            g_down = dot_nt(small_ref[8:, :], dq).astype(BF16)
            reduce_grad = dot_nn(g_down, hidden[row, s])
            up_sum[...] += jnp.where(rank_row, up_grad, 0.0)
            reduce_sum[...] += jnp.where(rank_row, reduce_grad, 0.0)

    def before_first():
        arrive(0, 1)
        wave_two(0)
        wave_one(2)
        wave_two(1)
        for s in range(2, seq):
            if s == seq - 1:
                wave_three(0)
                wave_three(1)
            arrive(0, s)
        wave_end(0)
        wave_one(3)

    def before_second():
        for s in range(1, seq):
            arrive(1, s)

    def amid_second():
        wave_two(2)
        wave_two(3)
        arrive(2, 1)

    def after_second():
        for s in range(2, seq):
            arrive(2, s)
        wave_three(2)
        wave_three(3)
        for t in range(1, 4):
            wave_end(t)

    def before_later(row):
        for s in range(1, seq):
            arrive(row, s)

    @pl.loop(0, rows + 1)
    def _(turn):
        for index in range(rows):
            if index != 2:
                action = before_first if index == 0 else before_second if index == 1 else partial(before_later, index)
                pl.when(turn == index)(action)

        @pl.when(turn == 1)
        def _():
            for copy in spills(0):
                copy.wait()

        @pl.when(turn < rows)
        def _():
            attend(turn, lambda: pl.when(turn == 1)(amid_second))
            for copy in spills(turn):
                copy.start()

        pl.when(turn == 1)(after_second)

        @pl.when(turn > 0)
        def _():
            row = turn - 1
            feed(row)

            @pl.when(row > 0)
            def _():
                chain(row - 1, seq - 3)

            for copy in reloads(row):
                copy.wait()
            dq_ref[...] = jnp.zeros_like(dq_ref)

            @pl.loop(0, seq - 1)
            def _(step):
                s = seq - 1 - step

                @pl.when((row > 0) & (s < seq - 3))
                def _():
                    chain(row - 1, s)

                @pl.when(place >= s)
                def _():
                    attend_chunk(row, s)

            chain(row, seq - 2)

            @pl.when(row > 0)
            def _():
                chain_end(row - 1)

            attend_chunk(row, 0)

    def send(source, target, slot, device):
        copy = pltpu.make_async_remote_copy(
            src_ref=source, dst_ref=target, send_sem=sum_send.at[slot], recv_sem=sum_recv.at[slot],
            device_id=device, device_id_type=mesh_type,
        )
        copy.start()
        return copy

    piece = part_ref.shape[1]
    lanes = width // PAIR
    part_ref[...] = jnp.zeros_like(part_ref)
    for half, total in enumerate((reduce_sum[...] * ADAPTER_SCALE, up_sum[...])):
        for block_lane in range(lanes):
            line = (half * lanes + block_lane) * 8
            part_ref[line // piece, line % piece : line % piece + 8, :] = total[:, block_lane * PAIR : (block_lane + 1) * PAIR]
    copies = [send(part_ref.at[lax.rem(me + delta, dp)], plane_ref.at[delta], delta, peer(delta)) for delta in range(1, dp)]
    last = rows - 1
    chain(last, seq - 3)
    total = part_ref[me]
    for delta in range(1, dp):
        copies[delta - 1].wait()
        total = total + plane_ref[delta]
    line_ref[place] = total
    copies = [send(line_ref.at[place], line_ref.at[place], dp + delta, line_peer(delta)) for delta in range(1, seq)]
    for copy in copies:
        copy.wait()
    total = line_ref[0]
    for other in range(1, seq):
        total = total + line_ref[other]
    sum_out[me] = total
    copies = [send(sum_out.at[me], sum_out.at[me], dp + seq + delta, peer(delta)) for delta in range(1, dp)]
    for s in range(seq - 4, 0, -1):
        chain(last, s)
    chain_end(last)
    for copy in copies:
        copy.wait()
    for copy in flights.values():
        copy.wait_send()
    for row in range(rows):
        for s in range(1, seq):
            @pl.when((place >= s - 1) & (place < top))
            def _():
                hop(row, s).wait_send()
    for s in range(1, seq):
        @pl.when(place >= s)
        def _():
            leave(last, s).wait_send()
    out_store(last).wait()
    for row in range(max(0, rows - 2), rows):
        grad_store(row).wait()


def run_block(plane, seq, x, seg, small, vectors, shards, gout):
    rows, tokens, width = x.shape
    length = seq * tokens
    dp = plane[0] * plane[1] * 2
    hidden_units = shards[2].shape[1]
    block = 1024
    quads = width // QUAD
    piece = max(8, 16 * width // (PAIR * dp))
    nx, ny = plane
    flights = nx - 1 + ny - 1 + 2 * (nx - 1) * (ny - 1) + nx * ny
    sums = 2 * dp + seq
    anywhere = pl.BlockSpec(memory_space=pl.ANY)
    vmem = pl.BlockSpec(memory_space=pltpu.VMEM)
    dma = pltpu.SemaphoreType.DMA

    def held(*dims, dtype=BF16):
        return pltpu.VMEM(dims, dtype)

    def shape(*dims, dtype=BF16):
        return jax.ShapeDtypeStruct(dims, dtype)

    result = pl.pallas_call(
        partial(block_kernel, plane, seq, rows, block),
        in_specs=[vmem] * 12 + [anywhere] * 5,
        out_specs=[anywhere, anywhere, vmem] + [anywhere] * 3,
        out_shape=[
            shape(rows, tokens, width), shape(rows, tokens, width, dtype=F32), shape(dp, piece, PAIR, dtype=F32),
            shape(rows, tokens, width), shape(rows, length, width), shape(rows, length, width),
        ],
        scratch_shapes=[
            held(width, 3 * width), held(width, width), held(width, hidden_units), held(hidden_units, width),
            held(rows, seq, tokens, width), held(tokens, width), held(length, width), held(length, width),
            held(2, tokens, width), held(tokens, width),
            held(tokens, width), held(tokens, width),
            held(tokens, width, dtype=F32), held(tokens, width, dtype=F32), held(2, tokens, width, dtype=F32),
            held(tokens, width, dtype=F32), held(tokens, length, dtype=F32), held(quads, 8, tokens, dtype=F32),
            held(width, tokens, dtype=F32), held(tokens, 2 * width),
            held(seq - 1, tokens, width), held(rows, seq - 1, tokens, width),
            held(rows, 8, tokens, dtype=F32), held(width, 8, dtype=F32),
            held(rows, quads, 8, tokens, dtype=F32), held(rows, 8, length),
            held(8, width, dtype=F32), held(8, width, dtype=F32),
            held(dp, piece, PAIR, dtype=F32), held(dp, piece, PAIR, dtype=F32), held(seq, piece, PAIR, dtype=F32),
            dma((4, flights)), dma((4, flights)), dma((rows, seq - 1)), dma((rows, seq - 1)),
            dma((4,)), dma((6,)), dma, dma((3,)),
            dma((seq - 1,)), dma((rows, seq - 1)), dma((sums,)), dma((sums,)),
        ],
        compiler_params=pltpu.CompilerParams(
            vmem_limit_bytes=VMEM_BYTES, collective_id=0, has_side_effects=True
        ),
        name="block",
    )(x, seg, small, *vectors, *shards, gout)
    out, grad, total = result[:3]
    flat = total.reshape(-1, PAIR)[: 16 * width // PAIR]
    return out, grad, flat.reshape(2, width // PAIR, 8, PAIR).transpose(0, 2, 1, 3).reshape(2, 8, width)


def on_device(
    dp,
    seq,
    block_input,
    seg_start,
    ln1_gain,
    ln1_bias,
    qkv_weight,
    query_bias,
    value_bias,
    query_adapter_reduce,
    query_up,
    value_adapter_reduce,
    value_up,
    out_weight,
    out_bias,
    ln2_gain,
    ln2_bias,
    fc_weight,
    fc_bias,
    proj_weight,
    proj_bias,
    grad_out,
):
    rows, tokens, width = block_input.shape
    rank = query_up.shape[0]
    side = math.isqrt(dp // 2)
    small = jnp.concatenate([query_adapter_reduce.T, value_adapter_reduce.T, query_up, value_up], axis=0)

    def as_row(vector):
        return vector.reshape(1, -1)

    vectors = tuple(
        as_row(a)
        for a in (ln1_gain, ln1_bias, query_bias, value_bias, out_bias, ln2_gain, ln2_bias, proj_bias, fc_bias)
    )
    out, grad, sums = run_block(
        (side, dp // (2 * side)), seq, block_input, seg_start, small, vectors,
        (qkv_weight, out_weight, fc_weight, proj_weight), grad_out,
    )
    reduce, up = sums[0], sums[1]
    return out, grad, reduce[:rank].T, up[:rank], reduce[rank : 2 * rank].T, up[rank : 2 * rank]


def solution(mesh):
    return jax.shard_map(
        partial(on_device, mesh.shape["dp"], mesh.shape["seq"]),
        mesh=mesh,
        in_specs=(
            P("dp", "seq", None),
            P("dp", None),
            P(),
            P(),
            P("dp", None),
            P(),
            P(),
            P(),
            P(),
            P(),
            P(),
            P("dp", None),
            P(),
            P(),
            P(),
            P("dp", None),
            P(),
            P("dp", None),
            P(),
            P("dp", "seq", None),
        ),
        out_specs=(P("dp", "seq", None), P("dp", "seq", None), P(), P(), P(), P()),
        check_vma=False,
    )
```

```python
import math
from functools import partial

import jax
import jax.numpy as jnp
from jax import lax
from jax.experimental import pallas as pl
from jax.experimental.pallas import tpu as pltpu
from jax.sharding import PartitionSpec as P

HEAD = 64
QUAD = 256
PAIR = 128
NORM_EPSILON = 1e-05
ADAPTER_SCALE = 8.0
MASKED = -1e30
GELU_A = 0.7978845608028654
GELU_B = 0.044715

F32 = jnp.float32
BF16 = jnp.bfloat16
VMEM_BYTES = 65400 * 1024


def dot_nn(left, right):
    return lax.dot_general(left, right, (((1,), (0,)), ((), ())), preferred_element_type=F32)


def dot_nt(left, right):
    return lax.dot_general(left, right, (((1,), (1,)), ((), ())), preferred_element_type=F32)


def norm_parts(values):
    average = jnp.mean(values, axis=-1, keepdims=True)
    centered = values - average
    inverse = lax.rsqrt(jnp.mean(centered * centered, axis=-1, keepdims=True) + NORM_EPSILON)
    return centered * inverse, inverse


def norm_backward(gradient, normed, inverse, gain):
    scaled = gradient * gain
    return inverse * (
        scaled
        - jnp.mean(scaled, axis=-1, keepdims=True)
        - normed * jnp.mean(scaled * normed, axis=-1, keepdims=True)
    )


def head_lanes(rows, dtype):
    lane = lax.broadcasted_iota(jnp.int32, (rows, PAIR), 1)
    return lane < HEAD


def own_starts(seg_ref, begin_ref, place, seq):
    rows, _, tokens = begin_ref.shape
    own = jnp.zeros((rows, tokens), jnp.int32)
    for index in range(seq):
        own = jnp.where(place == index, seg_ref[:, index * tokens : (index + 1) * tokens], own)
    own = own.astype(F32)
    for row in range(rows):
        begin_ref[row] = jnp.broadcast_to(own[row : row + 1], (8, tokens))


def block_kernel(
    plane, seq, rows, block,
    x_in, seg_in, small_in, gain1_in, shift1_in, bias_q_in, bias_v_in, out_bias_in, gain2_in, shift2_in, proj_bias_in,
    fc_bias_in, shard_in, wo_in, fc_in, proj_in, gout_in,
    out_out, grad_out, sum_out, q_spill, k_spill, v_spill, mix_spill,
    x_ref, seg_ref, small_ref, gain1, shift1, bias_q, bias_v, out_bias, gain2, shift2, proj_bias, fc_bias, input_sems,
    w_held, wo_held, fc_held, proj_held, hidden, q_held, k_held, v_held, mix_row, mix_held, gout_held,
    gmix_ref, h2_ref, acc_ref, back_ref, gmid_ref, own_ref, mask_ref, delta_ref, dq_ref, dkv_ref,
    leaving, arriving, begin_ref, bias_held, lse_ref, down_ref, up_sum, reduce_sum,
    part_ref, plane_ref, line_ref,
    send_sems, recv_sems, hop_send, hop_recv, own_sems, spill_sems, load_sems, store_sems,
    leave_sems, arrive_sems, sum_send, sum_recv,
):
    nx, ny = plane
    dp = nx * ny * 2
    inputs = [
        pltpu.make_async_copy(source, target, input_sems.at[i])
        for i, (source, target) in enumerate(
            (
                (x_in, x_ref), (gain1_in, gain1), (shift1_in, shift1), (seg_in, seg_ref), (small_in, small_ref),
                (bias_q_in, bias_q), (bias_v_in, bias_v), (out_bias_in, out_bias), (gain2_in, gain2),
                (shift2_in, shift2), (proj_bias_in, proj_bias), (fc_bias_in, fc_bias),
            )
        )
    ]
    tokens, width = x_ref.shape[1], x_ref.shape[2]
    quads = width // QUAD
    columns, chunk_units = fc_held.shape[0], fc_held.shape[2]
    per_chunk = chunk_units // block
    steps = columns * per_chunk
    early = (columns - 1) * per_chunk
    top = seq - 1
    mesh_type = pl.DeviceIdType.MESH
    me, place = lax.axis_index("dp"), lax.axis_index("seq")
    core = lax.rem(me, 2)
    my_x = lax.rem(me // 2, nx)
    my_y = me // (2 * nx)

    def index(y, x, c):
        return (y * nx + x) * 2 + c

    def x_peer(delta):
        return index(my_y, lax.rem(my_x + delta, nx), core), place

    def y_peer(delta):
        return index(lax.rem(my_y + delta, ny), my_x, core), place

    twin = (index(my_y, my_x, 1 - core), place)

    def owner(dy, dx, c):
        return index(lax.rem(my_y + ny - dy, ny), lax.rem(my_x + nx - dx, nx), c)

    def peer(delta):
        return lax.rem(me + delta, dp), place

    def line_peer(delta):
        return me, lax.rem(place + delta, seq)

    barrier = pltpu.get_barrier_semaphore()
    for delta in range(1, dp):
        pl.semaphore_signal(barrier, inc=1, device_id=peer(delta), device_id_type=mesh_type)
    for delta in range(1, seq):
        pl.semaphore_signal(barrier, inc=1, device_id=line_peer(delta), device_id_type=mesh_type)

    share = fc_in.shape[1] // dp
    cut = share // columns
    tensors = [(w_held, shard_in.shape[0]), (wo_held, wo_in.shape[0])]
    for j in range(columns):
        tensors += [(fc_held.at[j], fc_in.shape[0]), (proj_held.at[j], cut)]

    def region(t, device, half=None):
        target, size = tensors[t]
        if half is None:
            return target.at[pl.ds(pl.multiple_of(device * size, size), size), :]
        part = size // 2
        return target.at[pl.ds(pl.multiple_of(device * size + half * part, part), part), :]

    def flight(t, slot, part, device):
        return pltpu.make_async_remote_copy(
            src_ref=part, dst_ref=part, send_sem=send_sems.at[t, slot], recv_sem=recv_sems.at[t, slot],
            device_id=device, device_id_type=mesh_type,
        )

    flights = {}
    for t in range(len(tensors)):
        names = [("x", 0, dx) for dx in range(1, nx)] + [("y", dy, 0) for dy in range(1, ny)]
        names += [(kind, dy, dx) for kind in "ab" for dy in range(1, ny) for dx in range(1, nx)]
        names += [("t", dy, dx) for dy in range(ny) for dx in range(nx)]
        for slot, (kind, dy, dx) in enumerate(names):
            if kind == "x":
                part, device = region(t, me), x_peer(dx)
            elif kind == "y":
                part, device = region(t, me), y_peer(dy)
            elif kind == "a":
                part, device = region(t, owner(0, dx, core), 0), y_peer(dy)
            elif kind == "b":
                part, device = region(t, owner(dy, 0, core), 1), x_peer(dx)
            else:
                part, device = region(t, owner(dy, dx, core)), twin
            flights[t, kind, dy, dx] = flight(t, slot, part, device)

    def wave_one(t):
        for dx in range(1, nx):
            flights[t, "x", 0, dx].start()
        for dy in range(1, ny):
            flights[t, "y", dy, 0].start()
        flights[t, "t", 0, 0].start()

    def wave_two(t):
        for dx in range(1, nx):
            flights[t, "x", 0, dx].wait_recv()
            for dy in range(1, ny):
                flights[t, "a", dy, dx].start()
        for dy in range(1, ny):
            flights[t, "y", dy, 0].wait_recv()
            for dx in range(1, nx):
                flights[t, "b", dy, dx].start()
        for dx in range(1, nx):
            flights[t, "t", 0, dx].start()
        for dy in range(1, ny):
            flights[t, "t", dy, 0].start()

    def wave_three(t):
        for dy in range(1, ny):
            for dx in range(1, nx):
                flights[t, "a", dy, dx].wait_recv()
                flights[t, "b", dy, dx].wait_recv()
                flights[t, "t", dy, dx].start()

    def wave_end(t):
        for dy in range(ny):
            for dx in range(nx):
                flights[t, "t", dy, dx].wait_recv()

    def hop(row, s):
        return pltpu.make_async_remote_copy(
            src_ref=hidden.at[row, s - 1], dst_ref=hidden.at[row, s],
            send_sem=hop_send.at[row, s - 1], recv_sem=hop_recv.at[row, s - 1],
            device_id=(me, place + 1), device_id_type=mesh_type,
        )

    def hop_start(row, s):
        @pl.when((place >= s - 1) & (place < top))
        def _():
            hop(row, s).start()

    def arrive(row, s):
        @pl.when(place >= s)
        def _():
            hop(row, s).wait_recv()

        if s < seq - 1:
            hop_start(row, s + 1)
        if s == seq - 1 and row < rows - 1:
            hop_start(row + 1, 1)

    def first_norm(row):
        normed, _ = norm_parts(x_ref[row].astype(F32))
        hidden[row, 0] = (normed * gain1[...] + shift1[...]).astype(BF16)

    def gout_load(row):
        return pltpu.make_async_copy(gout_in.at[row], gout_held, load_sems.at[0])

    def mix_load(row):
        return pltpu.make_async_copy(mix_spill.at[row], mix_held, load_sems.at[1])

    own_copies = [
        pltpu.make_async_copy(source, region(t, me), own_sems.at[t, 0]) for t, source in enumerate((shard_in, wo_in))
    ]
    for j in range(columns):
        for d in range(dp):
            part = region(2 + 2 * j, me).at[:, d * cut : (d + 1) * cut]
            source = fc_in.at[:, d * share + j * cut : d * share + (j + 1) * cut]
            own_copies.append(pltpu.make_async_copy(source, part, own_sems.at[2 + 2 * j, d]))
        source = proj_in.at[j * cut : (j + 1) * cut, :]
        own_copies.append(pltpu.make_async_copy(source, region(3 + 2 * j, me), own_sems.at[3 + 2 * j, 0]))
    for copy in inputs[:5]:
        copy.start()
    own_copies[0].start()
    for copy in inputs[5:]:
        copy.start()
    for copy in inputs[:3]:
        copy.wait()
    first_norm(0)
    inputs[4].wait()
    dq_ref[:, :8] = small_ref[:8, :].astype(F32).T
    pl.semaphore_wait(barrier, dp + seq - 2)
    hop_start(0, 1)
    own_copies[0].wait()
    size = shard_in.shape[0]
    mine = pl.ds(pl.multiple_of(me * size, size), size)
    reduce_own = dq_ref[mine, :8].astype(BF16)
    up = small_ref[8:, :]
    low_rank = lax.broadcasted_iota(jnp.int32, up.shape, 0) < 4
    for column, rank_up in ((0, jnp.where(low_rank, up, jnp.zeros_like(up))), (2, jnp.where(low_rank, jnp.zeros_like(up), up))):
        span = slice(column * width, (column + 1) * width)
        change = dot_nn(reduce_own, rank_up) * ADAPTER_SCALE
        w_held[mine, span] = (w_held[mine, span].astype(F32) + change).astype(BF16)
    wave_one(0)
    for copy in own_copies[1:]:
        copy.start()
    gout_load(0).start()
    for copy in inputs[5:] + inputs[3:4] + own_copies[1:]:
        copy.wait()
    own_starts(seg_ref, begin_ref, place, seq)
    for row in range(1, rows):
        first_norm(row)
    for s in range(1, seq):
        @pl.when(place < s)
        def _():
            for row in range(rows):
                hidden[row, s] = jnp.zeros((tokens, width), BF16)
    for j in range(columns):
        for d in range(dp):
            bias_held[j, :1, d * cut : (d + 1) * cut] = fc_bias[:, d * share + j * cut : d * share + (j + 1) * cut]
    up_sum[...] = jnp.zeros_like(up_sum)
    reduce_sum[...] = jnp.zeros_like(reduce_sum)

    low = head_lanes(tokens, BF16)
    lane = lax.broadcasted_iota(jnp.int32, (tokens, PAIR), 1)
    rank_row = lax.broadcasted_iota(jnp.int32, (8, width), 0) < 4

    def both_heads(pair):
        none = jnp.zeros_like(pair)
        return jnp.concatenate([jnp.where(low, pair, none), jnp.where(low, none, pair)], axis=0)

    def spills(row):
        return [
            pltpu.make_async_copy(held, spill.at[row], spill_sems.at[i])
            for i, (held, spill) in enumerate(
                ((q_held, q_spill), (k_held, k_spill), (v_held, v_spill), (mix_row, mix_spill))
            )
        ]

    def reloads(row):
        return [
            pltpu.make_async_copy(spill.at[row], held, spill_sems.at[4 + i])
            for i, (held, spill) in enumerate(((q_held, q_spill), (k_held, k_spill), (v_held, v_spill)))
        ]

    def attend(row, middle):
        query = place * tokens + lax.broadcasted_iota(jnp.int32, (tokens, tokens), 0)
        start = begin_ref[row].T[:, :1].astype(jnp.int32)
        for s in range(seq):
            key = (place - s) * tokens + lax.broadcasted_iota(jnp.int32, (tokens, tokens), 1)
            span = slice(s * tokens, (s + 1) * tokens)
            mask_ref[:, span] = jnp.where((key >= start) & (key <= query), 0.0, MASKED)
            down_ref[row, :, span] = (dot_nt(small_ref[:8, :], hidden[row, s]) * ADAPTER_SCALE).astype(BF16)

        for quad in range(quads):
            own = slice(quad * QUAD, (quad + 1) * QUAD)
            key_span = slice(width + quad * QUAD, width + (quad + 1) * QUAD)
            value_span = slice(2 * width + quad * QUAD, 2 * width + (quad + 1) * QUAD)
            q = dot_nn(hidden[row, 0], w_held[:, own]) + bias_q[:, own]
            q_held[:, own] = (q.astype(BF16) * (HEAD**-0.5)).astype(BF16)
            for s in range(seq):
                span = slice(s * tokens, (s + 1) * tokens)
                k_held[span, own] = dot_nn(hidden[row, s], w_held[:, key_span]).astype(BF16)
                v_held[span, own] = (dot_nn(hidden[row, s], w_held[:, value_span]) + bias_v[:, own]).astype(BF16)
            totals = jnp.zeros((tokens, PAIR), F32)
            for pair in range(QUAD // PAIR):
                span = slice(quad * QUAD + pair * PAIR, quad * QUAD + (pair + 1) * PAIR)
                score = dot_nt(both_heads(q_held[:, span]), k_held[:, span])
                score = jnp.concatenate([score[:tokens] + mask_ref[...], score[tokens:] + mask_ref[...]], axis=0)
                highest = jnp.max(score, axis=-1, keepdims=True)
                weight = jnp.exp(score - highest)
                total = jnp.sum(weight, axis=-1, keepdims=True)
                mixed = dot_nn(weight.astype(BF16), v_held[:, span]) * (1.0 / total)
                mix_row[:, span] = jnp.where(low, mixed[:tokens], mixed[tokens:]).astype(BF16)
                lse = highest + jnp.log(total)
                totals = jnp.where(lane == 2 * pair, lse[:tokens], totals)
                totals = jnp.where(lane == 2 * pair + 1, lse[tokens:], totals)
            lse_ref[row, quad] = totals.T[:8]
            if 2 * (quad + 1) == quads:
                middle()

    def out_store(row):
        return pltpu.make_async_copy(h2_ref, out_out.at[row], store_sems.at[0])

    def grad_store(row):
        slot = lax.rem(row, 2)
        return pltpu.make_async_copy(gmid_ref.at[slot], grad_out.at[row], store_sems.at[1 + slot])

    def leave(row, s):
        return pltpu.make_async_remote_copy(
            src_ref=leaving.at[s - 1], dst_ref=arriving.at[row, s - 1],
            send_sem=leave_sems.at[s - 1], recv_sem=arrive_sems.at[row, s - 1],
            device_id=(me, place - 1), device_id_type=mesh_type,
        )

    def chain(row, s):
        @pl.when((place < top) & (place >= s))
        def _():
            leave(row, s + 1).wait_recv()
            leaving[s - 1] = (leaving[s - 1].astype(F32) + arriving[row, s].astype(F32)).astype(BF16)
            leave(row, s).start()

    def chain_end(row):
        @pl.when(place < top)
        def _():
            leave(row, 1).wait_recv()
            own_ref[...] += arriving[row, 0].astype(F32)

        slot = lax.rem(row, 2)
        normed, inverse = norm_parts(x_ref[row].astype(F32))
        gmid_ref[slot] = gmid_ref[slot] + norm_backward(own_ref[...], normed, inverse, gain1[...])
        grad_store(row).start()

    def feed_begin(row):
        gout_load(row).wait()
        mix_load(row).wait()

        @pl.when(row >= 1)
        def _():
            out_store(row - 1).wait()
            for copy in reloads(row):
                copy.start()

        @pl.when(row >= 2)
        def _():
            grad_store(row - 2).wait()

        middle = x_ref[row].astype(F32) + dot_nn(mix_held[...], wo_held[...]) + out_bias[...]
        gmid_ref[lax.rem(row, 2)] = middle
        normed, _ = norm_parts(middle)
        h2_ref[...] = (normed * gain2[...] + shift2[...]).astype(BF16)
        acc_ref[...] = jnp.zeros_like(acc_ref)
        back_ref[...] = jnp.zeros_like(back_ref)

    def feed_step(step):
        j = step // per_chunk
        part = pl.ds(pl.multiple_of(lax.rem(step, per_chunk) * block, block), block)
        before = dot_nn(h2_ref[...], fc_held[j, :, part]) + bias_held[j, :1, part]
        square = before * before
        bend = jnp.tanh(GELU_A * before * (1.0 + GELU_B * square))
        half = 0.5 * (1.0 + bend)
        slope = half + 0.5 * before * (1.0 - bend * bend) * (GELU_A * (1.0 + 3.0 * GELU_B * square))
        act = (before * half).astype(BF16)
        g_before = (dot_nt(gout_held[...], proj_held[j, part, :]) * slope).astype(BF16)
        acc_ref[...] += dot_nn(act, proj_held[j, part, :])
        back_ref[...] += dot_nt(g_before, fc_held[j, :, part])

    def feed_end(row):
        slot = lax.rem(row, 2)
        middle = gmid_ref[slot]
        h2_ref[...] = (middle + acc_ref[...] + proj_bias[...]).astype(BF16)
        out_store(row).start()
        normed, inverse = norm_parts(middle)
        g_middle = gout_held[...].astype(F32) + norm_backward(back_ref[...], normed, inverse, gain2[...])
        gmid_ref[slot] = g_middle
        gmix_ref[...] = dot_nt(g_middle.astype(BF16), wo_held[...]).astype(BF16)
        for pair in range(width // PAIR):
            span = slice(pair * PAIR, (pair + 1) * PAIR)
            product = (gmix_ref[:, span].astype(F32) * mix_held[:, span].astype(F32)).T
            for half in range(2):
                head = pair * 2 + half
                delta_ref[head // 4, head % 4 : head % 4 + 1, :] = jnp.sum(
                    product[half * HEAD : (half + 1) * HEAD], axis=0, keepdims=True
                )

        @pl.when(row < rows - 1)
        def _():
            gout_load(row + 1).start()
            mix_load(row + 1).start()

    def attend_chunk(row, s):
        query = place * tokens + lax.broadcasted_iota(jnp.int32, (tokens, tokens), 1)
        key = (place - s) * tokens + lax.broadcasted_iota(jnp.int32, (tokens, tokens), 0)
        start = begin_ref[row, :1, :].astype(jnp.int32)
        mask = jnp.where((key >= start) & (key <= query), 0.0, MASKED)
        mask_ref[:, :tokens] = mask
        mask_ref[:, tokens : 2 * tokens] = mask
        rows_s = pl.ds(pl.multiple_of(s * tokens, tokens), tokens)
        for pair in range(width // PAIR):
            span = slice(pair * PAIR, (pair + 1) * PAIR)
            k_pair, v_pair = k_held[rows_s, span], v_held[rows_s, span]
            q_both, g_both = both_heads(q_held[:, span]), both_heads(gmix_ref[:, span])
            head = 2 * (pair % 2)
            lse, inner = [
                jnp.concatenate([ref[head : head + 1, :], ref[head + 1 : head + 2, :]], axis=1)
                for ref in (lse_ref.at[row, pair // 2], delta_ref.at[pair // 2])
            ]
            prob = jnp.exp(dot_nt(k_pair, q_both) + mask_ref[:, : 2 * tokens] - lse)
            g_score = (prob * (dot_nt(v_pair, g_both) - inner)).astype(BF16)
            dkv_ref[:, span] = dot_nn(g_score, q_both).astype(BF16)
            dkv_ref[:, width + pair * PAIR : width + (pair + 1) * PAIR] = dot_nn(prob.astype(BF16), g_both).astype(BF16)
            k_turned = k_pair.astype(F32).T.astype(BF16)
            for half in range(2):
                lines = slice(pair * PAIR + half * HEAD, pair * PAIR + (half + 1) * HEAD)
                part = g_score[:, half * tokens : (half + 1) * tokens]
                dq_ref[lines, :] += dot_nn(k_turned[half * HEAD : (half + 1) * HEAD], part)

        grad = dot_nt(dkv_ref[...], w_held[:, width:])
        dv = dkv_ref[:, width:]
        up_grad = dot_nn(down_ref[row, :, rows_s], dv)
        g_down = dot_nt(small_ref[8:, :], dv).astype(BF16)
        reduce_grad = dot_nn(g_down, hidden[row, s])
        up_sum[...] += jnp.where(rank_row, 0.0, up_grad)
        reduce_sum[...] += jnp.where(rank_row, 0.0, reduce_grad)
        if not isinstance(s, int):
            @pl.when(row > 0)
            def _():
                leave(row - 1, s).wait_send()

            leaving[s - 1] = grad.astype(BF16)

            @pl.when(place == top)
            def _():
                leave(row, s).start()
        else:
            dq = (dq_ref[...].T * (HEAD**-0.5)).astype(BF16)
            own_ref[...] = grad + dot_nt(dq, w_held[:, :width])
            up_grad = dot_nn(down_ref[row, :, rows_s], dq)
            g_down = dot_nt(small_ref[8:, :], dq).astype(BF16)
            reduce_grad = dot_nn(g_down, hidden[row, s])
            up_sum[...] += jnp.where(rank_row, up_grad, 0.0)
            reduce_sum[...] += jnp.where(rank_row, reduce_grad, 0.0)

    def backward(row):
        feed_end(row)

        @pl.when(row > 0)
        def _():
            chain(row - 1, seq - 3)

        for copy in reloads(row):
            copy.wait()
        dq_ref[...] = jnp.zeros_like(dq_ref)

        @pl.loop(0, seq - 1)
        def _(step):
            s = seq - 1 - step

            @pl.when((row > 0) & (s < seq - 3))
            def _():
                chain(row - 1, s)

            @pl.when(place >= s)
            def _():
                attend_chunk(row, s)

        chain(row, seq - 2)

        @pl.when(row > 0)
        def _():
            chain_end(row - 1)

        attend_chunk(row, 0)

    def both(action, j):
        if j < columns:
            action(2 + 2 * j)
            action(3 + 2 * j)

    def before_first():
        arrive(0, 1)
        wave_two(0)
        wave_one(1)
        for s in range(2, seq):
            if s == seq - 1:
                wave_three(0)
                both(wave_one, 0)
                wave_two(1)
            arrive(0, s)
        wave_end(0)
        both(wave_one, 1)

    def before_second():
        both(wave_two, 0)
        both(wave_one, 2)
        for s in range(1, seq):
            if s == seq - 1:
                both(wave_two, 1)
                wave_three(1)
                both(wave_three, 0)
            arrive(1, s)
        both(wave_one, 3)

    def amid_second():
        both(wave_two, 2)
        both(wave_three, 1)

    def before_third():
        arrive(2, 1)
        wave_end(1)
        both(wave_two, 3)

    def amid_early(step):
        for j in range(columns - 1):
            @pl.when(step == j * per_chunk)
            def _():
                if j == 1:
                    for s in range(2, seq - 1):
                        arrive(2, s)
                if j >= 2:
                    both(wave_three, j)
                both(wave_end, j)

    def after_early():
        for s in range(2, seq):
            if columns < 3 or s == seq - 1:
                arrive(2, s)

    def amid_third():
        if columns > 2:
            both(wave_three, columns - 1)

    def before_later(row):
        for s in range(1, seq):
            arrive(row, s)

    last = rows - 1

    @pl.loop(0, 2 * rows)
    def _(turn):
        row = jnp.maximum(turn - rows, 0)
        for index in range(rows):
            befores = (before_first, before_second, before_third)
            pl.when(turn == index)(befores[index] if index < 3 else partial(before_later, index))

        @pl.when((turn > 0) & (turn <= rows))
        def _():
            for copy in spills(turn - 1):
                copy.wait()

        @pl.when(turn == 1)
        def _():
            mix_load(0).start()

        @pl.when(turn == rows)
        def _():
            for copy in reloads(0):
                copy.start()
            both(wave_end, columns - 1)

        pl.when((turn == last) | (turn > rows))(partial(feed_begin, row))

        @pl.when(turn >= last)
        def _():
            @pl.loop(jnp.where(turn == rows, early, 0), jnp.where(turn == last, early, steps))
            def _(step):
                pl.when(turn == last)(partial(amid_early, step))
                feed_step(step)

        pl.when(turn == 2)(after_early)

        def middle():
            pl.when(turn == 1)(amid_second)
            pl.when(turn == 2)(amid_third)

        @pl.when(turn < rows)
        def _():
            attend(turn, middle)
            for copy in spills(turn):
                copy.start()

        pl.when(turn >= rows)(partial(backward, row))

    def send(source, target, slot, device):
        copy = pltpu.make_async_remote_copy(
            src_ref=source, dst_ref=target, send_sem=sum_send.at[slot], recv_sem=sum_recv.at[slot],
            device_id=device, device_id_type=mesh_type,
        )
        copy.start()
        return copy

    piece = part_ref.shape[1]
    lanes = width // PAIR
    part_ref[...] = jnp.zeros_like(part_ref)
    for half, total in enumerate((reduce_sum[...] * ADAPTER_SCALE, up_sum[...])):
        for block_lane in range(lanes):
            line = (half * lanes + block_lane) * 8
            part_ref[line // piece, line % piece : line % piece + 8, :] = total[:, block_lane * PAIR : (block_lane + 1) * PAIR]
    copies = [send(part_ref.at[lax.rem(me + delta, dp)], plane_ref.at[delta], delta, peer(delta)) for delta in range(1, dp)]
    chain(last, seq - 3)
    total = part_ref[me]
    for delta in range(1, dp):
        copies[delta - 1].wait()
        total = total + plane_ref[delta]
    line_ref[place] = total
    copies = [send(line_ref.at[place], line_ref.at[place], dp + delta, line_peer(delta)) for delta in range(1, seq)]
    for copy in copies:
        copy.wait()
    total = line_ref[0]
    for other in range(1, seq):
        total = total + line_ref[other]
    sum_out[me] = total
    copies = [send(sum_out.at[me], sum_out.at[me], dp + seq + delta, peer(delta)) for delta in range(1, dp)]
    for s in range(seq - 4, 0, -1):
        chain(last, s)
    chain_end(last)
    for copy in copies:
        copy.wait()
    for copy in flights.values():
        copy.wait_send()
    for row in range(rows):
        for s in range(1, seq):
            @pl.when((place >= s - 1) & (place < top))
            def _():
                hop(row, s).wait_send()
    for s in range(1, seq):
        @pl.when(place >= s)
        def _():
            leave(last, s).wait_send()
    out_store(last).wait()
    for row in range(max(0, rows - 2), rows):
        grad_store(row).wait()


def run_block(plane, seq, x, seg, small, vectors, shards, gout):
    rows, tokens, width = x.shape
    length = seq * tokens
    dp = plane[0] * plane[1] * 2
    hidden_units = shards[2].shape[1]
    block = 1024
    quads = width // QUAD
    piece = max(8, 16 * width // (PAIR * dp))
    nx, ny = plane
    columns = max(1, min(4, hidden_units // (dp * PAIR)))
    flights = nx - 1 + ny - 1 + 2 * (nx - 1) * (ny - 1) + nx * ny
    sums = 2 * dp + seq
    anywhere = pl.BlockSpec(memory_space=pl.ANY)
    vmem = pl.BlockSpec(memory_space=pltpu.VMEM)
    dma = pltpu.SemaphoreType.DMA

    def held(*dims, dtype=BF16):
        return pltpu.VMEM(dims, dtype)

    def shape(*dims, dtype=BF16):
        return jax.ShapeDtypeStruct(dims, dtype)

    result = pl.pallas_call(
        partial(block_kernel, plane, seq, rows, block),
        in_specs=[anywhere] * 17,
        out_specs=[anywhere, anywhere, vmem] + [anywhere] * 4,
        out_shape=[
            shape(rows, tokens, width), shape(rows, tokens, width, dtype=F32), shape(dp, piece, PAIR, dtype=F32),
            shape(rows, tokens, width), shape(rows, length, width), shape(rows, length, width),
            shape(rows, tokens, width),
        ],
        scratch_shapes=[
            *(held(*a.shape, dtype=a.dtype) for a in (x, seg, small, *vectors)), dma((12,)),
            held(width, 3 * width), held(width, width), held(columns, width, hidden_units // columns), held(columns, hidden_units // columns, width),
            held(rows, seq, tokens, width), held(tokens, width), held(length, width), held(length, width),
            held(tokens, width), held(tokens, width), held(tokens, width),
            held(tokens, width), held(tokens, width),
            held(tokens, width, dtype=F32), held(tokens, width, dtype=F32), held(2, tokens, width, dtype=F32),
            held(tokens, width, dtype=F32), held(tokens, length, dtype=F32), held(quads, 8, tokens, dtype=F32),
            held(width, tokens, dtype=F32), held(tokens, 2 * width),
            held(seq - 1, tokens, width), held(rows, seq - 1, tokens, width),
            held(rows, 8, tokens, dtype=F32), held(columns, 8, hidden_units // columns, dtype=F32),
            held(rows, quads, 8, tokens, dtype=F32), held(rows, 8, length),
            held(8, width, dtype=F32), held(8, width, dtype=F32),
            held(dp, piece, PAIR, dtype=F32), held(dp, piece, PAIR, dtype=F32), held(seq, piece, PAIR, dtype=F32),
            dma((2 + 2 * columns, flights)), dma((2 + 2 * columns, flights)), dma((rows, seq - 1)), dma((rows, seq - 1)),
            dma((2 + 2 * columns, dp)), dma((7,)), dma((2,)), dma((3,)),
            dma((seq - 1,)), dma((rows, seq - 1)), dma((sums,)), dma((sums,)),
        ],
        compiler_params=pltpu.CompilerParams(
            vmem_limit_bytes=VMEM_BYTES, collective_id=0, has_side_effects=True
        ),
        name="block",
    )(x, seg, small, *vectors, *shards, gout)
    out, grad, total = result[:3]
    flat = total.reshape(-1, PAIR)[: 16 * width // PAIR]
    return out, grad, flat.reshape(2, width // PAIR, 8, PAIR).transpose(0, 2, 1, 3).reshape(2, 8, width)


def on_device(
    dp,
    seq,
    block_input,
    seg_start,
    ln1_gain,
    ln1_bias,
    qkv_weight,
    query_bias,
    value_bias,
    query_adapter_reduce,
    query_up,
    value_adapter_reduce,
    value_up,
    out_weight,
    out_bias,
    ln2_gain,
    ln2_bias,
    fc_weight,
    fc_bias,
    proj_weight,
    proj_bias,
    grad_out,
):
    rows, tokens, width = block_input.shape
    rank = query_up.shape[0]
    side = math.isqrt(dp // 2)
    small = jnp.concatenate([query_adapter_reduce.T, value_adapter_reduce.T, query_up, value_up], axis=0)

    def as_row(vector):
        return vector.reshape(1, -1)

    vectors = tuple(
        as_row(a)
        for a in (ln1_gain, ln1_bias, query_bias, value_bias, out_bias, ln2_gain, ln2_bias, proj_bias, fc_bias)
    )
    out, grad, sums = run_block(
        (side, dp // (2 * side)), seq, block_input, seg_start, small, vectors,
        (qkv_weight, out_weight, fc_weight, proj_weight), grad_out,
    )
    reduce, up = sums[0], sums[1]
    return out, grad, reduce[:rank].T, up[:rank], reduce[rank : 2 * rank].T, up[rank : 2 * rank]


def solution(mesh):
    return jax.shard_map(
        partial(on_device, mesh.shape["dp"], mesh.shape["seq"]),
        mesh=mesh,
        in_specs=(
            P("dp", "seq", None),
            P("dp", None),
            P(),
            P(),
            P("dp", None),
            P(),
            P(),
            P(),
            P(),
            P(),
            P(),
            P("dp", None),
            P(),
            P(),
            P(),
            P("dp", None),
            P(),
            P("dp", None),
            P(),
            P("dp", "seq", None),
        ),
        out_specs=(P("dp", "seq", None), P("dp", "seq", None), P(), P(), P(), P()),
        check_vma=False,
    )
```

```python
import math
from functools import partial

import jax
import jax.numpy as jnp
from jax import lax
from jax.experimental import pallas as pl
from jax.experimental.pallas import tpu as pltpu
from jax.sharding import PartitionSpec as P

HEAD = 64
QUAD = 256
PAIR = 128
NORM_EPSILON = 1e-05
ADAPTER_SCALE = 8.0
MASKED = -1e30
GELU_A = 0.7978845608028654
GELU_B = 0.044715

F32 = jnp.float32
BF16 = jnp.bfloat16
VMEM_BYTES = 65400 * 1024


def dot_nn(left, right):
    return lax.dot_general(left, right, (((1,), (0,)), ((), ())), preferred_element_type=F32)


def dot_nt(left, right):
    return lax.dot_general(left, right, (((1,), (1,)), ((), ())), preferred_element_type=F32)


def norm_parts(values):
    average = jnp.mean(values, axis=-1, keepdims=True)
    centered = values - average
    inverse = lax.rsqrt(jnp.mean(centered * centered, axis=-1, keepdims=True) + NORM_EPSILON)
    return centered * inverse, inverse


def norm_backward(gradient, normed, inverse, gain):
    scaled = gradient * gain
    return inverse * (
        scaled
        - jnp.mean(scaled, axis=-1, keepdims=True)
        - normed * jnp.mean(scaled * normed, axis=-1, keepdims=True)
    )


def head_lanes(rows, dtype):
    lane = lax.broadcasted_iota(jnp.int32, (rows, PAIR), 1)
    return lane < HEAD


def own_starts(seg_ref, begin_ref, place, seq):
    rows, _, tokens = begin_ref.shape
    own = jnp.zeros((rows, tokens), jnp.int32)
    for index in range(seq):
        own = jnp.where(place == index, seg_ref[:, index * tokens : (index + 1) * tokens], own)
    own = own.astype(F32)
    for row in range(rows):
        begin_ref[row] = jnp.broadcast_to(own[row : row + 1], (8, tokens))


def block_kernel(
    plane, seq, rows, block,
    x_in, seg_in, small_in, gain1_in, shift1_in, bias_q_in, bias_v_in, out_bias_in, gain2_in, shift2_in, proj_bias_in,
    fc_bias_in, shard_in, wo_in, fc_in, proj_in, gout_in,
    out_out, grad_out, sum_out, q_spill, k_spill, v_spill, mix_spill, gmix_spill, dq_spill,
    x_ref, seg_ref, small_ref, gain1, shift1, bias_q, bias_v, out_bias, gain2, shift2, proj_bias, fc_bias, input_sems,
    w_held, wo_held, fc_held, proj_held, hidden, q_held, k_held, v_held, mix_row, mix_held, gout_held,
    gmix_ref, h2_ref, acc_ref, back_ref, gmid_ref, own_ref, mask_ref, delta_ref, dq_ref, dkv_ref,
    leaving, arriving, begin_ref, bias_held, lse_ref, down_ref, up_sum, reduce_sum,
    part_ref, plane_ref, line_ref,
    send_sems, recv_sems, hop_send, hop_recv, own_sems, spill_sems, load_sems, late_sems, store_sems,
    leave_sems, arrive_sems, sum_send, sum_recv,
):
    nx, ny = plane
    dp = nx * ny * 2
    inputs = [
        pltpu.make_async_copy(source, target, input_sems.at[i])
        for i, (source, target) in enumerate(
            (
                (x_in, x_ref), (gain1_in, gain1), (shift1_in, shift1), (seg_in, seg_ref), (small_in, small_ref),
                (bias_q_in, bias_q), (bias_v_in, bias_v), (out_bias_in, out_bias), (gain2_in, gain2),
                (shift2_in, shift2), (proj_bias_in, proj_bias), (fc_bias_in, fc_bias),
            )
        )
    ]
    tokens, width = x_ref.shape[1], x_ref.shape[2]
    quads = width // QUAD
    columns, chunk_units = fc_held.shape[0], fc_held.shape[2]
    per_chunk = chunk_units // block
    steps = columns * per_chunk
    last = rows - 1
    late_slot = 1 - last % 2
    top = seq - 1
    mesh_type = pl.DeviceIdType.MESH
    me, place = lax.axis_index("dp"), lax.axis_index("seq")
    core = lax.rem(me, 2)
    my_x = lax.rem(me // 2, nx)
    my_y = me // (2 * nx)

    def index(y, x, c):
        return (y * nx + x) * 2 + c

    def x_peer(delta):
        return index(my_y, lax.rem(my_x + delta, nx), core), place

    def y_peer(delta):
        return index(lax.rem(my_y + delta, ny), my_x, core), place

    twin = (index(my_y, my_x, 1 - core), place)

    def owner(dy, dx, c):
        return index(lax.rem(my_y + ny - dy, ny), lax.rem(my_x + nx - dx, nx), c)

    def peer(delta):
        return lax.rem(me + delta, dp), place

    def line_peer(delta):
        return me, lax.rem(place + delta, seq)

    barrier = pltpu.get_barrier_semaphore()
    for delta in range(1, dp):
        pl.semaphore_signal(barrier, inc=1, device_id=peer(delta), device_id_type=mesh_type)
    for delta in range(1, seq):
        pl.semaphore_signal(barrier, inc=1, device_id=line_peer(delta), device_id_type=mesh_type)

    share = fc_in.shape[1] // dp
    cut = share // columns
    tensors = [(w_held, shard_in.shape[0]), (wo_held, wo_in.shape[0])]
    for j in range(columns):
        tensors += [(fc_held.at[j], fc_in.shape[0]), (proj_held.at[j], cut)]

    def region(t, device, half=None):
        target, size = tensors[t]
        if half is None:
            return target.at[pl.ds(pl.multiple_of(device * size, size), size), :]
        part = size // 2
        return target.at[pl.ds(pl.multiple_of(device * size + half * part, part), part), :]

    def flight(t, slot, part, device):
        return pltpu.make_async_remote_copy(
            src_ref=part, dst_ref=part, send_sem=send_sems.at[t, slot], recv_sem=recv_sems.at[t, slot],
            device_id=device, device_id_type=mesh_type,
        )

    flights = {}
    for t in range(len(tensors)):
        names = [("x", 0, dx) for dx in range(1, nx)] + [("y", dy, 0) for dy in range(1, ny)]
        names += [(kind, dy, dx) for kind in "ab" for dy in range(1, ny) for dx in range(1, nx)]
        names += [("t", dy, dx) for dy in range(ny) for dx in range(nx)]
        for slot, (kind, dy, dx) in enumerate(names):
            if kind == "x":
                part, device = region(t, me), x_peer(dx)
            elif kind == "y":
                part, device = region(t, me), y_peer(dy)
            elif kind == "a":
                part, device = region(t, owner(0, dx, core), 0), y_peer(dy)
            elif kind == "b":
                part, device = region(t, owner(dy, 0, core), 1), x_peer(dx)
            else:
                part, device = region(t, owner(dy, dx, core)), twin
            flights[t, kind, dy, dx] = flight(t, slot, part, device)

    def wave_one(t):
        for dx in range(1, nx):
            flights[t, "x", 0, dx].start()
        for dy in range(1, ny):
            flights[t, "y", dy, 0].start()
        flights[t, "t", 0, 0].start()

    def wave_two(t):
        for dx in range(1, nx):
            flights[t, "x", 0, dx].wait_recv()
            for dy in range(1, ny):
                flights[t, "a", dy, dx].start()
        for dy in range(1, ny):
            flights[t, "y", dy, 0].wait_recv()
            for dx in range(1, nx):
                flights[t, "b", dy, dx].start()
        for dx in range(1, nx):
            flights[t, "t", 0, dx].start()
        for dy in range(1, ny):
            flights[t, "t", dy, 0].start()

    def wave_three(t):
        for dy in range(1, ny):
            for dx in range(1, nx):
                flights[t, "a", dy, dx].wait_recv()
                flights[t, "b", dy, dx].wait_recv()
                flights[t, "t", dy, dx].start()

    def wave_end(t):
        for dy in range(ny):
            for dx in range(nx):
                flights[t, "t", dy, dx].wait_recv()

    def hop(row, s):
        return pltpu.make_async_remote_copy(
            src_ref=hidden.at[row, s - 1], dst_ref=hidden.at[row, s],
            send_sem=hop_send.at[row, s - 1], recv_sem=hop_recv.at[row, s - 1],
            device_id=(me, place + 1), device_id_type=mesh_type,
        )

    def hop_start(row, s):
        @pl.when((place >= s - 1) & (place < top))
        def _():
            hop(row, s).start()

    def arrive(row, s):
        @pl.when(place >= s)
        def _():
            hop(row, s).wait_recv()

        if s < seq - 1:
            hop_start(row, s + 1)
        if s == seq - 1 and row < rows - 1:
            hop_start(row + 1, 1)

    def first_norm(row):
        normed, _ = norm_parts(x_ref[row].astype(F32))
        hidden[row, 0] = (normed * gain1[...] + shift1[...]).astype(BF16)

    def gout_load(row):
        return pltpu.make_async_copy(gout_in.at[row], gout_held, load_sems.at[0])

    def mix_load(row):
        return pltpu.make_async_copy(mix_spill.at[row], mix_held, load_sems.at[1])

    own_copies = [
        pltpu.make_async_copy(source, region(t, me), own_sems.at[t, 0]) for t, source in enumerate((shard_in, wo_in))
    ]
    for j in range(columns):
        for d in range(dp):
            part = region(2 + 2 * j, me).at[:, d * cut : (d + 1) * cut]
            source = fc_in.at[:, d * share + j * cut : d * share + (j + 1) * cut]
            own_copies.append(pltpu.make_async_copy(source, part, own_sems.at[2 + 2 * j, d]))
        source = proj_in.at[j * cut : (j + 1) * cut, :]
        own_copies.append(pltpu.make_async_copy(source, region(3 + 2 * j, me), own_sems.at[3 + 2 * j, 0]))
    for copy in inputs[:5]:
        copy.start()
    own_copies[0].start()
    for copy in inputs[5:]:
        copy.start()
    for copy in inputs[:3]:
        copy.wait()
    first_norm(0)
    inputs[4].wait()
    dq_ref[:, :8] = small_ref[:8, :].astype(F32).T
    pl.semaphore_wait(barrier, dp + seq - 2)
    hop_start(0, 1)
    own_copies[0].wait()
    size = shard_in.shape[0]
    mine = pl.ds(pl.multiple_of(me * size, size), size)
    reduce_own = dq_ref[mine, :8].astype(BF16)
    up = small_ref[8:, :]
    low_rank = lax.broadcasted_iota(jnp.int32, up.shape, 0) < 4
    for column, rank_up in ((0, jnp.where(low_rank, up, jnp.zeros_like(up))), (2, jnp.where(low_rank, jnp.zeros_like(up), up))):
        span = slice(column * width, (column + 1) * width)
        change = dot_nn(reduce_own, rank_up) * ADAPTER_SCALE
        w_held[mine, span] = (w_held[mine, span].astype(F32) + change).astype(BF16)
    wave_one(0)
    for copy in own_copies[1:]:
        copy.start()
    gout_load(0).start()
    for copy in inputs[5:] + inputs[3:4] + own_copies[1:]:
        copy.wait()
    own_starts(seg_ref, begin_ref, place, seq)
    for row in range(1, rows):
        first_norm(row)
    for s in range(1, seq):
        @pl.when(place < s)
        def _():
            for row in range(rows):
                hidden[row, s] = jnp.zeros((tokens, width), BF16)
    for j in range(columns):
        for d in range(dp):
            bias_held[j, :1, d * cut : (d + 1) * cut] = fc_bias[:, d * share + j * cut : d * share + (j + 1) * cut]
    up_sum[...] = jnp.zeros_like(up_sum)
    reduce_sum[...] = jnp.zeros_like(reduce_sum)

    low = head_lanes(tokens, BF16)
    lane = lax.broadcasted_iota(jnp.int32, (tokens, PAIR), 1)
    rank_row = lax.broadcasted_iota(jnp.int32, (8, width), 0) < 4

    def both_heads(pair):
        none = jnp.zeros_like(pair)
        return jnp.concatenate([jnp.where(low, pair, none), jnp.where(low, none, pair)], axis=0)

    def spills(row):
        return [
            pltpu.make_async_copy(held, spill.at[row], spill_sems.at[i])
            for i, (held, spill) in enumerate(
                ((q_held, q_spill), (k_held, k_spill), (v_held, v_spill), (mix_row, mix_spill))
            )
        ]

    def reloads(row):
        return [
            pltpu.make_async_copy(spill.at[row], held, spill_sems.at[4 + i])
            for i, (held, spill) in enumerate(((q_held, q_spill), (k_held, k_spill), (v_held, v_spill)))
        ]

    def attend(row, middle):
        query = place * tokens + lax.broadcasted_iota(jnp.int32, (tokens, tokens), 0)
        start = begin_ref[row].T[:, :1].astype(jnp.int32)
        for s in range(seq):
            key = (place - s) * tokens + lax.broadcasted_iota(jnp.int32, (tokens, tokens), 1)
            span = slice(s * tokens, (s + 1) * tokens)
            mask_ref[:, span] = jnp.where((key >= start) & (key <= query), 0.0, MASKED)
            down_ref[row, :, span] = (dot_nt(small_ref[:8, :], hidden[row, s]) * ADAPTER_SCALE).astype(BF16)

        for quad in range(quads):
            own = slice(quad * QUAD, (quad + 1) * QUAD)
            key_span = slice(width + quad * QUAD, width + (quad + 1) * QUAD)
            value_span = slice(2 * width + quad * QUAD, 2 * width + (quad + 1) * QUAD)
            q = dot_nn(hidden[row, 0], w_held[:, own]) + bias_q[:, own]
            q_held[:, own] = (q.astype(BF16) * (HEAD**-0.5)).astype(BF16)
            for s in range(seq):
                span = slice(s * tokens, (s + 1) * tokens)
                k_held[span, own] = dot_nn(hidden[row, s], w_held[:, key_span]).astype(BF16)
                v_held[span, own] = (dot_nn(hidden[row, s], w_held[:, value_span]) + bias_v[:, own]).astype(BF16)
            totals = jnp.zeros((tokens, PAIR), F32)
            for pair in range(QUAD // PAIR):
                span = slice(quad * QUAD + pair * PAIR, quad * QUAD + (pair + 1) * PAIR)
                score = dot_nt(both_heads(q_held[:, span]), k_held[:, span])
                score = jnp.concatenate([score[:tokens] + mask_ref[...], score[tokens:] + mask_ref[...]], axis=0)
                highest = jnp.max(score, axis=-1, keepdims=True)
                weight = jnp.exp(score - highest)
                total = jnp.sum(weight, axis=-1, keepdims=True)
                mixed = dot_nn(weight.astype(BF16), v_held[:, span]) * (1.0 / total)
                mix_row[:, span] = jnp.where(low, mixed[:tokens], mixed[tokens:]).astype(BF16)
                lse = highest + jnp.log(total)
                totals = jnp.where(lane == 2 * pair, lse[:tokens], totals)
                totals = jnp.where(lane == 2 * pair + 1, lse[tokens:], totals)
            lse_ref[row, quad] = totals.T[:8]
            if 2 * (quad + 1) == quads:
                middle()

    def out_store(row):
        return pltpu.make_async_copy(h2_ref, out_out.at[row], store_sems.at[0])

    def grad_store(row, slot):
        return pltpu.make_async_copy(gmid_ref.at[slot], grad_out.at[row], store_sems.at[1 + slot])

    def late_spills(row):
        return [
            pltpu.make_async_copy(gmix_ref, gmix_spill.at[row], late_sems.at[0]),
            pltpu.make_async_copy(acc_ref, dq_spill.at[row], late_sems.at[1]),
        ]

    def late_loads(row):
        q_room, gmix_room = ((mix_row, mix_held), (gout_held, h2_ref))[row]
        lines = slice((2 + row) * tokens, (3 + row) * tokens)
        return [
            pltpu.make_async_copy(gmix_spill.at[row], gmix_room, late_sems.at[2 + 4 * row]),
            pltpu.make_async_copy(q_spill.at[row], q_room, late_sems.at[3 + 4 * row]),
            pltpu.make_async_copy(k_spill.at[row, :tokens, :], k_held.at[lines, :], late_sems.at[4 + 4 * row]),
            pltpu.make_async_copy(v_spill.at[row, :tokens, :], v_held.at[lines, :], late_sems.at[5 + 4 * row]),
        ]

    def dq_load(row):
        return pltpu.make_async_copy(dq_spill.at[row], acc_ref, late_sems.at[10])

    def gmid_load(row):
        return pltpu.make_async_copy(grad_out.at[row], gmid_ref.at[late_slot], late_sems.at[11])

    def late_ready(row):
        for copy in late_loads(row):
            copy.wait()
        dq_load(row).wait()
        q_room, gmix_room = ((mix_row, mix_held), (gout_held, h2_ref))[row]
        lines = slice((2 + row) * tokens, (3 + row) * tokens)
        q_held[...] = q_room[...]
        gmix_ref[...] = gmix_room[...]
        k_held[:tokens, :] = k_held[lines, :]
        v_held[:tokens, :] = v_held[lines, :]
        dq_ref[...] = acc_ref[...].T

    def leave(row, s):
        return pltpu.make_async_remote_copy(
            src_ref=leaving.at[s - 1], dst_ref=arriving.at[row, s - 1],
            send_sem=leave_sems.at[s - 1], recv_sem=arrive_sems.at[row, s - 1],
            device_id=(me, place - 1), device_id_type=mesh_type,
        )

    def chain(row, s):
        @pl.when((place < top) & (place >= s))
        def _():
            leave(row, s + 1).wait_recv()
            leaving[s - 1] = (leaving[s - 1].astype(F32) + arriving[row, s].astype(F32)).astype(BF16)
            leave(row, s).start()

    def chain_end(row, slot, own):
        @pl.when(place < top)
        def _():
            leave(row, 1).wait_recv()
            own[...] += arriving[row, 0].astype(F32)

        normed, inverse = norm_parts(x_ref[row].astype(F32))
        gmid_ref[slot] = gmid_ref[slot] + norm_backward(own[...], normed, inverse, gain1[...])
        grad_store(row, slot).start()

    def feed_begin(row):
        gout_load(row).wait()

        @pl.when(row < 2)
        def _():
            mix_load(row).wait()

        @pl.when(row >= 1)
        def _():
            out_store(row - 1).wait()

        @pl.when(row == 1)
        def _():
            for copy in reloads(row):
                copy.start()

        @pl.when(row >= 2)
        def _():
            grad_store(row - 2, lax.rem(row, 2)).wait()

        middle = x_ref[row].astype(F32) + dot_nn(mix_held[...], wo_held[...]) + out_bias[...]
        gmid_ref[lax.rem(row, 2)] = middle
        normed, _ = norm_parts(middle)
        h2_ref[...] = (normed * gain2[...] + shift2[...]).astype(BF16)

        @pl.when(row > 0)
        def _():
            late_spills(row - 1)[1].wait()

        acc_ref[...] = jnp.zeros_like(acc_ref)
        back_ref[...] = jnp.zeros_like(back_ref)

    def feed_step(step):
        j = step // per_chunk
        part = pl.ds(pl.multiple_of(lax.rem(step, per_chunk) * block, block), block)
        before = dot_nn(h2_ref[...], fc_held[j, :, part]) + bias_held[j, :1, part]
        square = before * before
        bend = jnp.tanh(GELU_A * before * (1.0 + GELU_B * square))
        half = 0.5 * (1.0 + bend)
        slope = half + 0.5 * before * (1.0 - bend * bend) * (GELU_A * (1.0 + 3.0 * GELU_B * square))
        act = (before * half).astype(BF16)
        g_before = (dot_nt(gout_held[...], proj_held[j, part, :]) * slope).astype(BF16)
        acc_ref[...] += dot_nn(act, proj_held[j, part, :])
        back_ref[...] += dot_nt(g_before, fc_held[j, :, part])

    def feed_end(row):
        slot = lax.rem(row, 2)
        middle = gmid_ref[slot]
        h2_ref[...] = (middle + acc_ref[...] + proj_bias[...]).astype(BF16)
        out_store(row).start()
        normed, inverse = norm_parts(middle)
        g_middle = gout_held[...].astype(F32) + norm_backward(back_ref[...], normed, inverse, gain2[...])
        gmid_ref[slot] = g_middle

        @pl.when(row < last)
        def _():
            grad_store(row, slot).start()

        @pl.when(row > 0)
        def _():
            late_spills(row - 1)[0].wait()

        gmix_ref[...] = dot_nt(g_middle.astype(BF16), wo_held[...]).astype(BF16)
        for pair in range(width // PAIR):
            span = slice(pair * PAIR, (pair + 1) * PAIR)
            product = (gmix_ref[:, span].astype(F32) * mix_held[:, span].astype(F32)).T
            for half in range(2):
                head = pair * 2 + half
                delta_ref[row, head // 4, head % 4 : head % 4 + 1, :] = jnp.sum(
                    product[half * HEAD : (half + 1) * HEAD], axis=0, keepdims=True
                )

        @pl.when(row < rows - 1)
        def _():
            gout_load(row + 1).start()

        @pl.when(row == 0)
        def _():
            mix_load(row + 1).start()

    def attend_chunk(row, s):
        query = place * tokens + lax.broadcasted_iota(jnp.int32, (tokens, tokens), 1)
        key = (place - s) * tokens + lax.broadcasted_iota(jnp.int32, (tokens, tokens), 0)
        start = begin_ref[row, :1, :].astype(jnp.int32)
        mask = jnp.where((key >= start) & (key <= query), 0.0, MASKED)
        mask_ref[:, :tokens] = mask
        mask_ref[:, tokens : 2 * tokens] = mask
        rows_s = pl.ds(pl.multiple_of(s * tokens, tokens), tokens)
        for pair in range(width // PAIR):
            span = slice(pair * PAIR, (pair + 1) * PAIR)
            k_pair, v_pair = k_held[rows_s, span], v_held[rows_s, span]
            q_both, g_both = both_heads(q_held[:, span]), both_heads(gmix_ref[:, span])
            head = 2 * (pair % 2)
            lse, inner = [
                jnp.concatenate([ref[head : head + 1, :], ref[head + 1 : head + 2, :]], axis=1)
                for ref in (lse_ref.at[row, pair // 2], delta_ref.at[row, pair // 2])
            ]
            prob = jnp.exp(dot_nt(k_pair, q_both) + mask_ref[:, : 2 * tokens] - lse)
            g_score = (prob * (dot_nt(v_pair, g_both) - inner)).astype(BF16)
            dkv_ref[:, span] = dot_nn(g_score, q_both).astype(BF16)
            dkv_ref[:, width + pair * PAIR : width + (pair + 1) * PAIR] = dot_nn(prob.astype(BF16), g_both).astype(BF16)
            k_turned = k_pair.astype(F32).T.astype(BF16)
            for half in range(2):
                lines = slice(pair * PAIR + half * HEAD, pair * PAIR + (half + 1) * HEAD)
                part = g_score[:, half * tokens : (half + 1) * tokens]
                dq_ref[lines, :] += dot_nn(k_turned[half * HEAD : (half + 1) * HEAD], part)

        grad = dot_nt(dkv_ref[...], w_held[:, width:])
        dv = dkv_ref[:, width:]
        up_grad = dot_nn(down_ref[row, :, rows_s], dv)
        g_down = dot_nt(small_ref[8:, :], dv).astype(BF16)
        reduce_grad = dot_nn(g_down, hidden[row, s])
        up_sum[...] += jnp.where(rank_row, 0.0, up_grad)
        reduce_sum[...] += jnp.where(rank_row, 0.0, reduce_grad)
        if not isinstance(s, int):
            @pl.when(row > 0)
            def _():
                leave(row - 1, s).wait_send()

            leaving[s - 1] = grad.astype(BF16)

            @pl.when(place == top)
            def _():
                leave(row, s).start()
        else:
            dq = (dq_ref[...].T * (HEAD**-0.5)).astype(BF16)
            own_ref[...] = grad + dot_nt(dq, w_held[:, :width])
            up_grad = dot_nn(down_ref[row, :, rows_s], dq)
            g_down = dot_nt(small_ref[8:, :], dq).astype(BF16)
            reduce_grad = dot_nn(g_down, hidden[row, s])
            up_sum[...] += jnp.where(rank_row, up_grad, 0.0)
            reduce_sum[...] += jnp.where(rank_row, reduce_grad, 0.0)

    def backward(row):
        feed_end(row)

        @pl.when(row > 0)
        def _():
            chain(row - 1, seq - 3)

        @pl.when(row < 2)
        def _():
            for copy in reloads(row):
                copy.wait()

        dq_ref[...] = jnp.zeros_like(dq_ref)

        @pl.loop(0, seq - 1)
        def _(step):
            s = seq - 1 - step

            @pl.when((row > 0) & (s < seq - 3))
            def _():
                chain(row - 1, s)

            @pl.when(place >= s)
            def _():
                attend_chunk(row, s)

        chain(row, seq - 2)

        @pl.when(row < last)
        def _():
            acc_ref[...] = dq_ref[...].T
            for copy in late_spills(row):
                copy.start()

    def both(action, j):
        if j < columns:
            action(2 + 2 * j)
            action(3 + 2 * j)

    def before_first():
        arrive(0, 1)
        wave_two(0)
        wave_one(1)
        for s in range(2, seq):
            if s == seq - 1:
                wave_three(0)
                both(wave_one, 0)
                wave_two(1)
            arrive(0, s)
        wave_end(0)
        both(wave_one, 1)

    def before_second():
        both(wave_two, 0)
        both(wave_one, 2)
        for s in range(1, seq):
            if s == seq - 1:
                both(wave_two, 1)
                wave_three(1)
                both(wave_three, 0)
            arrive(1, s)
        both(wave_one, 3)

    def amid_second():
        both(wave_two, 2)
        both(wave_three, 1)

    def before_feed():
        arrive(2, 1)
        wave_end(1)
        both(wave_two, 3)
        for copy in spills(1):
            copy.wait()
        for copy in reloads(0):
            copy.start()

    def amid_feed(step):
        for j in range(columns):
            @pl.when(step == j * per_chunk)
            def _():
                if j == min(1, columns - 1):
                    for s in range(2, seq - 1):
                        arrive(2, s)
                if j >= 2 or j == columns - 1:
                    both(wave_three, j)
                both(wave_end, j)

    def before_third():
        arrive(2, seq - 1)

    def before_later(row):
        for s in range(1, seq):
            arrive(row, s)

    @pl.loop(0, 2 * rows)
    def _(turn):
        attending = (turn < 2) | ((turn >= 4) & (lax.rem(turn, 2) == 0))
        attend_row = jnp.where(turn < 2, turn, turn // 2)
        row = jnp.where(turn < 4, jnp.maximum(turn - 2, 0), (turn - 1) // 2)
        for index in range(rows):
            befores = (before_first, before_second, before_third)
            action = befores[index] if index < 3 else partial(before_later, index)
            pl.when(turn == (index if index < 2 else 2 * index))(action)

        pl.when(turn == 2)(before_feed)

        @pl.when(turn == 1)
        def _():
            for copy in spills(0):
                copy.wait()
            mix_load(0).start()

        @pl.when(attending)
        def _():
            attend(attend_row, lambda: pl.when(turn == 1)(amid_second))

            @pl.when(turn < 2)
            def _():
                for copy in spills(turn):
                    copy.start()

            @pl.when(turn >= 2)
            def _():
                mix_held[...] = mix_row[...]

        @pl.when(jnp.logical_not(attending))
        def _():
            feed_begin(row)

            @pl.loop(0, steps)
            def _(step):
                pl.when(turn == 2)(partial(amid_feed, step))
                feed_step(step)

            backward(row)

    grad_store(last - 1, late_slot).wait()
    out_store(last).wait()
    for copy in [gmid_load(0), dq_load(0)] + late_loads(0) + late_loads(1):
        copy.start()

    @pl.loop(0, 3)
    def _(turn):
        @pl.when(turn == 1)
        def _():
            late_ready(0)
            dq_load(1).start()

        @pl.when(turn == 2)
        def _():
            late_ready(1)
            grad_store(0, late_slot).wait()
            gmid_load(1).start()

        attend_chunk(jnp.where(turn == 0, last, turn - 1), 0)

        @pl.when(turn == 0)
        def _():
            back_ref[...] = own_ref[...]

        @pl.when(turn > 0)
        def _():
            gmid_load(turn - 1).wait()
            chain_end(turn - 1, late_slot, own_ref)

        pl.when(turn == 1)(partial(chain, last, seq - 3))

    def send(source, target, slot, device):
        copy = pltpu.make_async_remote_copy(
            src_ref=source, dst_ref=target, send_sem=sum_send.at[slot], recv_sem=sum_recv.at[slot],
            device_id=device, device_id_type=mesh_type,
        )
        copy.start()
        return copy

    piece = part_ref.shape[1]
    lanes = width // PAIR
    part_ref[...] = jnp.zeros_like(part_ref)
    for half, total in enumerate((reduce_sum[...] * ADAPTER_SCALE, up_sum[...])):
        for block_lane in range(lanes):
            line = (half * lanes + block_lane) * 8
            part_ref[line // piece, line % piece : line % piece + 8, :] = total[:, block_lane * PAIR : (block_lane + 1) * PAIR]
    copies = [send(part_ref.at[lax.rem(me + delta, dp)], plane_ref.at[delta], delta, peer(delta)) for delta in range(1, dp)]
    total = part_ref[me]
    for delta in range(1, dp):
        copies[delta - 1].wait()
        total = total + plane_ref[delta]
    line_ref[place] = total
    copies = [send(line_ref.at[place], line_ref.at[place], dp + delta, line_peer(delta)) for delta in range(1, seq)]
    for copy in copies:
        copy.wait()
    total = line_ref[0]
    for other in range(1, seq):
        total = total + line_ref[other]
    sum_out[me] = total
    copies = [send(sum_out.at[me], sum_out.at[me], dp + seq + delta, peer(delta)) for delta in range(1, dp)]
    for s in range(seq - 4, 0, -1):
        chain(last, s)
    chain_end(last, last % 2, back_ref)
    for copy in copies:
        copy.wait()
    for copy in flights.values():
        copy.wait_send()
    for row in range(rows):
        for s in range(1, seq):
            @pl.when((place >= s - 1) & (place < top))
            def _():
                hop(row, s).wait_send()
    for s in range(1, seq):
        @pl.when(place >= s)
        def _():
            leave(last, s).wait_send()
    grad_store(last - 1, late_slot).wait()
    grad_store(last, last % 2).wait()


def run_block(plane, seq, x, seg, small, vectors, shards, gout):
    rows, tokens, width = x.shape
    assert rows == 3
    length = seq * tokens
    dp = plane[0] * plane[1] * 2
    hidden_units = shards[2].shape[1]
    block = 1024
    quads = width // QUAD
    piece = max(8, 16 * width // (PAIR * dp))
    nx, ny = plane
    columns = max(1, min(4, hidden_units // (dp * PAIR)))
    flights = nx - 1 + ny - 1 + 2 * (nx - 1) * (ny - 1) + nx * ny
    sums = 2 * dp + seq
    anywhere = pl.BlockSpec(memory_space=pl.ANY)
    vmem = pl.BlockSpec(memory_space=pltpu.VMEM)
    dma = pltpu.SemaphoreType.DMA

    def held(*dims, dtype=BF16):
        return pltpu.VMEM(dims, dtype)

    def shape(*dims, dtype=BF16):
        return jax.ShapeDtypeStruct(dims, dtype)

    result = pl.pallas_call(
        partial(block_kernel, plane, seq, rows, block),
        in_specs=[anywhere] * 17,
        out_specs=[anywhere, anywhere, vmem] + [anywhere] * 6,
        out_shape=[
            shape(rows, tokens, width), shape(rows, tokens, width, dtype=F32), shape(dp, piece, PAIR, dtype=F32),
            shape(rows, tokens, width), shape(rows, length, width), shape(rows, length, width),
            shape(rows, tokens, width), shape(rows, tokens, width), shape(rows, tokens, width, dtype=F32),
        ],
        scratch_shapes=[
            *(held(*a.shape, dtype=a.dtype) for a in (x, seg, small, *vectors)), dma((12,)),
            held(width, 3 * width), held(width, width), held(columns, width, hidden_units // columns), held(columns, hidden_units // columns, width),
            held(rows, seq, tokens, width), held(tokens, width), held(length, width), held(length, width),
            held(tokens, width), held(tokens, width), held(tokens, width),
            held(tokens, width), held(tokens, width),
            held(tokens, width, dtype=F32), held(tokens, width, dtype=F32), held(2, tokens, width, dtype=F32),
            held(tokens, width, dtype=F32), held(tokens, length, dtype=F32), held(rows, quads, 8, tokens, dtype=F32),
            held(width, tokens, dtype=F32), held(tokens, 2 * width),
            held(seq - 1, tokens, width), held(rows, seq - 1, tokens, width),
            held(rows, 8, tokens, dtype=F32), held(columns, 8, hidden_units // columns, dtype=F32),
            held(rows, quads, 8, tokens, dtype=F32), held(rows, 8, length),
            held(8, width, dtype=F32), held(8, width, dtype=F32),
            held(dp, piece, PAIR, dtype=F32), held(dp, piece, PAIR, dtype=F32), held(seq, piece, PAIR, dtype=F32),
            dma((2 + 2 * columns, flights)), dma((2 + 2 * columns, flights)), dma((rows, seq - 1)), dma((rows, seq - 1)),
            dma((2 + 2 * columns, dp)), dma((7,)), dma((2,)), dma((12,)), dma((3,)),
            dma((seq - 1,)), dma((rows, seq - 1)), dma((sums,)), dma((sums,)),
        ],
        compiler_params=pltpu.CompilerParams(
            vmem_limit_bytes=VMEM_BYTES, collective_id=0, has_side_effects=True
        ),
        name="block",
    )(x, seg, small, *vectors, *shards, gout)
    out, grad, total = result[:3]
    flat = total.reshape(-1, PAIR)[: 16 * width // PAIR]
    return out, grad, flat.reshape(2, width // PAIR, 8, PAIR).transpose(0, 2, 1, 3).reshape(2, 8, width)


def on_device(
    dp,
    seq,
    block_input,
    seg_start,
    ln1_gain,
    ln1_bias,
    qkv_weight,
    query_bias,
    value_bias,
    query_adapter_reduce,
    query_up,
    value_adapter_reduce,
    value_up,
    out_weight,
    out_bias,
    ln2_gain,
    ln2_bias,
    fc_weight,
    fc_bias,
    proj_weight,
    proj_bias,
    grad_out,
):
    rows, tokens, width = block_input.shape
    rank = query_up.shape[0]
    side = math.isqrt(dp // 2)
    small = jnp.concatenate([query_adapter_reduce.T, value_adapter_reduce.T, query_up, value_up], axis=0)

    def as_row(vector):
        return vector.reshape(1, -1)

    vectors = tuple(
        as_row(a)
        for a in (ln1_gain, ln1_bias, query_bias, value_bias, out_bias, ln2_gain, ln2_bias, proj_bias, fc_bias)
    )
    out, grad, sums = run_block(
        (side, dp // (2 * side)), seq, block_input, seg_start, small, vectors,
        (qkv_weight, out_weight, fc_weight, proj_weight), grad_out,
    )
    reduce, up = sums[0], sums[1]
    return out, grad, reduce[:rank].T, up[:rank], reduce[rank : 2 * rank].T, up[rank : 2 * rank]


def solution(mesh):
    return jax.shard_map(
        partial(on_device, mesh.shape["dp"], mesh.shape["seq"]),
        mesh=mesh,
        in_specs=(
            P("dp", "seq", None),
            P("dp", None),
            P(),
            P(),
            P("dp", None),
            P(),
            P(),
            P(),
            P(),
            P(),
            P(),
            P("dp", None),
            P(),
            P(),
            P(),
            P("dp", None),
            P(),
            P("dp", None),
            P(),
            P("dp", "seq", None),
        ),
        out_specs=(P("dp", "seq", None), P("dp", "seq", None), P(), P(), P(), P()),
        check_vma=False,
    )
```

```python
import math
from functools import partial

import jax
import jax.numpy as jnp
from jax import lax
from jax.experimental import pallas as pl
from jax.experimental.pallas import tpu as pltpu
from jax.sharding import PartitionSpec as P

HEAD = 64
QUAD = 256
PAIR = 128
NORM_EPSILON = 1e-05
ADAPTER_SCALE = 8.0
MASKED = -1e30
GELU_A = 0.7978845608028654
GELU_B = 0.044715

F32 = jnp.float32
BF16 = jnp.bfloat16
VMEM_BYTES = 65400 * 1024


def dot_nn(left, right):
    return lax.dot_general(left, right, (((1,), (0,)), ((), ())), preferred_element_type=F32)


def dot_nt(left, right):
    return lax.dot_general(left, right, (((1,), (1,)), ((), ())), preferred_element_type=F32)


def norm_parts(values):
    average = jnp.mean(values, axis=-1, keepdims=True)
    centered = values - average
    inverse = lax.rsqrt(jnp.mean(centered * centered, axis=-1, keepdims=True) + NORM_EPSILON)
    return centered * inverse, inverse


def norm_backward(gradient, normed, inverse, gain):
    scaled = gradient * gain
    return inverse * (
        scaled
        - jnp.mean(scaled, axis=-1, keepdims=True)
        - normed * jnp.mean(scaled * normed, axis=-1, keepdims=True)
    )


def head_lanes(rows, dtype):
    lane = lax.broadcasted_iota(jnp.int32, (rows, PAIR), 1)
    return lane < HEAD


def own_starts(seg_ref, begin_ref, place, seq):
    rows, _, tokens = begin_ref.shape
    own = jnp.zeros((rows, tokens), jnp.int32)
    for index in range(seq):
        own = jnp.where(place == index, seg_ref[:, index * tokens : (index + 1) * tokens], own)
    own = own.astype(F32)
    for row in range(rows):
        begin_ref[row] = jnp.broadcast_to(own[row : row + 1], (8, tokens))


def block_kernel(
    plane, seq, rows, block,
    x_in, seg_in, reduce_q_in, reduce_v_in, up_q_in, up_v_in, gain1_in, shift1_in, bias_q_in, bias_v_in, out_bias_in, gain2_in, shift2_in, proj_bias_in,
    fc_bias_in, shard_in, wo_in, fc_in, proj_in, gout_in,
    out_out, grad_out, sum_out, q_spill, k_spill, v_spill, mix_spill, gmix_spill, dq_spill,
    x_ref, seg_ref, reduce_q, reduce_v, up_q, up_v, gain1, shift1, bias_q, bias_v, out_bias, gain2, shift2, proj_bias, fc_bias, small_ref, input_sems,
    w_held, wo_held, fc_held, proj_held, hidden, q_held, k_held, v_held, mix_row, mix_held, gout_held,
    gmix_ref, h2_ref, acc_ref, back_ref, gmid_ref, own_ref, mask_ref, delta_ref, dq_ref, dkv_ref,
    leaving, arriving, begin_ref, bias_held, lse_ref, down_ref, up_sum, reduce_sum,
    part_ref, plane_ref, line_ref,
    send_sems, recv_sems, hop_send, hop_recv, own_sems, spill_sems, load_sems, late_sems, store_sems,
    leave_sems, arrive_sems, sum_send, sum_recv,
):
    nx, ny = plane
    dp = nx * ny * 2
    inputs = [
        pltpu.make_async_copy(source, target, input_sems.at[i])
        for i, (source, target) in enumerate(
            (
                (x_in, x_ref), (gain1_in, gain1), (shift1_in, shift1), (seg_in, seg_ref),
                (reduce_q_in, reduce_q), (reduce_v_in, reduce_v), (up_q_in, up_q), (up_v_in, up_v),
                (bias_q_in, bias_q), (bias_v_in, bias_v), (out_bias_in, out_bias), (gain2_in, gain2),
                (shift2_in, shift2), (proj_bias_in, proj_bias), (fc_bias_in, fc_bias),
            )
        )
    ]
    tokens, width = x_ref.shape[1], x_ref.shape[2]
    quads = width // QUAD
    columns, chunk_units = fc_held.shape[0], fc_held.shape[2]
    per_chunk = chunk_units // block
    steps = columns * per_chunk
    last = rows - 1
    late_slot = 1 - last % 2
    top = seq - 1
    mesh_type = pl.DeviceIdType.MESH
    me, place = lax.axis_index("dp"), lax.axis_index("seq")
    core = lax.rem(me, 2)
    my_x = lax.rem(me // 2, nx)
    my_y = me // (2 * nx)

    def index(y, x, c):
        return (y * nx + x) * 2 + c

    def x_peer(delta):
        return index(my_y, lax.rem(my_x + delta, nx), core), place

    def y_peer(delta):
        return index(lax.rem(my_y + delta, ny), my_x, core), place

    twin = (index(my_y, my_x, 1 - core), place)

    def owner(dy, dx, c):
        return index(lax.rem(my_y + ny - dy, ny), lax.rem(my_x + nx - dx, nx), c)

    def peer(delta):
        return lax.rem(me + delta, dp), place

    def line_peer(delta):
        return me, lax.rem(place + delta, seq)

    barrier = pltpu.get_barrier_semaphore()
    for delta in range(1, dp):
        pl.semaphore_signal(barrier, inc=1, device_id=peer(delta), device_id_type=mesh_type)
    for delta in range(1, seq):
        pl.semaphore_signal(barrier, inc=1, device_id=line_peer(delta), device_id_type=mesh_type)

    share = fc_in.shape[1] // dp
    cut = share // columns
    tensors = [(w_held, shard_in.shape[0]), (wo_held, wo_in.shape[0])]
    for j in range(columns):
        tensors += [(fc_held.at[j], fc_in.shape[0]), (proj_held.at[j], cut)]

    def region(t, device, half=None):
        target, size = tensors[t]
        if half is None:
            return target.at[pl.ds(pl.multiple_of(device * size, size), size), :]
        part = size // 2
        return target.at[pl.ds(pl.multiple_of(device * size + half * part, part), part), :]

    def flight(t, slot, part, device):
        return pltpu.make_async_remote_copy(
            src_ref=part, dst_ref=part, send_sem=send_sems.at[t, slot], recv_sem=recv_sems.at[t, slot],
            device_id=device, device_id_type=mesh_type,
        )

    flights = {}
    for t in range(len(tensors)):
        names = [("x", 0, dx) for dx in range(1, nx)] + [("y", dy, 0) for dy in range(1, ny)]
        names += [(kind, dy, dx) for kind in "ab" for dy in range(1, ny) for dx in range(1, nx)]
        names += [("t", dy, dx) for dy in range(ny) for dx in range(nx)]
        for slot, (kind, dy, dx) in enumerate(names):
            if kind == "x":
                part, device = region(t, me), x_peer(dx)
            elif kind == "y":
                part, device = region(t, me), y_peer(dy)
            elif kind == "a":
                part, device = region(t, owner(0, dx, core), 0), y_peer(dy)
            elif kind == "b":
                part, device = region(t, owner(dy, 0, core), 1), x_peer(dx)
            else:
                part, device = region(t, owner(dy, dx, core)), twin
            flights[t, kind, dy, dx] = flight(t, slot, part, device)

    def wave_one(t):
        for dx in range(1, nx):
            flights[t, "x", 0, dx].start()
        for dy in range(1, ny):
            flights[t, "y", dy, 0].start()
        flights[t, "t", 0, 0].start()

    def wave_two(t):
        for dx in range(1, nx):
            flights[t, "x", 0, dx].wait_recv()
            for dy in range(1, ny):
                flights[t, "a", dy, dx].start()
        for dy in range(1, ny):
            flights[t, "y", dy, 0].wait_recv()
            for dx in range(1, nx):
                flights[t, "b", dy, dx].start()
        for dx in range(1, nx):
            flights[t, "t", 0, dx].start()
        for dy in range(1, ny):
            flights[t, "t", dy, 0].start()

    def wave_three(t):
        for dy in range(1, ny):
            for dx in range(1, nx):
                flights[t, "a", dy, dx].wait_recv()
                flights[t, "b", dy, dx].wait_recv()
                flights[t, "t", dy, dx].start()

    def wave_end(t):
        for dy in range(ny):
            for dx in range(nx):
                flights[t, "t", dy, dx].wait_recv()

    def hop(row, s):
        return pltpu.make_async_remote_copy(
            src_ref=hidden.at[row, s - 1], dst_ref=hidden.at[row, s],
            send_sem=hop_send.at[row, s - 1], recv_sem=hop_recv.at[row, s - 1],
            device_id=(me, place + 1), device_id_type=mesh_type,
        )

    def hop_start(row, s):
        @pl.when((place >= s - 1) & (place < top))
        def _():
            hop(row, s).start()

    def arrive(row, s):
        @pl.when(place >= s)
        def _():
            hop(row, s).wait_recv()

        if s < seq - 1:
            hop_start(row, s + 1)
        if s == seq - 1 and row < rows - 1:
            hop_start(row + 1, 1)

    def first_norm(row):
        normed, _ = norm_parts(x_ref[row].astype(F32))
        hidden[row, 0] = (normed * gain1[...] + shift1[...]).astype(BF16)

    def gout_load(row):
        return pltpu.make_async_copy(gout_in.at[row], gout_held, load_sems.at[0])

    def mix_load(row):
        return pltpu.make_async_copy(mix_spill.at[row], mix_held, load_sems.at[1])

    own_copies = [
        pltpu.make_async_copy(source, region(t, me), own_sems.at[t, 0]) for t, source in enumerate((shard_in, wo_in))
    ]
    for j in range(columns):
        for d in range(dp):
            part = region(2 + 2 * j, me).at[:, d * cut : (d + 1) * cut]
            source = fc_in.at[:, d * share + j * cut : d * share + (j + 1) * cut]
            own_copies.append(pltpu.make_async_copy(source, part, own_sems.at[2 + 2 * j, d]))
        source = proj_in.at[j * cut : (j + 1) * cut, :]
        own_copies.append(pltpu.make_async_copy(source, region(3 + 2 * j, me), own_sems.at[3 + 2 * j, 0]))
    for copy in inputs[:8]:
        copy.start()
    own_copies[0].start()
    for copy in inputs[8:]:
        copy.start()
    for copy in inputs[:3]:
        copy.wait()
    first_norm(0)
    for copy in inputs[4:8]:
        copy.wait()
    small_ref[:8, :] = jnp.concatenate([reduce_q[...].astype(F32), reduce_v[...].astype(F32)], axis=0).astype(BF16)
    small_ref[8:, :] = jnp.concatenate([up_q[...].astype(F32), up_v[...].astype(F32)], axis=0).astype(BF16)
    dq_ref[:, :8] = small_ref[:8, :].astype(F32).T
    pl.semaphore_wait(barrier, dp + seq - 2)
    hop_start(0, 1)
    own_copies[0].wait()
    size = shard_in.shape[0]
    mine = pl.ds(pl.multiple_of(me * size, size), size)
    reduce_own = dq_ref[mine, :8].astype(BF16)
    up = small_ref[8:, :]
    low_rank = lax.broadcasted_iota(jnp.int32, up.shape, 0) < 4
    for column, rank_up in ((0, jnp.where(low_rank, up, jnp.zeros_like(up))), (2, jnp.where(low_rank, jnp.zeros_like(up), up))):
        span = slice(column * width, (column + 1) * width)
        change = dot_nn(reduce_own, rank_up) * ADAPTER_SCALE
        w_held[mine, span] = (w_held[mine, span].astype(F32) + change).astype(BF16)
    wave_one(0)
    for copy in own_copies[1:]:
        copy.start()
    gout_load(0).start()
    for copy in inputs[8:] + inputs[3:4] + own_copies[1:]:
        copy.wait()
    own_starts(seg_ref, begin_ref, place, seq)
    for row in range(1, rows):
        first_norm(row)
    for s in range(1, seq):
        @pl.when(place < s)
        def _():
            for row in range(rows):
                hidden[row, s] = jnp.zeros((tokens, width), BF16)
    for j in range(columns):
        for d in range(dp):
            bias_held[j, :1, d * cut : (d + 1) * cut] = fc_bias[:, d * share + j * cut : d * share + (j + 1) * cut]
    up_sum[...] = jnp.zeros_like(up_sum)
    reduce_sum[...] = jnp.zeros_like(reduce_sum)

    low = head_lanes(tokens, BF16)
    lane = lax.broadcasted_iota(jnp.int32, (tokens, PAIR), 1)
    rank_row = lax.broadcasted_iota(jnp.int32, (8, width), 0) < 4

    def both_heads(pair):
        none = jnp.zeros_like(pair)
        return jnp.concatenate([jnp.where(low, pair, none), jnp.where(low, none, pair)], axis=0)

    def spills(row):
        return [
            pltpu.make_async_copy(held, spill.at[row], spill_sems.at[i])
            for i, (held, spill) in enumerate(
                ((q_held, q_spill), (k_held, k_spill), (v_held, v_spill), (mix_row, mix_spill))
            )
        ]

    def reloads(row):
        return [
            pltpu.make_async_copy(spill.at[row], held, spill_sems.at[4 + i])
            for i, (held, spill) in enumerate(((q_held, q_spill), (k_held, k_spill), (v_held, v_spill)))
        ]

    def attend(row, middle):
        query = place * tokens + lax.broadcasted_iota(jnp.int32, (tokens, tokens), 0)
        start = begin_ref[row].T[:, :1].astype(jnp.int32)
        for s in range(seq):
            key = (place - s) * tokens + lax.broadcasted_iota(jnp.int32, (tokens, tokens), 1)
            span = slice(s * tokens, (s + 1) * tokens)
            mask_ref[:, span] = jnp.where((key >= start) & (key <= query), 0.0, MASKED)
            down_ref[row, :, span] = (dot_nt(small_ref[:8, :], hidden[row, s]) * ADAPTER_SCALE).astype(BF16)

        for quad in range(quads):
            own = slice(quad * QUAD, (quad + 1) * QUAD)
            key_span = slice(width + quad * QUAD, width + (quad + 1) * QUAD)
            value_span = slice(2 * width + quad * QUAD, 2 * width + (quad + 1) * QUAD)
            q = dot_nn(hidden[row, 0], w_held[:, own]) + bias_q[:, own]
            q_held[:, own] = (q.astype(BF16) * (HEAD**-0.5)).astype(BF16)
            for s in range(seq):
                span = slice(s * tokens, (s + 1) * tokens)
                k_held[span, own] = dot_nn(hidden[row, s], w_held[:, key_span]).astype(BF16)
                v_held[span, own] = (dot_nn(hidden[row, s], w_held[:, value_span]) + bias_v[:, own]).astype(BF16)
            totals = jnp.zeros((tokens, PAIR), F32)
            for pair in range(QUAD // PAIR):
                span = slice(quad * QUAD + pair * PAIR, quad * QUAD + (pair + 1) * PAIR)
                score = dot_nt(both_heads(q_held[:, span]), k_held[:, span])
                score = jnp.concatenate([score[:tokens] + mask_ref[...], score[tokens:] + mask_ref[...]], axis=0)
                highest = jnp.max(score, axis=-1, keepdims=True)
                weight = jnp.exp(score - highest)
                total = jnp.sum(weight, axis=-1, keepdims=True)
                mixed = dot_nn(weight.astype(BF16), v_held[:, span]) * (1.0 / total)
                mix_row[:, span] = jnp.where(low, mixed[:tokens], mixed[tokens:]).astype(BF16)
                lse = highest + jnp.log(total)
                totals = jnp.where(lane == 2 * pair, lse[:tokens], totals)
                totals = jnp.where(lane == 2 * pair + 1, lse[tokens:], totals)
            lse_ref[row, quad] = totals.T[:8]
            if 2 * (quad + 1) == quads:
                middle()

    def out_store(row):
        return pltpu.make_async_copy(h2_ref, out_out.at[row], store_sems.at[0])

    def grad_store(row, slot):
        return pltpu.make_async_copy(gmid_ref.at[slot], grad_out.at[row], store_sems.at[1 + slot])

    def late_spills(row):
        return [
            pltpu.make_async_copy(gmix_ref, gmix_spill.at[row], late_sems.at[0]),
            pltpu.make_async_copy(acc_ref, dq_spill.at[row], late_sems.at[1]),
        ]

    def late_loads(row):
        q_room, gmix_room = ((mix_row, mix_held), (gout_held, h2_ref))[row]
        lines = slice((2 + row) * tokens, (3 + row) * tokens)
        return [
            pltpu.make_async_copy(gmix_spill.at[row], gmix_room, late_sems.at[2 + 4 * row]),
            pltpu.make_async_copy(q_spill.at[row], q_room, late_sems.at[3 + 4 * row]),
            pltpu.make_async_copy(k_spill.at[row, :tokens, :], k_held.at[lines, :], late_sems.at[4 + 4 * row]),
            pltpu.make_async_copy(v_spill.at[row, :tokens, :], v_held.at[lines, :], late_sems.at[5 + 4 * row]),
        ]

    def dq_load(row):
        return pltpu.make_async_copy(dq_spill.at[row], acc_ref, late_sems.at[10])

    def gmid_load(row):
        return pltpu.make_async_copy(grad_out.at[row], gmid_ref.at[late_slot], late_sems.at[11])

    def late_ready(row):
        for copy in late_loads(row):
            copy.wait()
        dq_load(row).wait()
        q_room, gmix_room = ((mix_row, mix_held), (gout_held, h2_ref))[row]
        lines = slice((2 + row) * tokens, (3 + row) * tokens)
        q_held[...] = q_room[...]
        gmix_ref[...] = gmix_room[...]
        k_held[:tokens, :] = k_held[lines, :]
        v_held[:tokens, :] = v_held[lines, :]
        dq_ref[...] = acc_ref[...].T

    def leave(row, s):
        return pltpu.make_async_remote_copy(
            src_ref=leaving.at[s - 1], dst_ref=arriving.at[row, s - 1],
            send_sem=leave_sems.at[s - 1], recv_sem=arrive_sems.at[row, s - 1],
            device_id=(me, place - 1), device_id_type=mesh_type,
        )

    def chain(row, s):
        @pl.when((place < top) & (place >= s))
        def _():
            leave(row, s + 1).wait_recv()
            leaving[s - 1] = (leaving[s - 1].astype(F32) + arriving[row, s].astype(F32)).astype(BF16)
            leave(row, s).start()

    def chain_end(row, slot, own):
        @pl.when(place < top)
        def _():
            leave(row, 1).wait_recv()
            own[...] += arriving[row, 0].astype(F32)

        normed, inverse = norm_parts(x_ref[row].astype(F32))
        gmid_ref[slot] = gmid_ref[slot] + norm_backward(own[...], normed, inverse, gain1[...])
        grad_store(row, slot).start()

    def feed_begin(row):
        gout_load(row).wait()

        @pl.when(row < 2)
        def _():
            mix_load(row).wait()

        @pl.when(row >= 1)
        def _():
            out_store(row - 1).wait()

        @pl.when(row == 1)
        def _():
            for copy in reloads(row):
                copy.start()

        @pl.when(row >= 2)
        def _():
            grad_store(row - 2, lax.rem(row, 2)).wait()

        middle = x_ref[row].astype(F32) + dot_nn(mix_held[...], wo_held[...]) + out_bias[...]
        gmid_ref[lax.rem(row, 2)] = middle
        normed, _ = norm_parts(middle)
        h2_ref[...] = (normed * gain2[...] + shift2[...]).astype(BF16)

        @pl.when(row > 0)
        def _():
            late_spills(row - 1)[1].wait()

        acc_ref[...] = jnp.zeros_like(acc_ref)
        back_ref[...] = jnp.zeros_like(back_ref)

    def feed_step(step):
        j = step // per_chunk
        part = pl.ds(pl.multiple_of(lax.rem(step, per_chunk) * block, block), block)
        before = dot_nn(h2_ref[...], fc_held[j, :, part]) + bias_held[j, :1, part]
        square = before * before
        bend = jnp.tanh(GELU_A * before * (1.0 + GELU_B * square))
        half = 0.5 * (1.0 + bend)
        slope = half + 0.5 * before * (1.0 - bend * bend) * (GELU_A * (1.0 + 3.0 * GELU_B * square))
        act = (before * half).astype(BF16)
        g_before = (dot_nt(gout_held[...], proj_held[j, part, :]) * slope).astype(BF16)
        acc_ref[...] += dot_nn(act, proj_held[j, part, :])
        back_ref[...] += dot_nt(g_before, fc_held[j, :, part])

    def feed_end(row):
        slot = lax.rem(row, 2)
        middle = gmid_ref[slot]
        h2_ref[...] = (middle + acc_ref[...] + proj_bias[...]).astype(BF16)
        out_store(row).start()
        normed, inverse = norm_parts(middle)
        g_middle = gout_held[...].astype(F32) + norm_backward(back_ref[...], normed, inverse, gain2[...])
        gmid_ref[slot] = g_middle

        @pl.when(row < last)
        def _():
            grad_store(row, slot).start()

        @pl.when(row > 0)
        def _():
            late_spills(row - 1)[0].wait()

        gmix_ref[...] = dot_nt(g_middle.astype(BF16), wo_held[...]).astype(BF16)
        for pair in range(width // PAIR):
            span = slice(pair * PAIR, (pair + 1) * PAIR)
            product = (gmix_ref[:, span].astype(F32) * mix_held[:, span].astype(F32)).T
            for half in range(2):
                head = pair * 2 + half
                delta_ref[row, head // 4, head % 4 : head % 4 + 1, :] = jnp.sum(
                    product[half * HEAD : (half + 1) * HEAD], axis=0, keepdims=True
                )

        @pl.when(row < rows - 1)
        def _():
            gout_load(row + 1).start()

        @pl.when(row == 0)
        def _():
            mix_load(row + 1).start()

    def attend_chunk(row, s, summed=None):
        query = place * tokens + lax.broadcasted_iota(jnp.int32, (tokens, tokens), 1)
        key = (place - s) * tokens + lax.broadcasted_iota(jnp.int32, (tokens, tokens), 0)
        start = begin_ref[row, :1, :].astype(jnp.int32)
        mask = jnp.where((key >= start) & (key <= query), 0.0, MASKED)
        mask_ref[:, :tokens] = mask
        mask_ref[:, tokens : 2 * tokens] = mask
        rows_s = pl.ds(pl.multiple_of(s * tokens, tokens), tokens)
        for pair in range(width // PAIR):
            span = slice(pair * PAIR, (pair + 1) * PAIR)
            k_pair, v_pair = k_held[rows_s, span], v_held[rows_s, span]
            q_both, g_both = both_heads(q_held[:, span]), both_heads(gmix_ref[:, span])
            head = 2 * (pair % 2)
            lse, inner = [
                jnp.concatenate([ref[head : head + 1, :], ref[head + 1 : head + 2, :]], axis=1)
                for ref in (lse_ref.at[row, pair // 2], delta_ref.at[row, pair // 2])
            ]
            prob = jnp.exp(dot_nt(k_pair, q_both) + mask_ref[:, : 2 * tokens] - lse)
            g_score = (prob * (dot_nt(v_pair, g_both) - inner)).astype(BF16)
            dkv_ref[:, span] = dot_nn(g_score, q_both).astype(BF16)
            dkv_ref[:, width + pair * PAIR : width + (pair + 1) * PAIR] = dot_nn(prob.astype(BF16), g_both).astype(BF16)
            k_turned = k_pair.astype(F32).T.astype(BF16)
            for half in range(2):
                lines = slice(pair * PAIR + half * HEAD, pair * PAIR + (half + 1) * HEAD)
                part = g_score[:, half * tokens : (half + 1) * tokens]
                dq_ref[lines, :] += dot_nn(k_turned[half * HEAD : (half + 1) * HEAD], part)

        dv = dkv_ref[:, width:]
        up_grad = dot_nn(down_ref[row, :, rows_s], dv)
        g_down = dot_nt(small_ref[8:, :], dv).astype(BF16)
        reduce_grad = dot_nn(g_down, hidden[row, s])
        up_sum[...] += jnp.where(rank_row, 0.0, up_grad)
        reduce_sum[...] += jnp.where(rank_row, 0.0, reduce_grad)
        if summed is None:
            @pl.when(row > 0)
            def _():
                leave(row - 1, s).wait_send()

            leaving[s - 1] = dot_nt(dkv_ref[...], w_held[:, width:]).astype(BF16)

            @pl.when(place == top)
            def _():
                leave(row, s).start()
        else:
            dq = (dq_ref[...].T * (HEAD**-0.5)).astype(BF16)
            up_grad = dot_nn(down_ref[row, :, rows_s], dq)
            g_down = dot_nt(small_ref[8:, :], dq).astype(BF16)
            reduce_grad = dot_nn(g_down, hidden[row, s])
            up_sum[...] += jnp.where(rank_row, up_grad, 0.0)
            reduce_sum[...] += jnp.where(rank_row, reduce_grad, 0.0)
            summed()
            own_ref[...] = dot_nt(dkv_ref[...], w_held[:, width:]) + dot_nt(dq, w_held[:, :width])

    def backward(row):
        feed_end(row)

        @pl.when(row > 0)
        def _():
            chain(row - 1, seq - 3)

        @pl.when(row < 2)
        def _():
            for copy in reloads(row):
                copy.wait()

        dq_ref[...] = jnp.zeros_like(dq_ref)

        @pl.loop(0, seq - 1)
        def _(step):
            s = seq - 1 - step

            @pl.when((row > 0) & (s < seq - 3))
            def _():
                chain(row - 1, s)

            @pl.when(place >= s)
            def _():
                attend_chunk(row, s)

        chain(row, seq - 2)

        @pl.when(row < last)
        def _():
            acc_ref[...] = dq_ref[...].T
            for copy in late_spills(row):
                copy.start()

    def both(action, j):
        if j < columns:
            action(2 + 2 * j)
            action(3 + 2 * j)

    def before_first():
        arrive(0, 1)
        wave_two(0)
        wave_one(1)
        for s in range(2, seq):
            if s == seq - 1:
                wave_three(0)
                both(wave_one, 0)
                wave_two(1)
            arrive(0, s)
        wave_end(0)
        both(wave_one, 1)

    def before_second():
        both(wave_two, 0)
        both(wave_one, 2)
        for s in range(1, seq):
            if s == seq - 1:
                both(wave_two, 1)
                wave_three(1)
                both(wave_three, 0)
            arrive(1, s)
        both(wave_one, 3)

    def amid_second():
        both(wave_two, 2)
        both(wave_three, 1)

    def before_feed():
        arrive(2, 1)
        wave_end(1)
        both(wave_two, 3)
        for copy in spills(1):
            copy.wait()
        for copy in reloads(0):
            copy.start()

    def amid_feed(step):
        for j in range(columns):
            @pl.when(step == j * per_chunk)
            def _():
                if j == min(1, columns - 1):
                    for s in range(2, seq - 1):
                        arrive(2, s)
                if j >= 2 or j == columns - 1:
                    both(wave_three, j)
                both(wave_end, j)

    def before_third():
        arrive(2, seq - 1)

    def before_later(row):
        for s in range(1, seq):
            arrive(row, s)

    @pl.loop(0, 2 * rows)
    def _(turn):
        attending = (turn < 2) | ((turn >= 4) & (lax.rem(turn, 2) == 0))
        attend_row = jnp.where(turn < 2, turn, turn // 2)
        row = jnp.where(turn < 4, jnp.maximum(turn - 2, 0), (turn - 1) // 2)
        for index in range(rows):
            befores = (before_first, before_second, before_third)
            action = befores[index] if index < 3 else partial(before_later, index)
            pl.when(turn == (index if index < 2 else 2 * index))(action)

        pl.when(turn == 2)(before_feed)

        @pl.when(turn == 1)
        def _():
            for copy in spills(0):
                copy.wait()
            mix_load(0).start()

        @pl.when(attending)
        def _():
            attend(attend_row, lambda: pl.when(turn == 1)(amid_second))

            @pl.when(turn < 2)
            def _():
                for copy in spills(turn):
                    copy.start()

            @pl.when(turn >= 2)
            def _():
                mix_held[...] = mix_row[...]

        @pl.when(jnp.logical_not(attending))
        def _():
            feed_begin(row)

            @pl.loop(0, steps)
            def _(step):
                pl.when(turn == 2)(partial(amid_feed, step))
                feed_step(step)

            backward(row)

    def sum_copy(source, target, slot, device):
        return pltpu.make_async_remote_copy(
            src_ref=source, dst_ref=target, send_sem=sum_send.at[slot], recv_sem=sum_recv.at[slot],
            device_id=device, device_id_type=mesh_type,
        )

    def piece_copies():
        return [
            sum_copy(part_ref.at[lax.rem(me + delta, dp)], plane_ref.at[delta], delta, peer(delta))
            for delta in range(1, dp)
        ]

    piece = part_ref.shape[1]
    lanes = width // PAIR

    def start_sums():
        part_ref[...] = jnp.zeros_like(part_ref)
        for half, total in enumerate((reduce_sum[...] * ADAPTER_SCALE, up_sum[...])):
            for block_lane in range(lanes):
                line = (half * lanes + block_lane) * 8
                part_ref[line // piece, line % piece : line % piece + 8, :] = total[:, block_lane * PAIR : (block_lane + 1) * PAIR]
        for copy in piece_copies():
            copy.start()

    grad_store(last - 1, late_slot).wait()
    out_store(last).wait()
    for copy in [gmid_load(0), dq_load(0)] + late_loads(0) + late_loads(1):
        copy.start()

    @pl.loop(0, 3)
    def _(turn):
        @pl.when(turn == 1)
        def _():
            late_ready(0)
            dq_load(1).start()

        @pl.when(turn == 2)
        def _():
            late_ready(1)
            grad_store(0, late_slot).wait()
            gmid_load(1).start()

        attend_chunk(jnp.where(turn == 0, last, turn - 1), 0, lambda: pl.when(turn == 2)(start_sums))

        @pl.when(turn == 0)
        def _():
            back_ref[...] = own_ref[...]

        @pl.when(turn > 0)
        def _():
            gmid_load(turn - 1).wait()
            chain_end(turn - 1, late_slot, own_ref)

        pl.when(turn == 1)(partial(chain, last, seq - 3))

    total = part_ref[me]
    for delta, copy in enumerate(piece_copies()):
        copy.wait()
        total = total + plane_ref[delta + 1]
    line_ref[place] = total
    line_copies = [
        sum_copy(line_ref.at[place], line_ref.at[place], dp + delta, line_peer(delta)) for delta in range(1, seq)
    ]
    for copy in line_copies:
        copy.start()
    for copy in line_copies:
        copy.wait()
    total = line_ref[0]
    for other in range(1, seq):
        total = total + line_ref[other]
    sum_out[me] = total
    copies = [sum_copy(sum_out.at[me], sum_out.at[me], dp + seq + delta, peer(delta)) for delta in range(1, dp)]
    for copy in copies:
        copy.start()
    for s in range(seq - 4, 0, -1):
        chain(last, s)
    chain_end(last, last % 2, back_ref)
    for copy in copies:
        copy.wait()
    for copy in flights.values():
        copy.wait_send()
    for row in range(rows):
        for s in range(1, seq):
            @pl.when((place >= s - 1) & (place < top))
            def _():
                hop(row, s).wait_send()
    for s in range(1, seq):
        @pl.when(place >= s)
        def _():
            leave(last, s).wait_send()
    grad_store(last - 1, late_slot).wait()
    grad_store(last, last % 2).wait()


def run_block(plane, seq, x, seg, adapters, vectors, shards, gout):
    rows, tokens, width = x.shape
    assert rows == 3
    length = seq * tokens
    dp = plane[0] * plane[1] * 2
    hidden_units = shards[2].shape[1]
    block = 1024
    quads = width // QUAD
    piece = max(8, 16 * width // (PAIR * dp))
    nx, ny = plane
    columns = max(1, min(4, hidden_units // (dp * PAIR)))
    flights = nx - 1 + ny - 1 + 2 * (nx - 1) * (ny - 1) + nx * ny
    sums = 2 * dp + seq
    anywhere = pl.BlockSpec(memory_space=pl.ANY)
    vmem = pl.BlockSpec(memory_space=pltpu.VMEM)
    dma = pltpu.SemaphoreType.DMA

    def held(*dims, dtype=BF16):
        return pltpu.VMEM(dims, dtype)

    def shape(*dims, dtype=BF16):
        return jax.ShapeDtypeStruct(dims, dtype)

    result = pl.pallas_call(
        partial(block_kernel, plane, seq, rows, block),
        in_specs=[anywhere] * 20,
        out_specs=[anywhere, anywhere, vmem] + [anywhere] * 6,
        out_shape=[
            shape(rows, tokens, width), shape(rows, tokens, width, dtype=F32), shape(dp, piece, PAIR, dtype=F32),
            shape(rows, tokens, width), shape(rows, length, width), shape(rows, length, width),
            shape(rows, tokens, width), shape(rows, tokens, width), shape(rows, tokens, width, dtype=F32),
        ],
        scratch_shapes=[
            *(held(*a.shape, dtype=a.dtype) for a in (x, seg, *adapters, *vectors)), held(16, width), dma((15,)),
            held(width, 3 * width), held(width, width), held(columns, width, hidden_units // columns), held(columns, hidden_units // columns, width),
            held(rows, seq, tokens, width), held(tokens, width), held(length, width), held(length, width),
            held(tokens, width), held(tokens, width), held(tokens, width),
            held(tokens, width), held(tokens, width),
            held(tokens, width, dtype=F32), held(tokens, width, dtype=F32), held(2, tokens, width, dtype=F32),
            held(tokens, width, dtype=F32), held(tokens, length, dtype=F32), held(rows, quads, 8, tokens, dtype=F32),
            held(width, tokens, dtype=F32), held(tokens, 2 * width),
            held(seq - 1, tokens, width), held(rows, seq - 1, tokens, width),
            held(rows, 8, tokens, dtype=F32), held(columns, 8, hidden_units // columns, dtype=F32),
            held(rows, quads, 8, tokens, dtype=F32), held(rows, 8, length),
            held(8, width, dtype=F32), held(8, width, dtype=F32),
            held(dp, piece, PAIR, dtype=F32), held(dp, piece, PAIR, dtype=F32), held(seq, piece, PAIR, dtype=F32),
            dma((2 + 2 * columns, flights)), dma((2 + 2 * columns, flights)), dma((rows, seq - 1)), dma((rows, seq - 1)),
            dma((2 + 2 * columns, dp)), dma((7,)), dma((2,)), dma((12,)), dma((3,)),
            dma((seq - 1,)), dma((rows, seq - 1)), dma((sums,)), dma((sums,)),
        ],
        compiler_params=pltpu.CompilerParams(
            vmem_limit_bytes=VMEM_BYTES, collective_id=0, has_side_effects=True
        ),
        name="block",
    )(x, seg, *adapters, *vectors, *shards, gout)
    out, grad, total = result[:3]
    flat = total.reshape(-1, PAIR)[: 16 * width // PAIR]
    return out, grad, flat.reshape(2, width // PAIR, 8, PAIR).transpose(0, 2, 1, 3).reshape(2, 8, width)


def on_device(
    dp,
    seq,
    block_input,
    seg_start,
    ln1_gain,
    ln1_bias,
    qkv_weight,
    query_bias,
    value_bias,
    query_adapter_reduce,
    query_up,
    value_adapter_reduce,
    value_up,
    out_weight,
    out_bias,
    ln2_gain,
    ln2_bias,
    fc_weight,
    fc_bias,
    proj_weight,
    proj_bias,
    grad_out,
):
    rows, tokens, width = block_input.shape
    rank = query_up.shape[0]
    side = math.isqrt(dp // 2)
    adapters = (query_adapter_reduce.T, value_adapter_reduce.T, query_up, value_up)

    def as_row(vector):
        return vector.reshape(1, -1)

    vectors = tuple(
        as_row(a)
        for a in (ln1_gain, ln1_bias, query_bias, value_bias, out_bias, ln2_gain, ln2_bias, proj_bias, fc_bias)
    )
    out, grad, sums = run_block(
        (side, dp // (2 * side)), seq, block_input, seg_start, adapters, vectors,
        (qkv_weight, out_weight, fc_weight, proj_weight), grad_out,
    )
    reduce, up = sums[0], sums[1]
    return out, grad, reduce[:rank].T, up[:rank], reduce[rank : 2 * rank].T, up[rank : 2 * rank]


def solution(mesh):
    return jax.shard_map(
        partial(on_device, mesh.shape["dp"], mesh.shape["seq"]),
        mesh=mesh,
        in_specs=(
            P("dp", "seq", None),
            P("dp", None),
            P(),
            P(),
            P("dp", None),
            P(),
            P(),
            P(),
            P(),
            P(),
            P(),
            P("dp", None),
            P(),
            P(),
            P(),
            P("dp", None),
            P(),
            P("dp", None),
            P(),
            P("dp", "seq", None),
        ),
        out_specs=(P("dp", "seq", None), P("dp", "seq", None), P(), P(), P(), P()),
        check_vma=False,
    )
```

```python
import math
from functools import partial

import jax
import jax.numpy as jnp
from jax import lax
from jax.experimental import pallas as pl
from jax.experimental.pallas import tpu as pltpu
from jax.sharding import PartitionSpec as P

HEAD = 64
QUAD = 256
PAIR = 128
NORM_EPSILON = 1e-05
ADAPTER_SCALE = 8.0
MASKED = -1e30
GELU_A = 0.7978845608028654
GELU_B = 0.044715

F32 = jnp.float32
BF16 = jnp.bfloat16
VMEM_BYTES = 65400 * 1024


def dot_nn(left, right):
    return lax.dot_general(left, right, (((1,), (0,)), ((), ())), preferred_element_type=F32)


def dot_nt(left, right):
    return lax.dot_general(left, right, (((1,), (1,)), ((), ())), preferred_element_type=F32)


def norm_parts(values):
    average = jnp.mean(values, axis=-1, keepdims=True)
    centered = values - average
    inverse = lax.rsqrt(jnp.mean(centered * centered, axis=-1, keepdims=True) + NORM_EPSILON)
    return centered * inverse, inverse


def norm_backward(gradient, normed, inverse, gain):
    scaled = gradient * gain
    return inverse * (
        scaled
        - jnp.mean(scaled, axis=-1, keepdims=True)
        - normed * jnp.mean(scaled * normed, axis=-1, keepdims=True)
    )


def head_lanes(rows, dtype):
    lane = lax.broadcasted_iota(jnp.int32, (rows, PAIR), 1)
    return lane < HEAD


def own_starts(seg_ref, begin_ref, place, seq):
    rows, _, tokens = begin_ref.shape
    own = jnp.zeros((rows, tokens), jnp.int32)
    for index in range(seq):
        own = jnp.where(place == index, seg_ref[:, index * tokens : (index + 1) * tokens], own)
    own = own.astype(F32)
    for row in range(rows):
        begin_ref[row] = jnp.broadcast_to(own[row : row + 1], (8, tokens))


def block_kernel(
    plane, seq, rows, block,
    x_in, seg_in, reduce_q_in, reduce_v_in, up_q_in, up_v_in, gain1_in, shift1_in, bias_q_in, bias_v_in, out_bias_in, gain2_in, shift2_in, proj_bias_in,
    fc_bias_in, shard_in, wo_in, fc_in, proj_in, gout_in,
    out_out, grad_out, sum_out, q_spill, k_spill, v_spill, mix_spill, gmix_spill, dq_spill,
    x_ref, seg_ref, reduce_q, reduce_v, up_q, up_v, gain1, shift1, bias_q, bias_v, out_bias, gain2, shift2, proj_bias, fc_bias, small_ref, input_sems,
    w_held, wo_held, fc_held, proj_held, hidden, q_held, k_held, v_held, mix_row, mix_held, gout_held,
    gmix_ref, h2_ref, acc_ref, back_ref, gmid_ref, own_ref, mask_ref, delta_ref, dq_ref, dkv_ref,
    leaving, arriving, begin_ref, bias_held, lse_ref, down_ref, up_sum, reduce_sum,
    part_ref, plane_ref, line_ref,
    send_sems, recv_sems, hop_send, hop_recv, own_sems, spill_sems, load_sems, late_sems, store_sems,
    leave_sems, arrive_sems, sum_send, sum_recv,
):
    nx, ny = plane
    dp = nx * ny * 2
    inputs = [
        pltpu.make_async_copy(source, target, input_sems.at[i])
        for i, (source, target) in enumerate(
            (
                (x_in.at[0], x_ref.at[0]), (gain1_in, gain1), (shift1_in, shift1), (seg_in, seg_ref),
                (reduce_q_in, reduce_q), (reduce_v_in, reduce_v), (up_q_in, up_q), (up_v_in, up_v),
                (bias_q_in, bias_q), (bias_v_in, bias_v), (out_bias_in, out_bias), (gain2_in, gain2),
                (shift2_in, shift2), (proj_bias_in, proj_bias), (fc_bias_in, fc_bias),
            )
        )
    ]
    later_inputs = [
        pltpu.make_async_copy(x_in.at[row], x_ref.at[row], input_sems.at[14 + row]) for row in range(1, rows)
    ]
    tokens, width = x_ref.shape[1], x_ref.shape[2]
    quads = width // QUAD
    columns, chunk_units = fc_held.shape[0], fc_held.shape[2]
    per_chunk = chunk_units // block
    steps = columns * per_chunk
    last = rows - 1
    late_slot = 1 - last % 2
    top = seq - 1
    mesh_type = pl.DeviceIdType.MESH
    me, place = lax.axis_index("dp"), lax.axis_index("seq")
    core = lax.rem(me, 2)
    my_x = lax.rem(me // 2, nx)
    my_y = me // (2 * nx)

    def index(y, x, c):
        return (y * nx + x) * 2 + c

    def x_peer(delta):
        return index(my_y, lax.rem(my_x + delta, nx), core), place

    def y_peer(delta):
        return index(lax.rem(my_y + delta, ny), my_x, core), place

    twin = (index(my_y, my_x, 1 - core), place)

    def owner(dy, dx, c):
        return index(lax.rem(my_y + ny - dy, ny), lax.rem(my_x + nx - dx, nx), c)

    def peer(delta):
        return lax.rem(me + delta, dp), place

    def line_peer(delta):
        return me, lax.rem(place + delta, seq)

    barrier = pltpu.get_barrier_semaphore()
    for delta in range(1, dp):
        pl.semaphore_signal(barrier, inc=1, device_id=peer(delta), device_id_type=mesh_type)
    for delta in range(1, seq):
        pl.semaphore_signal(barrier, inc=1, device_id=line_peer(delta), device_id_type=mesh_type)

    share = fc_in.shape[1] // dp
    cut = share // columns
    tensors = [(w_held, shard_in.shape[0]), (wo_held, wo_in.shape[0])]
    for j in range(columns):
        tensors += [(fc_held.at[j], fc_in.shape[0]), (proj_held.at[j], cut)]

    def region(t, device, half=None):
        target, size = tensors[t]
        if half is None:
            return target.at[pl.ds(pl.multiple_of(device * size, size), size), :]
        part = size // 2
        return target.at[pl.ds(pl.multiple_of(device * size + half * part, part), part), :]

    def flight(t, slot, part, device):
        return pltpu.make_async_remote_copy(
            src_ref=part, dst_ref=part, send_sem=send_sems.at[t, slot], recv_sem=recv_sems.at[t, slot],
            device_id=device, device_id_type=mesh_type,
        )

    flights = {}
    for t in range(len(tensors)):
        names = [("x", 0, dx) for dx in range(1, nx)] + [("y", dy, 0) for dy in range(1, ny)]
        names += [(kind, dy, dx) for kind in "ab" for dy in range(1, ny) for dx in range(1, nx)]
        names += [("t", dy, dx) for dy in range(ny) for dx in range(nx)]
        for slot, (kind, dy, dx) in enumerate(names):
            if kind == "x":
                part, device = region(t, me), x_peer(dx)
            elif kind == "y":
                part, device = region(t, me), y_peer(dy)
            elif kind == "a":
                part, device = region(t, owner(0, dx, core), 0), y_peer(dy)
            elif kind == "b":
                part, device = region(t, owner(dy, 0, core), 1), x_peer(dx)
            else:
                part, device = region(t, owner(dy, dx, core)), twin
            flights[t, kind, dy, dx] = flight(t, slot, part, device)

    def wave_one(t):
        for dx in range(1, nx):
            flights[t, "x", 0, dx].start()
        for dy in range(1, ny):
            flights[t, "y", dy, 0].start()
        flights[t, "t", 0, 0].start()

    def wave_two(t):
        for dx in range(1, nx):
            flights[t, "x", 0, dx].wait_recv()
            for dy in range(1, ny):
                flights[t, "a", dy, dx].start()
        for dy in range(1, ny):
            flights[t, "y", dy, 0].wait_recv()
            for dx in range(1, nx):
                flights[t, "b", dy, dx].start()
        for dx in range(1, nx):
            flights[t, "t", 0, dx].start()
        for dy in range(1, ny):
            flights[t, "t", dy, 0].start()

    def wave_three(t):
        for dy in range(1, ny):
            for dx in range(1, nx):
                flights[t, "a", dy, dx].wait_recv()
                flights[t, "b", dy, dx].wait_recv()
                flights[t, "t", dy, dx].start()

    def wave_end(t):
        for dy in range(ny):
            for dx in range(nx):
                flights[t, "t", dy, dx].wait_recv()

    def hop(row, s):
        return pltpu.make_async_remote_copy(
            src_ref=hidden.at[row, s - 1], dst_ref=hidden.at[row, s],
            send_sem=hop_send.at[row, s - 1], recv_sem=hop_recv.at[row, s - 1],
            device_id=(me, place + 1), device_id_type=mesh_type,
        )

    def hop_start(row, s):
        @pl.when((place >= s - 1) & (place < top))
        def _():
            hop(row, s).start()

    def arrive(row, s):
        @pl.when(place >= s)
        def _():
            hop(row, s).wait_recv()

        if s < seq - 1:
            hop_start(row, s + 1)
        if s == seq - 1 and row < rows - 1:
            hop_start(row + 1, 1)

    def first_norm(row):
        normed, _ = norm_parts(x_ref[row].astype(F32))
        hidden[row, 0] = (normed * gain1[...] + shift1[...]).astype(BF16)

    def gout_load(row):
        return pltpu.make_async_copy(gout_in.at[row], gout_held, load_sems.at[0])

    def mix_load(row):
        return pltpu.make_async_copy(mix_spill.at[row], mix_held, load_sems.at[1])

    own_copies = [
        pltpu.make_async_copy(source, region(t, me), own_sems.at[t, 0]) for t, source in enumerate((shard_in, wo_in))
    ]
    for j in range(columns):
        for d in range(dp):
            part = region(2 + 2 * j, me).at[:, d * cut : (d + 1) * cut]
            source = fc_in.at[:, d * share + j * cut : d * share + (j + 1) * cut]
            own_copies.append(pltpu.make_async_copy(source, part, own_sems.at[2 + 2 * j, d]))
        source = proj_in.at[j * cut : (j + 1) * cut, :]
        own_copies.append(pltpu.make_async_copy(source, region(3 + 2 * j, me), own_sems.at[3 + 2 * j, 0]))
    for copy in inputs[:8]:
        copy.start()
    own_copies[0].start()
    for copy in inputs[8:]:
        copy.start()
    for copy in inputs[:3]:
        copy.wait()
    first_norm(0)
    for copy in inputs[4:8]:
        copy.wait()
    small_ref[:8, :] = jnp.concatenate([reduce_q[...].astype(F32), reduce_v[...].astype(F32)], axis=0).astype(BF16)
    small_ref[8:, :] = jnp.concatenate([up_q[...].astype(F32), up_v[...].astype(F32)], axis=0).astype(BF16)
    dq_ref[:, :8] = small_ref[:8, :].astype(F32).T
    own_copies[0].wait()
    size = shard_in.shape[0]
    mine = pl.ds(pl.multiple_of(me * size, size), size)
    reduce_own = dq_ref[mine, :8].astype(BF16)
    up = small_ref[8:, :]
    low_rank = lax.broadcasted_iota(jnp.int32, up.shape, 0) < 4
    for column, rank_up in ((0, jnp.where(low_rank, up, jnp.zeros_like(up))), (2, jnp.where(low_rank, jnp.zeros_like(up), up))):
        span = slice(column * width, (column + 1) * width)
        change = dot_nn(reduce_own, rank_up) * ADAPTER_SCALE
        w_held[mine, span] = (w_held[mine, span].astype(F32) + change).astype(BF16)
    pl.semaphore_wait(barrier, dp + seq - 2)
    wave_one(0)
    hop_start(0, 1)
    for copy in later_inputs:
        copy.start()
    for copy in own_copies[1:]:
        copy.start()
    gout_load(0).start()
    for copy in inputs[8:] + inputs[3:4] + own_copies[1:] + later_inputs:
        copy.wait()
    own_starts(seg_ref, begin_ref, place, seq)
    for row in range(1, rows):
        first_norm(row)
    for s in range(1, seq):
        @pl.when(place < s)
        def _():
            for row in range(rows):
                hidden[row, s] = jnp.zeros((tokens, width), BF16)
    for j in range(columns):
        for d in range(dp):
            bias_held[j, :1, d * cut : (d + 1) * cut] = fc_bias[:, d * share + j * cut : d * share + (j + 1) * cut]
    up_sum[...] = jnp.zeros_like(up_sum)
    reduce_sum[...] = jnp.zeros_like(reduce_sum)

    low = head_lanes(tokens, BF16)
    lane = lax.broadcasted_iota(jnp.int32, (tokens, PAIR), 1)
    rank_row = lax.broadcasted_iota(jnp.int32, (8, width), 0) < 4

    def both_heads(pair):
        none = jnp.zeros_like(pair)
        return jnp.concatenate([jnp.where(low, pair, none), jnp.where(low, none, pair)], axis=0)

    def spills(row):
        return [
            pltpu.make_async_copy(held, spill.at[row], spill_sems.at[i])
            for i, (held, spill) in enumerate(
                ((q_held, q_spill), (k_held, k_spill), (v_held, v_spill), (mix_row, mix_spill))
            )
        ]

    def reloads(row):
        return [
            pltpu.make_async_copy(spill.at[row], held, spill_sems.at[4 + i])
            for i, (held, spill) in enumerate(((q_held, q_spill), (k_held, k_spill), (v_held, v_spill)))
        ]

    def attend(row, middle):
        query = place * tokens + lax.broadcasted_iota(jnp.int32, (tokens, tokens), 0)
        start = begin_ref[row].T[:, :1].astype(jnp.int32)
        for s in range(seq):
            key = (place - s) * tokens + lax.broadcasted_iota(jnp.int32, (tokens, tokens), 1)
            span = slice(s * tokens, (s + 1) * tokens)
            mask_ref[:, span] = jnp.where((key >= start) & (key <= query), 0.0, MASKED)
            down_ref[row, :, span] = (dot_nt(small_ref[:8, :], hidden[row, s]) * ADAPTER_SCALE).astype(BF16)

        for quad in range(quads):
            own = slice(quad * QUAD, (quad + 1) * QUAD)
            key_span = slice(width + quad * QUAD, width + (quad + 1) * QUAD)
            value_span = slice(2 * width + quad * QUAD, 2 * width + (quad + 1) * QUAD)
            q = dot_nn(hidden[row, 0], w_held[:, own]) + bias_q[:, own]
            q_held[:, own] = (q.astype(BF16) * (HEAD**-0.5)).astype(BF16)
            for s in range(seq):
                span = slice(s * tokens, (s + 1) * tokens)
                k_held[span, own] = dot_nn(hidden[row, s], w_held[:, key_span]).astype(BF16)
                v_held[span, own] = (dot_nn(hidden[row, s], w_held[:, value_span]) + bias_v[:, own]).astype(BF16)
            totals = jnp.zeros((tokens, PAIR), F32)
            for pair in range(QUAD // PAIR):
                span = slice(quad * QUAD + pair * PAIR, quad * QUAD + (pair + 1) * PAIR)
                score = dot_nt(both_heads(q_held[:, span]), k_held[:, span])
                score = jnp.concatenate([score[:tokens] + mask_ref[...], score[tokens:] + mask_ref[...]], axis=0)
                highest = jnp.max(score, axis=-1, keepdims=True)
                weight = jnp.exp(score - highest)
                total = jnp.sum(weight, axis=-1, keepdims=True)
                mixed = dot_nn(weight.astype(BF16), v_held[:, span]) * (1.0 / total)
                mix_row[:, span] = jnp.where(low, mixed[:tokens], mixed[tokens:]).astype(BF16)
                lse = highest + jnp.log(total)
                totals = jnp.where(lane == 2 * pair, lse[:tokens], totals)
                totals = jnp.where(lane == 2 * pair + 1, lse[tokens:], totals)
            lse_ref[row, quad] = totals.T[:8]
            if 2 * (quad + 1) == quads:
                middle()

    def out_store(row):
        return pltpu.make_async_copy(h2_ref, out_out.at[row], store_sems.at[0])

    def grad_store(row, slot):
        return pltpu.make_async_copy(gmid_ref.at[slot], grad_out.at[row], store_sems.at[1 + slot])

    def late_spills(row):
        return [
            pltpu.make_async_copy(gmix_ref, gmix_spill.at[row], late_sems.at[0]),
            pltpu.make_async_copy(acc_ref, dq_spill.at[row], late_sems.at[1]),
        ]

    def late_loads(row):
        q_room, gmix_room = ((mix_row, mix_held), (gout_held, h2_ref))[row]
        lines = slice((2 + row) * tokens, (3 + row) * tokens)
        return [
            pltpu.make_async_copy(gmix_spill.at[row], gmix_room, late_sems.at[2 + 4 * row]),
            pltpu.make_async_copy(q_spill.at[row], q_room, late_sems.at[3 + 4 * row]),
            pltpu.make_async_copy(k_spill.at[row, :tokens, :], k_held.at[lines, :], late_sems.at[4 + 4 * row]),
            pltpu.make_async_copy(v_spill.at[row, :tokens, :], v_held.at[lines, :], late_sems.at[5 + 4 * row]),
        ]

    def dq_load(row):
        return pltpu.make_async_copy(dq_spill.at[row], acc_ref, late_sems.at[10])

    def gmid_load(row):
        return pltpu.make_async_copy(grad_out.at[row], gmid_ref.at[late_slot], late_sems.at[11])

    def late_ready(row):
        for copy in late_loads(row):
            copy.wait()
        dq_load(row).wait()
        q_room, gmix_room = ((mix_row, mix_held), (gout_held, h2_ref))[row]
        lines = slice((2 + row) * tokens, (3 + row) * tokens)
        q_held[...] = q_room[...]
        gmix_ref[...] = gmix_room[...]
        k_held[:tokens, :] = k_held[lines, :]
        v_held[:tokens, :] = v_held[lines, :]
        dq_ref[...] = acc_ref[...].T

    def leave(row, s):
        return pltpu.make_async_remote_copy(
            src_ref=leaving.at[s - 1], dst_ref=arriving.at[row, s - 1],
            send_sem=leave_sems.at[s - 1], recv_sem=arrive_sems.at[row, s - 1],
            device_id=(me, place - 1), device_id_type=mesh_type,
        )

    def chain(row, s):
        @pl.when((place < top) & (place >= s))
        def _():
            leave(row, s + 1).wait_recv()
            leaving[s - 1] = (leaving[s - 1].astype(F32) + arriving[row, s].astype(F32)).astype(BF16)
            leave(row, s).start()

    def chain_end(row, slot, own):
        @pl.when(place < top)
        def _():
            leave(row, 1).wait_recv()
            own[...] += arriving[row, 0].astype(F32)

        normed, inverse = norm_parts(x_ref[row].astype(F32))
        gmid_ref[slot] = gmid_ref[slot] + norm_backward(own[...], normed, inverse, gain1[...])
        grad_store(row, slot).start()

    def feed_begin(row):
        gout_load(row).wait()

        @pl.when(row < 2)
        def _():
            mix_load(row).wait()

        @pl.when(row >= 1)
        def _():
            out_store(row - 1).wait()

        @pl.when(row == 1)
        def _():
            for copy in reloads(row):
                copy.start()

        @pl.when(row >= 2)
        def _():
            grad_store(row - 2, lax.rem(row, 2)).wait()

        middle = x_ref[row].astype(F32) + dot_nn(mix_held[...], wo_held[...]) + out_bias[...]
        gmid_ref[lax.rem(row, 2)] = middle
        normed, _ = norm_parts(middle)
        h2_ref[...] = (normed * gain2[...] + shift2[...]).astype(BF16)

        @pl.when(row > 0)
        def _():
            late_spills(row - 1)[1].wait()

        acc_ref[...] = jnp.zeros_like(acc_ref)
        back_ref[...] = jnp.zeros_like(back_ref)

    def feed_step(step):
        j = step // per_chunk
        part = pl.ds(pl.multiple_of(lax.rem(step, per_chunk) * block, block), block)
        before = dot_nn(h2_ref[...], fc_held[j, :, part]) + bias_held[j, :1, part]
        square = before * before
        bend = jnp.tanh(GELU_A * before * (1.0 + GELU_B * square))
        half = 0.5 * (1.0 + bend)
        slope = half + 0.5 * before * (1.0 - bend * bend) * (GELU_A * (1.0 + 3.0 * GELU_B * square))
        act = (before * half).astype(BF16)
        g_before = (dot_nt(gout_held[...], proj_held[j, part, :]) * slope).astype(BF16)
        acc_ref[...] += dot_nn(act, proj_held[j, part, :])
        back_ref[...] += dot_nt(g_before, fc_held[j, :, part])

    def feed_end(row):
        slot = lax.rem(row, 2)
        middle = gmid_ref[slot]
        h2_ref[...] = (middle + acc_ref[...] + proj_bias[...]).astype(BF16)
        out_store(row).start()
        normed, inverse = norm_parts(middle)
        g_middle = gout_held[...].astype(F32) + norm_backward(back_ref[...], normed, inverse, gain2[...])
        gmid_ref[slot] = g_middle

        @pl.when(row < last)
        def _():
            grad_store(row, slot).start()

        @pl.when(row > 0)
        def _():
            late_spills(row - 1)[0].wait()

        gmix_ref[...] = dot_nt(g_middle.astype(BF16), wo_held[...]).astype(BF16)
        for pair in range(width // PAIR):
            span = slice(pair * PAIR, (pair + 1) * PAIR)
            product = (gmix_ref[:, span].astype(F32) * mix_held[:, span].astype(F32)).T
            for half in range(2):
                head = pair * 2 + half
                delta_ref[row, head // 4, head % 4 : head % 4 + 1, :] = jnp.sum(
                    product[half * HEAD : (half + 1) * HEAD], axis=0, keepdims=True
                )

        @pl.when(row < rows - 1)
        def _():
            gout_load(row + 1).start()

        @pl.when(row == 0)
        def _():
            mix_load(row + 1).start()

    def attend_chunk(row, s, summed=None):
        query = place * tokens + lax.broadcasted_iota(jnp.int32, (tokens, tokens), 1)
        key = (place - s) * tokens + lax.broadcasted_iota(jnp.int32, (tokens, tokens), 0)
        start = begin_ref[row, :1, :].astype(jnp.int32)
        mask = jnp.where((key >= start) & (key <= query), 0.0, MASKED)
        mask_ref[:, :tokens] = mask
        mask_ref[:, tokens : 2 * tokens] = mask
        rows_s = pl.ds(pl.multiple_of(s * tokens, tokens), tokens)
        for pair in range(width // PAIR):
            span = slice(pair * PAIR, (pair + 1) * PAIR)
            k_pair, v_pair = k_held[rows_s, span], v_held[rows_s, span]
            q_both, g_both = both_heads(q_held[:, span]), both_heads(gmix_ref[:, span])
            head = 2 * (pair % 2)
            lse, inner = [
                jnp.concatenate([ref[head : head + 1, :], ref[head + 1 : head + 2, :]], axis=1)
                for ref in (lse_ref.at[row, pair // 2], delta_ref.at[row, pair // 2])
            ]
            prob = jnp.exp(dot_nt(k_pair, q_both) + mask_ref[:, : 2 * tokens] - lse)
            g_score = (prob * (dot_nt(v_pair, g_both) - inner)).astype(BF16)
            dkv_ref[:, span] = dot_nn(g_score, q_both).astype(BF16)
            dkv_ref[:, width + pair * PAIR : width + (pair + 1) * PAIR] = dot_nn(prob.astype(BF16), g_both).astype(BF16)
            k_turned = k_pair.astype(F32).T.astype(BF16)
            for half in range(2):
                lines = slice(pair * PAIR + half * HEAD, pair * PAIR + (half + 1) * HEAD)
                part = g_score[:, half * tokens : (half + 1) * tokens]
                dq_ref[lines, :] += dot_nn(k_turned[half * HEAD : (half + 1) * HEAD], part)

        dv = dkv_ref[:, width:]
        up_grad = dot_nn(down_ref[row, :, rows_s], dv)
        g_down = dot_nt(small_ref[8:, :], dv).astype(BF16)
        reduce_grad = dot_nn(g_down, hidden[row, s])
        up_sum[...] += jnp.where(rank_row, 0.0, up_grad)
        reduce_sum[...] += jnp.where(rank_row, 0.0, reduce_grad)
        if summed is None:
            @pl.when(row > 0)
            def _():
                leave(row - 1, s).wait_send()

            leaving[s - 1] = dot_nt(dkv_ref[...], w_held[:, width:]).astype(BF16)

            @pl.when(place == top)
            def _():
                leave(row, s).start()
        else:
            dq = (dq_ref[...].T * (HEAD**-0.5)).astype(BF16)
            up_grad = dot_nn(down_ref[row, :, rows_s], dq)
            g_down = dot_nt(small_ref[8:, :], dq).astype(BF16)
            reduce_grad = dot_nn(g_down, hidden[row, s])
            up_sum[...] += jnp.where(rank_row, up_grad, 0.0)
            reduce_sum[...] += jnp.where(rank_row, reduce_grad, 0.0)
            summed()
            own_ref[...] = dot_nt(dkv_ref[...], w_held[:, width:]) + dot_nt(dq, w_held[:, :width])

    def backward(row):
        feed_end(row)

        @pl.when(row > 0)
        def _():
            chain(row - 1, seq - 3)

        @pl.when(row < 2)
        def _():
            for copy in reloads(row):
                copy.wait()

        dq_ref[...] = jnp.zeros_like(dq_ref)

        @pl.loop(0, seq - 1)
        def _(step):
            s = seq - 1 - step

            @pl.when((row > 0) & (s < seq - 3))
            def _():
                chain(row - 1, s)

            @pl.when(place >= s)
            def _():
                attend_chunk(row, s)

        chain(row, seq - 2)

        @pl.when(row < last)
        def _():
            acc_ref[...] = dq_ref[...].T
            for copy in late_spills(row):
                copy.start()

    def both(action, j):
        if j < columns:
            action(2 + 2 * j)
            action(3 + 2 * j)

    def before_first():
        arrive(0, 1)
        wave_two(0)
        wave_one(1)
        for s in range(2, seq):
            if s == seq - 1:
                wave_three(0)
                both(wave_one, 0)
                wave_two(1)
            arrive(0, s)
        wave_end(0)
        both(wave_one, 1)

    def before_second():
        both(wave_two, 0)
        both(wave_one, 2)
        for s in range(1, seq):
            if s == seq - 1:
                both(wave_two, 1)
                wave_three(1)
                both(wave_three, 0)
            arrive(1, s)
        both(wave_one, 3)

    def amid_second():
        both(wave_two, 2)
        both(wave_three, 1)

    def before_feed():
        arrive(2, 1)
        wave_end(1)
        both(wave_two, 3)
        for copy in spills(1):
            copy.wait()
        for copy in reloads(0):
            copy.start()

    def amid_feed(step):
        for j in range(columns):
            @pl.when(step == j * per_chunk)
            def _():
                if j == min(1, columns - 1):
                    for s in range(2, seq - 1):
                        arrive(2, s)
                if j >= 2 or j == columns - 1:
                    both(wave_three, j)
                both(wave_end, j)

    def before_third():
        arrive(2, seq - 1)

    def before_later(row):
        for s in range(1, seq):
            arrive(row, s)

    @pl.loop(0, 2 * rows)
    def _(turn):
        attending = (turn < 2) | ((turn >= 4) & (lax.rem(turn, 2) == 0))
        attend_row = jnp.where(turn < 2, turn, turn // 2)
        row = jnp.where(turn < 4, jnp.maximum(turn - 2, 0), (turn - 1) // 2)
        for index in range(rows):
            befores = (before_first, before_second, before_third)
            action = befores[index] if index < 3 else partial(before_later, index)
            pl.when(turn == (index if index < 2 else 2 * index))(action)

        pl.when(turn == 2)(before_feed)

        @pl.when(turn == 1)
        def _():
            for copy in spills(0):
                copy.wait()
            mix_load(0).start()

        @pl.when(attending)
        def _():
            attend(attend_row, lambda: pl.when(turn == 1)(amid_second))

            @pl.when(turn < 2)
            def _():
                for copy in spills(turn):
                    copy.start()

            @pl.when(turn >= 2)
            def _():
                mix_held[...] = mix_row[...]

        @pl.when(jnp.logical_not(attending))
        def _():
            feed_begin(row)

            @pl.loop(0, steps)
            def _(step):
                pl.when(turn == 2)(partial(amid_feed, step))
                feed_step(step)

            backward(row)

    def sum_copy(source, target, slot, device):
        return pltpu.make_async_remote_copy(
            src_ref=source, dst_ref=target, send_sem=sum_send.at[slot], recv_sem=sum_recv.at[slot],
            device_id=device, device_id_type=mesh_type,
        )

    def piece_copies():
        return [
            sum_copy(part_ref.at[lax.rem(me + delta, dp)], plane_ref.at[delta], delta, peer(delta))
            for delta in range(1, dp)
        ]

    piece = part_ref.shape[1]
    lanes = width // PAIR

    def start_sums():
        part_ref[...] = jnp.zeros_like(part_ref)
        for half, total in enumerate((reduce_sum[...] * ADAPTER_SCALE, up_sum[...])):
            for block_lane in range(lanes):
                line = (half * lanes + block_lane) * 8
                part_ref[line // piece, line % piece : line % piece + 8, :] = total[:, block_lane * PAIR : (block_lane + 1) * PAIR]
        for copy in piece_copies():
            copy.start()

    grad_store(last - 1, late_slot).wait()
    out_store(last).wait()
    for copy in [gmid_load(0), dq_load(0)] + late_loads(0) + late_loads(1):
        copy.start()

    @pl.loop(0, 3)
    def _(turn):
        @pl.when(turn == 1)
        def _():
            late_ready(0)
            dq_load(1).start()

        @pl.when(turn == 2)
        def _():
            late_ready(1)
            grad_store(0, late_slot).wait()
            gmid_load(1).start()

        attend_chunk(jnp.where(turn == 0, last, turn - 1), 0, lambda: pl.when(turn == 2)(start_sums))

        @pl.when(turn == 0)
        def _():
            back_ref[...] = own_ref[...]

        @pl.when(turn > 0)
        def _():
            gmid_load(turn - 1).wait()
            chain_end(turn - 1, late_slot, own_ref)

        pl.when(turn == 1)(partial(chain, last, seq - 3))

    total = part_ref[me]
    for delta, copy in enumerate(piece_copies()):
        copy.wait()
        total = total + plane_ref[delta + 1]
    line_ref[place] = total
    line_copies = [
        sum_copy(line_ref.at[place], line_ref.at[place], dp + delta, line_peer(delta)) for delta in range(1, seq)
    ]
    for copy in line_copies:
        copy.start()
    for copy in line_copies:
        copy.wait()
    total = line_ref[0]
    for other in range(1, seq):
        total = total + line_ref[other]
    sum_out[me] = total
    copies = [sum_copy(sum_out.at[me], sum_out.at[me], dp + seq + delta, peer(delta)) for delta in range(1, dp)]
    for copy in copies:
        copy.start()
    for s in range(seq - 4, 0, -1):
        chain(last, s)
    chain_end(last, last % 2, back_ref)
    for copy in copies:
        copy.wait()
    for copy in flights.values():
        copy.wait_send()
    for row in range(rows):
        for s in range(1, seq):
            @pl.when((place >= s - 1) & (place < top))
            def _():
                hop(row, s).wait_send()
    for s in range(1, seq):
        @pl.when(place >= s)
        def _():
            leave(last, s).wait_send()
    grad_store(last - 1, late_slot).wait()
    grad_store(last, last % 2).wait()


def run_block(plane, seq, x, seg, adapters, vectors, shards, gout):
    rows, tokens, width = x.shape
    assert rows == 3
    length = seq * tokens
    dp = plane[0] * plane[1] * 2
    hidden_units = shards[2].shape[1]
    block = 1024
    quads = width // QUAD
    piece = max(8, 16 * width // (PAIR * dp))
    nx, ny = plane
    columns = max(1, min(4, hidden_units // (dp * PAIR)))
    flights = nx - 1 + ny - 1 + 2 * (nx - 1) * (ny - 1) + nx * ny
    sums = 2 * dp + seq
    anywhere = pl.BlockSpec(memory_space=pl.ANY)
    vmem = pl.BlockSpec(memory_space=pltpu.VMEM)
    dma = pltpu.SemaphoreType.DMA

    def held(*dims, dtype=BF16):
        return pltpu.VMEM(dims, dtype)

    def shape(*dims, dtype=BF16):
        return jax.ShapeDtypeStruct(dims, dtype)

    result = pl.pallas_call(
        partial(block_kernel, plane, seq, rows, block),
        in_specs=[anywhere] * 20,
        out_specs=[anywhere, anywhere, vmem] + [anywhere] * 6,
        out_shape=[
            shape(rows, tokens, width), shape(rows, tokens, width, dtype=F32), shape(dp, piece, PAIR, dtype=F32),
            shape(rows, tokens, width), shape(rows, length, width), shape(rows, length, width),
            shape(rows, tokens, width), shape(rows, tokens, width), shape(rows, tokens, width, dtype=F32),
        ],
        scratch_shapes=[
            *(held(*a.shape, dtype=a.dtype) for a in (x, seg, *adapters, *vectors)), held(16, width), dma((14 + rows,)),
            held(width, 3 * width), held(width, width), held(columns, width, hidden_units // columns), held(columns, hidden_units // columns, width),
            held(rows, seq, tokens, width), held(tokens, width), held(length, width), held(length, width),
            held(tokens, width), held(tokens, width), held(tokens, width),
            held(tokens, width), held(tokens, width),
            held(tokens, width, dtype=F32), held(tokens, width, dtype=F32), held(2, tokens, width, dtype=F32),
            held(tokens, width, dtype=F32), held(tokens, length, dtype=F32), held(rows, quads, 8, tokens, dtype=F32),
            held(width, tokens, dtype=F32), held(tokens, 2 * width),
            held(seq - 1, tokens, width), held(rows, seq - 1, tokens, width),
            held(rows, 8, tokens, dtype=F32), held(columns, 8, hidden_units // columns, dtype=F32),
            held(rows, quads, 8, tokens, dtype=F32), held(rows, 8, length),
            held(8, width, dtype=F32), held(8, width, dtype=F32),
            held(dp, piece, PAIR, dtype=F32), held(dp, piece, PAIR, dtype=F32), held(seq, piece, PAIR, dtype=F32),
            dma((2 + 2 * columns, flights)), dma((2 + 2 * columns, flights)), dma((rows, seq - 1)), dma((rows, seq - 1)),
            dma((2 + 2 * columns, dp)), dma((7,)), dma((2,)), dma((12,)), dma((3,)),
            dma((seq - 1,)), dma((rows, seq - 1)), dma((sums,)), dma((sums,)),
        ],
        compiler_params=pltpu.CompilerParams(
            vmem_limit_bytes=VMEM_BYTES, collective_id=0, has_side_effects=True
        ),
        name="block",
    )(x, seg, *adapters, *vectors, *shards, gout)
    out, grad, total = result[:3]
    flat = total.reshape(-1, PAIR)[: 16 * width // PAIR]
    return out, grad, flat.reshape(2, width // PAIR, 8, PAIR).transpose(0, 2, 1, 3).reshape(2, 8, width)


def on_device(
    dp,
    seq,
    block_input,
    seg_start,
    ln1_gain,
    ln1_bias,
    qkv_weight,
    query_bias,
    value_bias,
    query_adapter_reduce,
    query_up,
    value_adapter_reduce,
    value_up,
    out_weight,
    out_bias,
    ln2_gain,
    ln2_bias,
    fc_weight,
    fc_bias,
    proj_weight,
    proj_bias,
    grad_out,
):
    rows, tokens, width = block_input.shape
    rank = query_up.shape[0]
    side = math.isqrt(dp // 2)
    adapters = (query_adapter_reduce.T, value_adapter_reduce.T, query_up, value_up)

    def as_row(vector):
        return vector.reshape(1, -1)

    vectors = tuple(
        as_row(a)
        for a in (ln1_gain, ln1_bias, query_bias, value_bias, out_bias, ln2_gain, ln2_bias, proj_bias, fc_bias)
    )
    out, grad, sums = run_block(
        (side, dp // (2 * side)), seq, block_input, seg_start, adapters, vectors,
        (qkv_weight, out_weight, fc_weight, proj_weight), grad_out,
    )
    reduce, up = sums[0], sums[1]
    return out, grad, reduce[:rank].T, up[:rank], reduce[rank : 2 * rank].T, up[rank : 2 * rank]


def solution(mesh):
    return jax.shard_map(
        partial(on_device, mesh.shape["dp"], mesh.shape["seq"]),
        mesh=mesh,
        in_specs=(
            P("dp", "seq", None),
            P("dp", None),
            P(),
            P(),
            P("dp", None),
            P(),
            P(),
            P(),
            P(),
            P(),
            P(),
            P("dp", None),
            P(),
            P(),
            P(),
            P("dp", None),
            P(),
            P("dp", None),
            P(),
            P("dp", "seq", None),
        ),
        out_specs=(P("dp", "seq", None), P("dp", "seq", None), P(), P(), P(), P()),
        check_vma=False,
    )
```
